32 devices in a mesh: dp: 4 (over y, core), seq: 8 (over z, x).
Axes of the slice: x: 2, y: 2, z: 4, core: 2. Of those that a mesh axis runs over, the one named last changes fastest.
Arguments:
- tokens: bfloat16 [8, 4096, 768], P('dp', 'seq'), may hold values from -6 to 6
- encoder_states: bfloat16 [8, 256, 768], P('dp', 'seq'), may hold values from -6 to 6
- out_grad: bfloat16 [8, 4096, 768], P('dp', 'seq'), may hold values from -6 to 6
- block_map: int32 [8, 32], P('dp'), may hold values from 0 to 31, each once within a row
- branch_fork: int32 [8, 8], P('dp'), may hold values from 512 to 2048
- norm_gain: bfloat16 [3, 768], P(None, ('dp', 'seq')), may hold values from 0.5 to 1.5
- norm_bias: bfloat16 [3, 768], P(None, ('dp', 'seq')), may hold values from -1.75 to 1.75
- self_in: bfloat16 [3, 768, 768], P(None, ('dp', 'seq')), may hold values from -0.21875 to 0.21875
- self_out: bfloat16 [768, 768], P(('dp', 'seq')), may hold values from -1.75 to 1.75
- self_bias: bfloat16 [3, 768], P(None, ('dp', 'seq')), may hold values from -0.3125 to 0.3125
- cross_in: bfloat16 [3, 768, 768], P(None, ('dp', 'seq')), may hold values from -0.21875 to 0.21875
- cross_out: bfloat16 [768, 768], P(('dp', 'seq')), may hold values from -1.75 to 1.75
- cross_bias: bfloat16 [3, 768], P(None, ('dp', 'seq')), may hold values from -0.3125 to 0.3125
- up_weight: bfloat16 [768, 3072], P(('dp', 'seq')), may hold values from -0.21875 to 0.21875
- up_bias: bfloat16 [3072], P(('dp', 'seq')), may hold values from -3 to 3
- down_weight: bfloat16 [3072, 768], P(('dp', 'seq')), may hold values from -0.109375 to 0.109375
- down_bias: bfloat16 [768], P(('dp', 'seq')), may hold values from -1.25 to 1.25
Outputs:
- activations: bfloat16 [8, 4096, 768], P('dp', 'seq')
- tokens_grad: float32 [8, 4096, 768], P('dp', 'seq')
- encoder_grad: float32 [8, 256, 768], P('dp', 'seq')
- norm_gain_grad: float32 [3, 768], P(None, ('dp', 'seq'))
- norm_bias_grad: float32 [3, 768], P(None, ('dp', 'seq'))
- self_in_grad: float32 [3, 768, 768], P(None, ('dp', 'seq'))
- self_out_grad: float32 [768, 768], P(('dp', 'seq'))
- self_bias_grad: float32 [3, 768], P(None, ('dp', 'seq'))
- cross_in_grad: float32 [3, 768, 768], P(None, ('dp', 'seq'))
- cross_out_grad: float32 [768, 768], P(('dp', 'seq'))
- cross_bias_grad: float32 [3, 768], P(None, ('dp', 'seq'))
- up_weight_grad: float32 [768, 3072], P(('dp', 'seq'))
- up_bias_grad: float32 [3072], P(('dp', 'seq'))
- down_weight_grad: float32 [3072, 768], P(('dp', 'seq'))
- down_bias_grad: float32 [768], P(('dp', 'seq'))
The draws below stay inside these ranges and needn't reach their ends.
Inputs may be any that keep to these rules, and one draw needn't show every extreme that they name: Each row of block_map is a permutation of the group's 32 logical blocks.
All inputs are finite; a program needn't handle non-finite values.
Results may differ from the reference program's by a relative error of at most 0.02.
Values may be sent and summed in bfloat16 or wider, within the bound.
No kernel may reach another device: no remote copies, remote signals or barrier semaphores. Data moves between devices by JAX's collectives and lax.ppermute only.
A program may use at most 576 MiB of HBM per device.

```python
import jax
import jax.numpy as jnp
from jax import lax

D = 768
HEADS = 12
HEAD = 64
FF = 3072
PROMPT = 2048
BRANCHES = 8
BLEN = 256
BLOCK = 128
GROUP_TOK = 4096
NBLK = 32
FRAMES = 256
GROUPS = 8


def set_ends(array, stream_key, low, largest):
    extent = array.shape
    spot = [jax.random.randint(jax.random.fold_in(stream_key, axis), (), 0, extent[axis]) for axis in range(len(extent))]
    array = array.at[tuple(spot)].set(low)
    longest = extent.index(max(extent))
    spot[longest] = (spot[longest] + 1) % extent[longest]
    return array.at[tuple(spot)].set(largest)


def shard_levels(key, dims, split, low, largest):
    level = 1.0
    for dim, parts in split:
        draws = jax.random.uniform(jax.random.fold_in(jax.random.fold_in(key, 6), dim), (parts,), jnp.float32, low / len(split), largest / len(split))
        level = level * jnp.repeat(jnp.exp(draws), dims[dim] // parts).reshape((-1,) + (1,) * (len(dims) - 1 - dim))
    return level


def noise(key, dims, scale, most, cuts=(), held_as=jnp.bfloat16):
    array = jax.random.normal(key, dims, jnp.float32) * scale
    if len(cuts) > 0:
        array = shard_levels(key, dims, cuts, -0.22, 0.18) * array
    return jnp.clip(array, min=-most, max=most).astype(held_as)


def setup_inputs(seed: int = 0) -> dict:
    key_of = jax.random.split(jax.random.key(seed), 18)
    return {
        "tokens": noise(key_of[0], (GROUPS, GROUP_TOK, D), 1.0, 6.0, ((0, 4), (1, 8))),
        "encoder_states": noise(key_of[1], (GROUPS, FRAMES, D), 1.0, 6.0, ((0, 4), (1, 8))),
        "out_grad": noise(key_of[2], (GROUPS, GROUP_TOK, D), 1.0, 6.0, ((0, 4), (1, 8))),
        "block_map": jax.vmap(lambda own: jax.random.permutation(own, NBLK))(jax.random.split(key_of[3], GROUPS)).reshape((GROUPS, NBLK)).astype(jnp.int32),
        "branch_fork": set_ends(jax.random.randint(key_of[4], (GROUPS, BRANCHES), PROMPT // 4, PROMPT + 1), jax.random.fold_in(key_of[4], 1), PROMPT // 4, PROMPT).astype(jnp.int32),
        "norm_gain": jnp.clip(1.0 + 0.1 * jax.random.normal(key_of[5], (3, D), jnp.float32), 0.5, 1.5).astype(jnp.bfloat16),
        "norm_bias": noise(key_of[6], (3, D), 0.3, 1.75, ((1, 32),)),
        "self_in": noise(key_of[7], (3, D, D), D ** -0.5, 0.21875, ((1, 32),)),
        "self_out": noise(key_of[8], (D, D), (D // 64) ** -0.5, 1.75, ((0, 32),)),
        "self_bias": noise(key_of[9], (3, D), 0.05, 0.3125, ((1, 32),)),
        "cross_in": noise(key_of[10], (3, D, D), D ** -0.5, 0.21875, ((1, 32),)),
        "cross_out": noise(key_of[11], (D, D), (D // 64) ** -0.5, 1.75, ((0, 32),)),
        "cross_bias": noise(key_of[12], (3, D), 0.05, 0.3125, ((1, 32),)),
        "up_weight": noise(key_of[13], (D, FF), D ** -0.5, 0.21875, ((0, 32),)),
        "up_bias": noise(key_of[14], (FF,), 0.5, 3.0, ((0, 32),)),
        "down_weight": noise(key_of[15], (FF, D), FF ** -0.5, 0.109375, ((0, 32),)),
        "down_bias": noise(key_of[16], (D,), 0.2, 1.25, ((0, 32),)),
    }


@jax.custom_vjp
def low(v):
    return lax.optimization_barrier(v.astype(jnp.bfloat16)).astype(jnp.float32)

@jax.custom_vjp
def low_back(v):
    return v

def low_keep(v):
    return (low(v), None)

def low_pass(kept, grad):
    return (grad,)

def back_keep(v):
    return (v, None)

def back_low(kept, grad):
    return (low(grad),)
low.defvjp(low_keep, low_pass)
low_back.defvjp(back_keep, back_low)

def low_both(matrix):
    return low_back(low(matrix))

def product(former, latter):
    return jnp.dot(former, latter, precision=lax.Precision.HIGHEST, preferred_element_type=jnp.float32)

def norm_layer(stream, norm_gain, norm_shift):
    center = lax.optimization_barrier(jnp.mean(stream, axis=-1, keepdims=True))
    centered = stream - center
    spread = lax.optimization_barrier(jnp.mean(centered * centered, axis=-1, keepdims=True))
    return centered * lax.rsqrt(spread + 1e-05) * norm_gain + norm_shift

def token_info(blocks, branch_forks):
    offsets = jnp.arange(BLOCK, dtype=jnp.int32)
    logical = (blocks[:, None] * BLOCK + offsets[None, :]).reshape(-1).astype(jnp.int32)
    relative = logical - PROMPT
    in_branch = relative >= 0
    segment = jnp.where(in_branch, relative // BLEN + 1, 0).astype(jnp.int32)
    position = jnp.where(in_branch, relative % BLEN, logical).astype(jnp.int32)
    labels = jnp.arange(1, BRANCHES + 1, dtype=jnp.int32)
    fork_reach = lax.optimization_barrier(jnp.sum(jnp.where(segment[:, None] == labels[None, :], branch_forks[None, :], 0), axis=1)).astype(jnp.int32)
    return (segment, position, fork_reach)

def allowed(query_info, key_info):
    same = (query_info[0][:, None] == key_info[0][None, :]) & (key_info[1][None, :] <= query_info[1][:, None])
    shared = (query_info[0][:, None] > 0) & (key_info[0][None, :] == 0) & (key_info[1][None, :] < query_info[2][:, None])
    return same | shared

def head_split(matrix):
    return matrix.reshape(matrix.shape[0], HEADS, HEAD)

def attend(queries, key_rows, value_rows, key_mask):
    scores = low_back(jnp.einsum('rhd,khd->hrk', head_split(queries), head_split(key_rows), precision=lax.Precision.HIGHEST) * HEAD ** (-0.5))
    if key_mask is not None:
        scores = jnp.where(key_mask[None], scores, -1e+30)
    row_max = lax.optimization_barrier(jnp.max(scores, axis=2, keepdims=True))
    weights = jnp.exp(scores - row_max)
    row_total = lax.optimization_barrier(jnp.sum(weights, axis=2, keepdims=True))
    shares = low(weights / row_total)
    attended = jnp.einsum('hrk,khd->rhd', shares, head_split(value_rows), precision=lax.Precision.HIGHEST)
    return attended.reshape(queries.shape[0], HEADS * HEAD)

def attention(queries, key_rows, value_rows, query_info, key_info):
    row_count = queries.shape[0]
    block_rows = min(512, row_count)
    block_count = row_count // block_rows

    def one_block(pieces):
        block_queries = pieces[0]
        key_mask = None
        if key_info is not None:
            key_mask = allowed((pieces[1], pieces[2], pieces[3]), key_info)
        return attend(block_queries, key_rows, value_rows, key_mask)
    pieces = (queries.reshape(block_count, block_rows, queries.shape[1]),) + tuple((column.reshape(block_count, block_rows) for column in query_info))
    return lax.map(jax.checkpoint(one_block), pieces).reshape(row_count, queries.shape[1])

def layer(stream, encoded, weights, query_info):
    norm_gain, norm_bias, self_in, self_out, self_bias, cross_in, cross_out, cross_bias, up_weight, up_bias, down_weight, down_bias = weights
    norm_first = low(norm_layer(stream, norm_gain[0], norm_bias[0]))
    queries = low_both(product(norm_first, self_in[0]) + self_bias[0])
    key_rows = low_both(product(norm_first, self_in[1]))
    value_rows = low_both(product(norm_first, self_in[2]) + self_bias[1])
    attended = low_both(attention(queries, key_rows, value_rows, query_info, query_info))
    middle = stream + low_back(product(attended, self_out) + self_bias[2])
    norm_second = low(norm_layer(middle, norm_gain[1], norm_bias[1]))
    cross_queries = low_both(product(norm_second, cross_in[0]) + cross_bias[0])
    cross_keys = low_both(product(encoded, cross_in[1]))
    cross_values = low_both(product(encoded, cross_in[2]) + cross_bias[1])
    cross_attended = low_both(attention(cross_queries, cross_keys, cross_values, query_info, None))
    after_cross = middle + low_back(product(cross_attended, cross_out) + cross_bias[2])
    norm_third = low(norm_layer(after_cross, norm_gain[2], norm_bias[2]))
    before = low_back(product(norm_third, up_weight) + up_bias)
    activated = low(jax.nn.gelu(before, approximate=False))
    return after_cross + product(activated, down_weight) + down_bias

def reference(tokens, encoder_states, out_grad, block_map, branch_fork, norm_gain, norm_bias, self_in, self_out, self_bias, cross_in, cross_out, cross_bias, up_weight, up_bias, down_weight, down_bias):
    weights = tuple((matrix.astype(jnp.float32) for matrix in (norm_gain, norm_bias, self_in, self_out, self_bias, cross_in, cross_out, cross_bias, up_weight, up_bias, down_weight, down_bias)))

    def one_group(grad_sums, group):
        stream, encoded, cotangent, blocks, branch_forks = group
        query_info = token_info(blocks, branch_forks)

        def forward(stream_in, encoded_in, weights_in):
            return layer(stream_in, encoded_in, weights_in, query_info)
        result, pull_back = jax.vjp(forward, stream.astype(jnp.float32), encoded.astype(jnp.float32), weights)
        grad_stream, grad_encoded, grad_weights = pull_back(cotangent.astype(jnp.float32))
        grad_sums = tuple((former + latter for former, latter in zip(grad_sums, grad_weights)))
        return (grad_sums, (result.astype(jnp.bfloat16), grad_stream, grad_encoded))
    starting = tuple((jnp.zeros_like(matrix) for matrix in weights))
    grad_sums, outputs = lax.scan(one_group, starting, (tokens, encoder_states, out_grad, block_map, branch_fork))
    return (outputs[0], outputs[1], outputs[2], grad_sums[0], grad_sums[1], grad_sums[2], grad_sums[3], grad_sums[4], grad_sums[5], grad_sums[6], grad_sums[7], grad_sums[8], grad_sums[9], grad_sums[10], grad_sums[11])
```

```python
import functools

import jax
import jax.numpy as jnp
from jax import lax
from jax.experimental import pallas as pl
from jax.experimental.pallas import tpu as pltpu
from jax.sharding import PartitionSpec as P

HEADS = 12
HEAD = 64
PROMPT = 2048
BRANCHES = 8
BLEN = 256
BLOCK = 128


def product(former, latter):
    return jnp.dot(former, latter, preferred_element_type=jnp.float32)


def product_left(former, latter):
    return lax.dot_general(
        former, latter, (((0,), (0,)), ((), ())), preferred_element_type=jnp.float32
    )


def product_right(former, latter):
    return lax.dot_general(
        former, latter, (((1,), (1,)), ((), ())), preferred_element_type=jnp.float32
    )


def column_sum(matrix):
    return jnp.sum(matrix.astype(jnp.float32), axis=0)


def norm_layer(stream, norm_gain, norm_shift):
    center = jnp.mean(stream, axis=-1, keepdims=True)
    centered = stream - center
    spread = jnp.mean(centered * centered, axis=-1, keepdims=True)
    return centered * lax.rsqrt(spread + 1e-05) * norm_gain + norm_shift


def gelu_exact(before):
    return jax.nn.gelu(before, approximate=False)


def token_info(blocks, branch_forks):
    offsets = jnp.arange(BLOCK, dtype=jnp.int32)
    logical = (blocks[:, None] * BLOCK + offsets[None, :]).reshape(-1)
    relative = logical - PROMPT
    in_branch = relative >= 0
    segment = jnp.where(in_branch, relative // BLEN + 1, 0)
    position = jnp.where(in_branch, relative % BLEN, logical)
    labels = jnp.arange(1, BRANCHES + 1, dtype=jnp.int32)
    fork_reach = jnp.sum(
        jnp.where(segment[:, None] == labels[None, :], branch_forks[None, :], 0), axis=1
    )
    return (segment, position, fork_reach)


def allowed(query_info, key_info):
    same = (query_info[0][:, None] == key_info[0][None, :]) & (
        key_info[1][None, :] <= query_info[1][:, None]
    )
    shared = (
        (query_info[0][:, None] > 0)
        & (key_info[0][None, :] == 0)
        & (key_info[1][None, :] < query_info[2][:, None])
    )
    return same | shared


def head_split(matrix):
    return matrix.reshape(matrix.shape[0], HEADS, HEAD)


def score_block(queries, key_rows, key_mask):
    scores = jnp.einsum(
        "rhd,khd->hrk",
        head_split(queries),
        head_split(key_rows),
        preferred_element_type=jnp.float32,
    ) * HEAD ** (-0.5)
    if key_mask is None:
        return scores
    return jnp.where(key_mask[None], scores, -1e30)


def attend_forward(queries, key_rows, value_rows, key_mask):
    scores = score_block(queries, key_rows, key_mask)
    row_max = jnp.max(scores, axis=2, keepdims=True)
    weights = jnp.exp(scores - row_max)
    row_total = jnp.sum(weights, axis=2, keepdims=True)
    shares = (weights / row_total).astype(jnp.bfloat16)
    attended = jnp.einsum(
        "hrk,khd->rhd", shares, head_split(value_rows), preferred_element_type=jnp.float32
    )
    return (attended.reshape(queries.shape[0], -1).astype(jnp.bfloat16), row_max, row_total)


def attend_backward(queries, key_rows, value_rows, key_mask, row_max, row_total, incoming):
    scores = score_block(queries, key_rows, key_mask)
    shares_full = jnp.exp(scores - row_max) / row_total
    shares_low = shares_full.astype(jnp.bfloat16)
    grad_heads = head_split(incoming)
    grad_values = jnp.einsum(
        "hrk,rhd->khd", shares_low, grad_heads, preferred_element_type=jnp.float32
    )
    grad_shares = jnp.einsum(
        "rhd,khd->hrk", grad_heads, head_split(value_rows), preferred_element_type=jnp.float32
    )
    inner_sum = jnp.sum(grad_shares * shares_full, axis=2, keepdims=True)
    grad_scores = (shares_full * (grad_shares - inner_sum)).astype(jnp.bfloat16)
    grad_queries = jnp.einsum(
        "hrk,khd->rhd", grad_scores, head_split(key_rows), preferred_element_type=jnp.float32
    ) * HEAD ** (-0.5)
    grad_keys = jnp.einsum(
        "hrk,rhd->khd", grad_scores, head_split(queries), preferred_element_type=jnp.float32
    ) * HEAD ** (-0.5)
    row_count = queries.shape[0]
    key_count = key_rows.shape[0]
    return (
        grad_queries.reshape(row_count, -1),
        grad_keys.reshape(key_count, -1),
        grad_values.reshape(key_count, -1),
    )


def fetch_self(shards):
    return (
        lax.all_gather(shards[0][0], ("dp", "seq"), axis=0, tiled=True),
        lax.all_gather(shards[1][0], ("dp", "seq"), axis=0, tiled=True),
        lax.all_gather(shards[2], ("dp", "seq"), axis=1, tiled=True),
        lax.all_gather(shards[3], ("dp", "seq"), axis=0, tiled=True),
        lax.all_gather(shards[4], ("dp", "seq"), axis=1, tiled=True),
    )


def fetch_cross(shards):
    return (
        lax.all_gather(shards[0][1], ("dp", "seq"), axis=0, tiled=True),
        lax.all_gather(shards[1][1], ("dp", "seq"), axis=0, tiled=True),
        lax.all_gather(shards[5], ("dp", "seq"), axis=1, tiled=True),
        lax.all_gather(shards[6], ("dp", "seq"), axis=0, tiled=True),
        lax.all_gather(shards[7], ("dp", "seq"), axis=1, tiled=True),
    )


def fetch_feed(shards):
    return (
        lax.all_gather(shards[0][2], ("dp", "seq"), axis=0, tiled=True),
        lax.all_gather(shards[1][2], ("dp", "seq"), axis=0, tiled=True),
        lax.all_gather(shards[8], ("dp", "seq"), axis=0, tiled=True),
        lax.all_gather(shards[9], ("dp", "seq"), axis=0, tiled=True),
        lax.all_gather(shards[10], ("dp", "seq"), axis=0, tiled=True),
        lax.all_gather(shards[11], ("dp", "seq"), axis=0, tiled=True),
    )


def body(
    tokens,
    encoder_states,
    out_grad,
    block_map,
    branch_fork,
    norm_gain,
    norm_bias,
    self_in,
    self_out,
    self_bias,
    cross_in,
    cross_out,
    cross_bias,
    up_weight,
    up_bias,
    down_weight,
    down_bias,
):
    shards = (
        norm_gain,
        norm_bias,
        self_in,
        self_out,
        self_bias,
        cross_in,
        cross_out,
        cross_bias,
        up_weight,
        up_bias,
        down_weight,
        down_bias,
    )
    model_width = tokens.shape[2]
    hidden_width = up_weight.shape[1]
    seq_count = lax.axis_size("seq")
    seq_place = lax.axis_index("seq")

    def micro_step(grad_sums, inputs):
        tokens_in, encoded, cotangent, blocks, branch_forks = inputs
        slot_count = blocks.shape[0] // seq_count
        own_blocks = lax.dynamic_slice_in_dim(blocks, seq_place * slot_count, slot_count)
        query_info = token_info(own_blocks, branch_forks)
        full_info = token_info(blocks, branch_forks)
        key_mask = allowed(query_info, full_info)
        gain_first, shift_first, attend_in, attend_out, attend_bias = fetch_self(shards)
        stream = tokens_in.astype(jnp.float32)
        norm_full, pull_first = jax.vjp(
            norm_layer, stream, gain_first.astype(jnp.float32), shift_first.astype(jnp.float32)
        )
        norm_first = norm_full.astype(jnp.bfloat16)
        queries = (product(norm_first, attend_in[0]) + attend_bias[0].astype(jnp.float32)).astype(
            jnp.bfloat16
        )
        key_local = product(norm_first, attend_in[1]).astype(jnp.bfloat16)
        value_local = (
            product(norm_first, attend_in[2]) + attend_bias[1].astype(jnp.float32)
        ).astype(jnp.bfloat16)
        key_rows, value_rows = (
            lax.all_gather(key_local, "seq", axis=0, tiled=True),
            lax.all_gather(value_local, "seq", axis=0, tiled=True),
        )
        attended, self_max, self_total = attend_forward(queries, key_rows, value_rows, key_mask)
        middle = stream + product(attended, attend_out) + attend_bias[2].astype(jnp.float32)
        gain_second, shift_second, cross_proj, cross_back, cross_shift = fetch_cross(shards)
        cross_key_local = product(encoded, cross_proj[1]).astype(jnp.bfloat16)
        cross_value_local = (
            product(encoded, cross_proj[2]) + cross_shift[1].astype(jnp.float32)
        ).astype(jnp.bfloat16)
        cross_keys, cross_values = (
            lax.all_gather(cross_key_local, "seq", axis=0, tiled=True),
            lax.all_gather(cross_value_local, "seq", axis=0, tiled=True),
        )
        norm_full_second, pull_second = jax.vjp(
            norm_layer, middle, gain_second.astype(jnp.float32), shift_second.astype(jnp.float32)
        )
        norm_second = norm_full_second.astype(jnp.bfloat16)
        cross_queries = (
            product(norm_second, cross_proj[0]) + cross_shift[0].astype(jnp.float32)
        ).astype(jnp.bfloat16)
        cross_attended, cross_max, cross_total = attend_forward(
            cross_queries, cross_keys, cross_values, None
        )
        after_cross = (
            middle + product(cross_attended, cross_back) + cross_shift[2].astype(jnp.float32)
        )
        gain_third, shift_third, feed_up, feed_up_bias, feed_down, feed_down_bias = fetch_feed(
            shards
        )
        norm_full_third, pull_third = jax.vjp(
            norm_layer, after_cross, gain_third.astype(jnp.float32), shift_third.astype(jnp.float32)
        )
        norm_third = norm_full_third.astype(jnp.bfloat16)
        before = product(norm_third, feed_up) + feed_up_bias.astype(jnp.float32)
        activated_full, gelu_pull = jax.vjp(gelu_exact, before)
        activated = activated_full.astype(jnp.bfloat16)
        result = after_cross + product(activated, feed_down) + feed_down_bias.astype(jnp.float32)
        gain_third, shift_third, feed_up, feed_up_bias, feed_down, feed_down_bias = fetch_feed(
            shards
        )
        cot_float = cotangent.astype(jnp.float32)
        grad_act = product_right(cotangent, feed_down)
        grad_down = product_left(activated, cotangent)
        grad_down_bias = jnp.sum(cot_float, axis=0)
        grad_before = gelu_pull(grad_act)[0].astype(jnp.bfloat16)
        grad_up = product_left(norm_third, grad_before)
        grad_up_bias = column_sum(grad_before)
        grad_third = product_right(grad_before, feed_up)
        grad_after_norm, grad_gain_third, grad_shift_third = pull_third(grad_third)
        grad_after = cot_float + grad_after_norm
        gain_second, shift_second, cross_proj, cross_back, cross_shift = fetch_cross(shards)
        grad_after_low = grad_after.astype(jnp.bfloat16)
        grad_cross_back = product_left(cross_attended, grad_after_low)
        grad_cross_out_bias = column_sum(grad_after_low)
        grad_cross_attended = product_right(grad_after_low, cross_back).astype(jnp.bfloat16)
        grad_cross_queries, grad_cross_keys, grad_cross_values = attend_backward(
            cross_queries,
            cross_keys,
            cross_values,
            None,
            cross_max,
            cross_total,
            grad_cross_attended,
        )
        cross_key_part, cross_value_part = (
            lax.psum_scatter(
                grad_cross_keys.astype(jnp.bfloat16), "seq", scatter_dimension=0, tiled=True
            ).astype(jnp.float32),
            lax.psum_scatter(
                grad_cross_values.astype(jnp.bfloat16), "seq", scatter_dimension=0, tiled=True
            ).astype(jnp.float32),
        )
        cross_key_low = cross_key_part.astype(jnp.bfloat16)
        cross_value_low = cross_value_part.astype(jnp.bfloat16)
        cross_query_low = grad_cross_queries.astype(jnp.bfloat16)
        grad_cross_proj = jnp.stack(
            [
                product_left(norm_second, cross_query_low),
                product_left(encoded, cross_key_low),
                product_left(encoded, cross_value_low),
            ]
        )
        grad_cross_shift = jnp.stack(
            [column_sum(cross_query_low), column_sum(cross_value_low), grad_cross_out_bias]
        )
        encoder_grad = product_right(cross_key_low, cross_proj[1]) + product_right(
            cross_value_low, cross_proj[2]
        )
        grad_second = product_right(cross_query_low, cross_proj[0])
        grad_middle_norm, grad_gain_second, grad_shift_second = pull_second(grad_second)
        grad_middle = grad_after + grad_middle_norm
        gain_first, shift_first, attend_in, attend_out, attend_bias = fetch_self(shards)
        grad_middle_low = grad_middle.astype(jnp.bfloat16)
        grad_attend_out = product_left(attended, grad_middle_low)
        grad_out_bias = column_sum(grad_middle_low)
        grad_attended = product_right(grad_middle_low, attend_out).astype(jnp.bfloat16)
        grad_queries, grad_keys, grad_values = attend_backward(
            queries, key_rows, value_rows, key_mask, self_max, self_total, grad_attended
        )
        key_part, value_part = (
            lax.psum_scatter(
                grad_keys.astype(jnp.bfloat16), "seq", scatter_dimension=0, tiled=True
            ).astype(jnp.float32),
            lax.psum_scatter(
                grad_values.astype(jnp.bfloat16), "seq", scatter_dimension=0, tiled=True
            ).astype(jnp.float32),
        )
        key_low = key_part.astype(jnp.bfloat16)
        value_low = value_part.astype(jnp.bfloat16)
        query_low = grad_queries.astype(jnp.bfloat16)
        grad_attend_in = jnp.stack(
            [
                product_left(norm_first, query_low),
                product_left(norm_first, key_low),
                product_left(norm_first, value_low),
            ]
        )
        grad_attend_bias = jnp.stack([column_sum(query_low), column_sum(value_low), grad_out_bias])
        grad_first = (
            product_right(query_low, attend_in[0])
            + product_right(key_low, attend_in[1])
            + product_right(value_low, attend_in[2])
        )
        grad_stream_norm, grad_gain_first, grad_shift_first = pull_first(grad_first)
        tokens_grad = grad_middle + grad_stream_norm
        updates = (
            jnp.stack([grad_gain_first, grad_gain_second, grad_gain_third]),
            jnp.stack([grad_shift_first, grad_shift_second, grad_shift_third]),
            grad_attend_in,
            grad_attend_out,
            grad_attend_bias,
            grad_cross_proj,
            grad_cross_back,
            grad_cross_shift,
            grad_up,
            grad_up_bias,
            grad_down,
            grad_down_bias,
        )
        grad_sums = tuple((former + latter for former, latter in zip(grad_sums, updates)))
        return (grad_sums, (result.astype(jnp.bfloat16), tokens_grad, encoder_grad))

    starting = (
        jnp.zeros((3, model_width), jnp.float32),
        jnp.zeros((3, model_width), jnp.float32),
        jnp.zeros((3, model_width, model_width), jnp.float32),
        jnp.zeros((model_width, model_width), jnp.float32),
        jnp.zeros((3, model_width), jnp.float32),
        jnp.zeros((3, model_width, model_width), jnp.float32),
        jnp.zeros((model_width, model_width), jnp.float32),
        jnp.zeros((3, model_width), jnp.float32),
        jnp.zeros((model_width, hidden_width), jnp.float32),
        jnp.zeros((hidden_width,), jnp.float32),
        jnp.zeros((hidden_width, model_width), jnp.float32),
        jnp.zeros((model_width,), jnp.float32),
    )
    grad_sums, outputs = lax.scan(
        micro_step, starting, (tokens, encoder_states, out_grad, block_map, branch_fork)
    )
    feed_part = (
        lax.psum_scatter(grad_sums[8], ("dp", "seq"), scatter_dimension=0, tiled=True),
        lax.psum_scatter(grad_sums[9], ("dp", "seq"), scatter_dimension=0, tiled=True),
        lax.psum_scatter(grad_sums[10], ("dp", "seq"), scatter_dimension=0, tiled=True),
        lax.psum_scatter(grad_sums[11], ("dp", "seq"), scatter_dimension=0, tiled=True),
    )
    cross_part = (
        lax.psum_scatter(grad_sums[5], ("dp", "seq"), scatter_dimension=1, tiled=True),
        lax.psum_scatter(grad_sums[6], ("dp", "seq"), scatter_dimension=0, tiled=True),
        lax.psum_scatter(grad_sums[7], ("dp", "seq"), scatter_dimension=1, tiled=True),
    )
    self_part = (
        lax.psum_scatter(grad_sums[0], ("dp", "seq"), scatter_dimension=1, tiled=True),
        lax.psum_scatter(grad_sums[1], ("dp", "seq"), scatter_dimension=1, tiled=True),
        lax.psum_scatter(grad_sums[2], ("dp", "seq"), scatter_dimension=1, tiled=True),
        lax.psum_scatter(grad_sums[3], ("dp", "seq"), scatter_dimension=0, tiled=True),
        lax.psum_scatter(grad_sums[4], ("dp", "seq"), scatter_dimension=1, tiled=True),
    )
    return (
        outputs[0],
        outputs[1],
        outputs[2],
        self_part[0],
        self_part[1],
        self_part[2],
        self_part[3],
        self_part[4],
        cross_part[0],
        cross_part[1],
        cross_part[2],
        feed_part[0],
        feed_part[1],
        feed_part[2],
        feed_part[3],
    )


LOG2E = 1.4426950408889634
LN2 = 0.6931471805599453
QSCALE = HEAD ** (-0.5) * LOG2E
AXES = ("dp", "seq")
F32 = jnp.float32
BF16 = jnp.bfloat16
ANY = pl.BlockSpec(memory_space=pl.ANY)
SMEM = pl.BlockSpec(memory_space=pltpu.SMEM)


def nn(a, b):
    return lax.dot_general(a, b, (((1,), (0,)), ((), ())), preferred_element_type=F32)


def nt(a, b):
    return lax.dot_general(a, b, (((1,), (1,)), ((), ())), preferred_element_type=F32)


def tn(a, b):
    return lax.dot_general(a, b, (((0,), (0,)), ((), ())), preferred_element_type=F32)


def whole(shape):
    zeros = (0,) * len(shape)
    return pl.BlockSpec(shape, lambda *_: zeros)


def params(**kw):
    return pltpu.CompilerParams(vmem_limit_bytes=60 * 1024 * 1024, **kw)


def cost(flops, nbytes, trans=0):
    return pl.CostEstimate(flops=int(flops), bytes_accessed=int(nbytes), transcendentals=int(trans))


def stats(v):
    mean = jnp.mean(v, axis=-1, keepdims=True)
    centered = v - mean
    var = jnp.mean(centered * centered, axis=-1, keepdims=True)
    rstd = lax.rsqrt(var + 1e-05)
    return centered * rstd, rstd


def norm_back(v, e, gain):
    z, rstd = stats(v)
    f = e * gain
    grad = rstd * (
        f - jnp.mean(f, axis=-1, keepdims=True) - z * jnp.mean(f * z, axis=-1, keepdims=True)
    )
    return grad, jnp.sum(e * z, axis=0, keepdims=True), jnp.sum(e, axis=0, keepdims=True)


def qkv_kernel(meta, *refs):
    pieces = refs[:8]
    w_ref, vec_ref, bias_ref, q_ref, kv_ref, tr_ref, n1_ref, buf, sem = refs[8:]
    rows = buf.shape[0] // 8
    step = pl.program_id(0)

    @pl.when(step == 0)
    def _():
        copies = [
            pltpu.make_async_copy(pieces[i], buf.at[pl.ds(i * rows, rows), :], sem.at[i])
            for i in range(8)
        ]
        for c in copies:
            c.start()
        for c in copies:
            c.wait()

    gain, shift = vec_ref[0:1, :], vec_ref[3:4, :]
    w = w_ref[...]
    bias = bias_ref[0:1, :]
    for u in range(4):
        b = meta[32 + step * 4 + u]
        off = pl.multiple_of((b // 4) * rows + (b % 4) * 128, 32)
        x = buf[pl.ds(off, 128), :].astype(F32)
        z, _ = stats(x)
        n1 = (z * gain + shift).astype(BF16)
        r = slice(u * 128, (u + 1) * 128)
        n1_ref[r, :] = n1
        y = nn(n1, w) + bias
        kvt = jnp.transpose(y[:, 192:576]).astype(BF16)
        for t in range(2):
            for h in range(3):
                o = (t * 3 + h) * 64
                tr_ref[t * 3 + h, :, r] = kvt[o : o + 64, :]
        yq = (y[:, 0:192] * QSCALE).astype(BF16)
        yk = y[:, 192:576].astype(BF16)
        zero = jnp.zeros((128, 64), BF16)
        for h in range(3):
            q_ref[h, r, :] = jnp.concatenate([yq[:, h * 64 : h * 64 + 64], zero], axis=1)
            kv_ref[h, r, :] = jnp.concatenate(
                [yk[:, h * 64 : h * 64 + 64], yk[:, 192 + h * 64 : 256 + h * 64]], axis=1
            )


def qkv_call(meta, pieces, w2, vecs, bias):
    rows = pieces[0].shape[0]
    grid = (8,)
    return pl.pallas_call(
        qkv_kernel,
        grid_spec=pltpu.PrefetchScalarGridSpec(
            num_scalar_prefetch=1,
            grid=grid,
            in_specs=[ANY] * 8 + [whole(w2.shape), whole(vecs.shape), whole(bias.shape)],
            out_specs=[
                pl.BlockSpec((3, 512, 128), lambda i, m: (0, i, 0)),
                pl.BlockSpec((3, 512, 128), lambda i, m: (0, i, 0)),
                pl.BlockSpec((6, 64, 512), lambda i, m: (0, 0, i)),
                pl.BlockSpec((512, 768), lambda i, m: (i, 0)),
            ],
            scratch_shapes=[pltpu.VMEM((8 * rows, 768), BF16), pltpu.SemaphoreType.DMA((8,))],
        ),
        out_shape=[
            jax.ShapeDtypeStruct((3, 4096, 128), BF16),
            jax.ShapeDtypeStruct((3, 4096, 128), BF16),
            jax.ShapeDtypeStruct((6, 64, 4096), BF16),
            jax.ShapeDtypeStruct((4096, 768), BF16),
        ],
        compiler_params=params(dimension_semantics=("arbitrary",)),
        cost_estimate=cost(2 * 4096 * 768 * 576, 20e6),
        name="qkv",
    )(meta, *pieces, w2, vecs, bias)


def tile_mask(diag, kt, limit):
    key = lax.broadcasted_iota(jnp.int32, (256, 256), 0)
    if diag:
        return key <= lax.broadcasted_iota(jnp.int32, (256, 256), 1)
    return key + kt * 256 < limit


def attend_kernel(meta, q_ref, kv_ref, tr_ref, o_ref, lse_ref, m_ref, l_ref, acc_ref):
    def q_tile(qi, carry):
        branch = qi >= 8
        fork = meta[64 + jnp.maximum(qi - 8, 0)]
        full = jnp.where(branch, fork // 256, qi)
        qs = pl.ds(pl.multiple_of(qi * 256, 256), 256)
        m_ref[...] = jnp.full_like(m_ref, -1e30)
        l_ref[...] = jnp.zeros_like(l_ref)
        acc_ref[...] = jnp.zeros_like(acc_ref)

        def k_tile(kt, mask):
            ks = pl.ds(pl.multiple_of(kt * 256, 256), 256)
            for h in range(3):
                s = nt(kv_ref[h, ks, :], q_ref[h, qs, :])
                if mask is not None:
                    s = jnp.where(mask, s, -1e30)
                old = m_ref[h : h + 1, :]
                new = jnp.maximum(old, jnp.max(s, axis=0, keepdims=True))
                p = jnp.exp2(s - new)
                alpha = jnp.exp2(old - new)
                m_ref[h : h + 1, :] = new
                l_ref[h : h + 1, :] = l_ref[h : h + 1, :] * alpha + jnp.sum(p, axis=0, keepdims=True)
                hs = slice(h * 64, h * 64 + 64)
                acc_ref[hs, :] = acc_ref[hs, :] * alpha + nn(tr_ref[3 + h, :, ks], p.astype(BF16))

        def full_tile(kt, c):
            k_tile(kt, None)
            return c

        lax.fori_loop(0, full, full_tile, 0)

        @pl.when(branch & (fork % 256 != 0))
        def _():
            k_tile(full, tile_mask(False, full, fork))

        k_tile(qi, tile_mask(True, 0, 0))
        for h in range(3):
            hs = slice(h * 64, h * 64 + 64)
            l = l_ref[h : h + 1, :]
            acc_ref[hs, :] = acc_ref[hs, :] * (1.0 / l)
            lse_ref[h : h + 1, qs] = m_ref[h : h + 1, :] + jnp.log2(l)
        out = jnp.transpose(acc_ref[...]).astype(BF16)
        for u in range(2):
            o_ref[meta[32 + qi * 2 + u]] = out[u * 128 : (u + 1) * 128, :]
        return carry

    lax.fori_loop(0, 16, q_tile, 0)


def attend_call(meta, q, kv, tr):
    return pl.pallas_call(
        attend_kernel,
        grid_spec=pltpu.PrefetchScalarGridSpec(
            num_scalar_prefetch=1,
            grid=(1,),
            in_specs=[whole(q.shape), whole(kv.shape), whole(tr.shape)],
            out_specs=[whole((32, 128, 192)), whole((8, 4096))],
            scratch_shapes=[
                pltpu.VMEM((8, 256), F32),
                pltpu.VMEM((8, 256), F32),
                pltpu.VMEM((192, 256), F32),
            ],
        ),
        out_shape=[
            jax.ShapeDtypeStruct((32, 128, 192), BF16),
            jax.ShapeDtypeStruct((8, 4096), F32),
        ],
        compiler_params=params(dimension_semantics=("arbitrary",)),
        cost_estimate=cost(20e9, 10e6, 20e6),
        name="attend",
    )(meta, q, kv, tr)


def attend_back_kernel(
    meta, q_ref, kv_ref, tr_ref, o_ref, lse_ref, d0, d1, d2, d3, out_ref, do_ref, di_ref, dq_ref, acc_ref
):
    pieces = (d0, d1, d2, d3)
    zero = jnp.zeros((128, 64), BF16)
    for k in range(4):
        for kk in range(8):
            b = k * 8 + kk
            at = pl.ds(pl.multiple_of(meta[b] * 128, 128), 128)
            do = pieces[k][kk * 128 : (kk + 1) * 128, :]
            prod = jnp.transpose(do.astype(F32) * o_ref[b].astype(F32))
            for h in range(3):
                di_ref[h : h + 1, at] = jnp.sum(prod[h * 64 : h * 64 + 64, :], axis=0, keepdims=True)
                do_ref[h, at, :] = jnp.concatenate([zero, do[:, h * 64 : h * 64 + 64]], axis=1)
    acc_ref[...] = jnp.zeros_like(acc_ref)

    def q_tile(qi, carry):
        branch = qi >= 8
        fork = meta[64 + jnp.maximum(qi - 8, 0)]
        full = jnp.where(branch, fork // 256, qi)
        qs = pl.ds(pl.multiple_of(qi * 256, 256), 256)
        dq_ref[...] = jnp.zeros_like(dq_ref)

        def k_tile(kt, mask):
            ks = pl.ds(pl.multiple_of(kt * 256, 256), 256)
            for h in range(3):
                kv = kv_ref[h, ks, :]
                q, do = q_ref[h, qs, :], do_ref[h, qs, :]
                p = jnp.exp2(nt(kv, q) - lse_ref[h : h + 1, qs])
                if mask is not None:
                    p = jnp.where(mask, p, 0.0)
                ds = (p * (nt(kv, do) - di_ref[h : h + 1, qs])).astype(BF16)
                acc_ref[h, ks, :] += nn(ds, q) + nn(p.astype(BF16), do)
                hs = slice(h * 64, h * 64 + 64)
                dq_ref[hs, :] += nn(tr_ref[h, :, ks], ds)

        def full_tile(kt, c):
            k_tile(kt, None)
            return c

        lax.fori_loop(0, full, full_tile, 0)

        @pl.when(branch & (fork % 256 != 0))
        def _():
            k_tile(full, tile_mask(False, full, fork))

        k_tile(qi, tile_mask(True, 0, 0))
        out_ref[qs, 0:192] = (jnp.transpose(dq_ref[...]) * HEAD ** (-0.5)).astype(BF16)
        return carry

    lax.fori_loop(0, 16, q_tile, 0)

    def finish(t, carry):
        rs = pl.ds(pl.multiple_of(t * 256, 256), 256)
        a = [acc_ref[h, rs, :] for h in range(3)]
        dk = jnp.concatenate([v[:, 0:64] for v in a], axis=1) * LN2
        dv = jnp.concatenate([v[:, 64:128] for v in a], axis=1)
        out_ref[rs, 192:576] = jnp.concatenate([dk, dv], axis=1).astype(BF16)
        return carry

    lax.fori_loop(0, 16, finish, 0)


def attend_back_call(meta, q, kv, tr, o, lse, pieces):
    ins = [q, kv, tr, o, lse, *pieces]
    return pl.pallas_call(
        attend_back_kernel,
        grid_spec=pltpu.PrefetchScalarGridSpec(
            num_scalar_prefetch=1,
            grid=(1,),
            in_specs=[whole(v.shape) for v in ins],
            out_specs=whole((4096, 576)),
            scratch_shapes=[
                pltpu.VMEM((3, 4096, 128), BF16),
                pltpu.VMEM((8, 4096), F32),
                pltpu.VMEM((192, 256), F32),
                pltpu.VMEM((3, 4096, 128), F32),
            ],
        ),
        out_shape=jax.ShapeDtypeStruct((4096, 576), BF16),
        compiler_params=params(dimension_semantics=("arbitrary",)),
        cost_estimate=cost(50e9, 15e6, 20e6),
        name="attend_back",
    )(meta, *ins)


def dx_kernel(meta, d_ref, w_ref, out_ref, *, piece):
    kk = pl.program_id(0)
    at = pl.ds(pl.multiple_of(meta[piece * 8 + kk] * 128, 128), 128)
    out_ref[...] = nt(d_ref[at, :], w_ref[...]).astype(BF16)


def dx_call(meta, dqkv, w2, piece):
    return pl.pallas_call(
        functools.partial(dx_kernel, piece=piece),
        grid_spec=pltpu.PrefetchScalarGridSpec(
            num_scalar_prefetch=1,
            grid=(8,),
            in_specs=[whole(dqkv.shape), whole(w2.shape)],
            out_specs=pl.BlockSpec((128, 768), lambda i, m: (i, 0)),
        ),
        out_shape=jax.ShapeDtypeStruct((1024, 768), BF16),
        compiler_params=params(dimension_semantics=("arbitrary",)),
        cost_estimate=cost(2 * 1024 * 768 * 576, 6e6),
        name="dx%d" % piece,
    )(meta, dqkv, w2)


def win_kernel(n_ref, d_ref, g_ref, s_ref, acc_ref):
    step = pl.program_id(0)

    @pl.when(step == 0)
    def _():
        acc_ref[...] = jnp.zeros_like(acc_ref)
        s_ref[...] = jnp.zeros_like(s_ref)

    d = d_ref[...]
    acc_ref[...] += tn(n_ref[...], d)
    s_ref[0:1, :] += jnp.sum(d.astype(F32), axis=0, keepdims=True)

    @pl.when(step == pl.num_programs(0) - 1)
    def _():
        g_ref[...] = acc_ref[...].astype(BF16)


def win_call(n1, dqkv):
    return pl.pallas_call(
        win_kernel,
        grid=(4,),
        in_specs=[
            pl.BlockSpec((1024, 768), lambda i: (i, 0)),
            pl.BlockSpec((1024, 576), lambda i: (i, 0)),
        ],
        out_specs=[whole((768, 576)), whole((8, 576))],
        out_shape=[
            jax.ShapeDtypeStruct((768, 576), BF16),
            jax.ShapeDtypeStruct((8, 576), F32),
        ],
        scratch_shapes=[pltpu.VMEM((768, 576), F32)],
        compiler_params=params(dimension_semantics=("arbitrary",)),
        cost_estimate=cost(2 * 4096 * 768 * 576, 12e6),
        name="win",
    )(n1, dqkv)


def head_masks(frames):
    lane = lax.broadcasted_iota(jnp.int32, (frames, 128), 1) < 64
    return lane, jnp.logical_not(lane)


def mid_kernel(
    meta, tok_ref, o0, o1, o2, o3, so_ref, ci_ref, co_ref, fr_ref, vec_ref,
    mid_ref, ac_ref, n2_ref, n3_ref, cq_ref, ca_ref, lse_ref, kc_ref, vc_ref,
    km_ref, vmt_ref,
):
    frames = fr_ref.shape[0]
    hset = meta[72]

    @pl.when(pl.program_id(0) == 0)
    def _():
        fr = fr_ref[...]
        kc = nn(fr, ci_ref[1]).astype(BF16)
        vc = (nn(fr, ci_ref[2]) + vec_ref[10:11, :]).astype(BF16)
        kc_ref[...] = kc
        vc_ref[...] = vc
        zero = jnp.zeros((frames, 128), BF16)
        masks = head_masks(frames)
        for hp in range(6):
            ls = slice(hp * 128, hp * 128 + 128)
            for e in range(2):
                km_ref[hp * 2 + e] = jnp.where(masks[e], kc[:, ls], zero)
                vmt_ref[hp * 2 + e] = jnp.transpose(
                    jnp.where(masks[e], vc[:, ls].astype(F32), 0.0)
                ).astype(BF16)

    acc = tok_ref[...].astype(F32) + vec_ref[8:9, :]
    for k, o in enumerate((o0, o1, o2, o3)):
        at = pl.ds(pl.multiple_of((hset ^ k) * 192, 64), 192)
        acc = acc + nn(o[...], so_ref[at, :])
    mid_ref[...] = acc
    z, _ = stats(acc)
    n2 = (z * vec_ref[1:2, :] + vec_ref[4:5, :]).astype(BF16)
    n2_ref[...] = n2
    cq = ((nn(n2, ci_ref[0]) + vec_ref[9:10, :]) * QSCALE).astype(BF16)
    cq_ref[...] = cq
    ca = []
    for hp in range(6):
        qp = cq[:, hp * 128 : hp * 128 + 128]
        out = None
        for e in range(2):
            h = hp * 2 + e
            s = nt(km_ref[h], qp)
            m = jnp.max(s, axis=0, keepdims=True)
            p = jnp.exp2(s - m)
            l = jnp.sum(p, axis=0, keepdims=True)
            lse_ref[h : h + 1, :] = m + jnp.log2(l)
            part = nn(vmt_ref[h], p.astype(BF16)) * (1.0 / l)
            out = part if out is None else out + part
        ca.append(jnp.transpose(out).astype(BF16))
    ca = jnp.concatenate(ca, axis=1)
    ca_ref[...] = ca
    ac = acc + nn(ca, co_ref[...]) + vec_ref[11:12, :]
    ac_ref[...] = ac
    z, _ = stats(ac)
    n3_ref[...] = (z * vec_ref[2:3, :] + vec_ref[5:6, :]).astype(BF16)


def mid_call(meta, tok, pieces, so, ci, co, frames, vecs):
    rows, width = tok.shape
    tile = 256
    nf = frames.shape[0]
    row = pl.BlockSpec((tile, width), lambda i, m: (i, 0))
    row4 = pl.BlockSpec((tile, 192), lambda i, m: (i, 0))
    sds = jax.ShapeDtypeStruct
    return pl.pallas_call(
        mid_kernel,
        grid_spec=pltpu.PrefetchScalarGridSpec(
            num_scalar_prefetch=1,
            grid=(rows // tile,),
            in_specs=[row] + [row4] * 4
            + [whole(so.shape), whole(ci.shape), whole(co.shape), whole(frames.shape), whole(vecs.shape)],
            out_specs=[row] * 6
            + [pl.BlockSpec((16, tile), lambda i, m: (0, i)), whole((nf, width)), whole((nf, width))],
            scratch_shapes=[pltpu.VMEM((12, nf, 128), BF16), pltpu.VMEM((12, 128, nf), BF16)],
        ),
        out_shape=[
            sds((rows, width), F32), sds((rows, width), F32), sds((rows, width), BF16),
            sds((rows, width), BF16), sds((rows, width), BF16), sds((rows, width), BF16),
            sds((16, rows), F32), sds((nf, width), BF16), sds((nf, width), BF16),
        ],
        compiler_params=params(dimension_semantics=("arbitrary",)),
        cost_estimate=cost(8e9, 25e6, 3e6),
        name="middle",
    )(meta, tok, *pieces, so, ci, co, frames, vecs)


def normal_parts(b):
    e = jnp.exp2(b * b * (-0.5 * LOG2E))
    a = jnp.abs(b) * 0.7071067811865476
    t = 1.0 / (1.0 + 0.3275911 * a)
    poly = t * (
        0.254829592 + t * (-0.284496736 + t * (1.421413741 + t * (-1.453152027 + t * 1.061405429)))
    )
    tail = 0.5 * poly * e
    return jnp.where(b < 0.0, tail, 1.0 - tail), e * 0.3989422804014327


def feed_kernel(
    n3_ref, og_ref, ac_ref, up_ref, dn_ref, ub_ref, vec_ref,
    res_ref, gt_ref, ug_ref, dg_ref, ubg_ref, dbg_ref,
    acc_ref, n3t_ref, act_ref, gb_ref,
):
    step = pl.program_id(0)
    rows, width = n3_ref.shape

    @pl.when(step == 0)
    def _():
        acc_ref[...] = ac_ref[...] + vec_ref[12:13, :]
        gt_ref[...] = jnp.zeros_like(gt_ref)
        dbg_ref[...] = jnp.zeros_like(dbg_ref)
        dbg_ref[0:1, :] = jnp.sum(og_ref[...].astype(F32), axis=0, keepdims=True)
        n3t_ref[...] = jnp.transpose(n3_ref[...])

    up = up_ref[...].reshape(width, width)
    dn = dn_ref[...].reshape(width, width)
    ub = ub_ref[pl.ds(step, 1), :]
    total = jnp.zeros((1, width), F32)
    for r in range(rows // 256):
        rs = slice(r * 256, (r + 1) * 256)
        n3 = n3_ref[rs, :]
        og = og_ref[rs, :]
        b = nn(n3, up) + ub
        cdf, pdf = normal_parts(b)
        act = (b * cdf).astype(BF16)
        gb = (nt(og, dn) * (cdf + b * pdf)).astype(BF16)
        act_ref[rs, :] = act
        gb_ref[rs, :] = gb
        total = total + jnp.sum(gb.astype(F32), axis=0, keepdims=True)
        acc_ref[rs, :] += nn(act, dn)
        gt_ref[rs, :] += nt(gb, up)
    ubg_ref[...] = jnp.broadcast_to(total, (8, width))
    ug_ref[...] = nn(n3t_ref[...], gb_ref[...]).astype(BF16).reshape(ug_ref.shape)
    dg_ref[...] = tn(act_ref[...], og_ref[...]).astype(BF16).reshape(dg_ref.shape)

    @pl.when(step == pl.num_programs(0) - 1)
    def _():
        res_ref[...] = acc_ref[...].astype(BF16)


def feed_call(n3, og, ac, up4, dn4, ub4, vecs):
    rows, width = n3.shape
    sds = jax.ShapeDtypeStruct
    tiles = up4.shape[0]
    tile = pl.BlockSpec((1, width, width), lambda i: (i, 0, 0))
    return pl.pallas_call(
        feed_kernel,
        grid=(tiles,),
        in_specs=[whole(n3.shape), whole(og.shape), whole(ac.shape), tile, tile, whole(ub4.shape), whole(vecs.shape)],
        out_specs=[
            whole((rows, width)), whole((rows, width)), tile, tile,
            pl.BlockSpec((8, width), lambda i: (i, 0)), whole((8, width)),
        ],
        out_shape=[
            sds((rows, width), BF16), sds((rows, width), F32),
            sds((tiles, width, width), BF16), sds((tiles, width, width), BF16),
            sds((tiles * 8, width), F32), sds((8, width), F32),
        ],
        scratch_shapes=[
            pltpu.VMEM((rows, width), F32), pltpu.VMEM((width, rows), BF16),
            pltpu.VMEM((rows, width), BF16), pltpu.VMEM((rows, width), BF16),
        ],
        compiler_params=params(dimension_semantics=("arbitrary",)),
        cost_estimate=cost(2 * 6 * rows * width * width * tiles, 35e6, 6e6),
        name="feed",
    )(n3, og, ac, up4, dn4, ub4, vecs)


def mid_back_kernel(
    meta, gt_ref, og_ref, ac_ref, mid_ref, n2_ref, cq_ref, ca_ref, lse_ref, kc_ref, vc_ref,
    fr_ref, so_ref, ci_ref, co_ref, vec_ref, o0, o1, o2, o3,
    gm_ref, do0, do1, do2, do3, sog_ref, cig_ref, cog_ref, eg_ref, sums_ref,
    km_ref, kmt_ref, vm_ref, dk_ref, dv_ref, so_acc, cq_acc, co_acc,
):
    frames = fr_ref.shape[0]
    hset = meta[72]
    step = pl.program_id(0)
    last = pl.num_programs(0) - 1
    masks = head_masks(frames)

    @pl.when(step == 0)
    def _():
        zero = jnp.zeros((frames, 128), BF16)
        for hp in range(6):
            ls = slice(hp * 128, hp * 128 + 128)
            k, v = kc_ref[:, ls], vc_ref[:, ls]
            for e in range(2):
                km_ref[hp * 2 + e] = jnp.where(masks[e], k, zero)
                vm_ref[hp * 2 + e] = jnp.where(masks[e], v, zero)
                kmt_ref[hp * 2 + e] = jnp.transpose(
                    jnp.where(masks[e], k.astype(F32), 0.0)
                ).astype(BF16)
        for ref in (dk_ref, dv_ref, so_acc, cq_acc, co_acc, sums_ref):
            ref[...] = jnp.zeros_like(ref)

    def count(row, value):
        sums_ref[row : row + 1, :] += value

    gt = gt_ref[...]
    back, gain, shift = norm_back(ac_ref[...], gt, vec_ref[2:3, :])
    count(2, gain)
    count(5, shift)
    ga = og_ref[...].astype(F32) + back
    gal = ga.astype(BF16)
    count(11, jnp.sum(gal.astype(F32), axis=0, keepdims=True))
    ca = ca_ref[...]
    co_acc[...] += tn(ca, gal)
    dca = nt(gal, co_ref[...]).astype(BF16)
    cq = cq_ref[...]
    dq = []
    for hp in range(6):
        ls = slice(hp * 128, hp * 128 + 128)
        qp, dp_ = cq[:, ls], dca[:, ls]
        dqt = None
        parts = []
        for e in range(2):
            h = hp * 2 + e
            p = jnp.exp2(nt(km_ref[h], qp) - lse_ref[h : h + 1, :])
            dp = nt(vm_ref[h], dp_)
            inner = jnp.sum(dp * p, axis=0, keepdims=True)
            ds = (p * (dp - inner)).astype(BF16)
            part = nn(kmt_ref[h], ds)
            dqt = part if dqt is None else dqt + part
            parts.append((nn(ds, qp), nn(p.astype(BF16), dp_)))
        dq.append(jnp.transpose(dqt))
        dk_ref[:, ls] += jnp.where(masks[0], parts[0][0], parts[1][0])
        dv_ref[:, ls] += jnp.where(masks[0], parts[0][1], parts[1][1])
    dcq = (jnp.concatenate(dq, axis=1) * HEAD ** (-0.5)).astype(BF16)
    count(9, jnp.sum(dcq.astype(F32), axis=0, keepdims=True))
    cq_acc[...] += tn(n2_ref[...], dcq)
    gs = nt(dcq, ci_ref[0])
    back, gain, shift = norm_back(mid_ref[...], gs, vec_ref[1:2, :])
    count(1, gain)
    count(4, shift)
    gm = ga + back
    gm_ref[...] = gm
    gml = gm.astype(BF16)
    count(8, jnp.sum(gml.astype(F32), axis=0, keepdims=True))
    for k, (o, do) in enumerate(zip((o0, o1, o2, o3), (do0, do1, do2, do3))):
        at = pl.ds(pl.multiple_of((hset ^ k) * 192, 64), 192)
        do[...] = nt(gml, so_ref[at, :]).astype(BF16)
        so_acc[at, :] += tn(o[...], gml)

    @pl.when(step == last)
    def _():
        dk = (dk_ref[...] * LN2).astype(BF16)
        dv = dv_ref[...].astype(BF16)
        count(10, jnp.sum(dv.astype(F32), axis=0, keepdims=True))
        fr = fr_ref[...]
        sog_ref[...] = so_acc[...].astype(BF16)
        cog_ref[...] = co_acc[...].astype(BF16)
        cig_ref[0] = cq_acc[...].astype(BF16)
        cig_ref[1] = tn(fr, dk).astype(BF16)
        cig_ref[2] = tn(fr, dv).astype(BF16)
        eg_ref[...] = (nt(dk, ci_ref[1]) + nt(dv, ci_ref[2])).astype(BF16)


def mid_back_call(meta, gt, og, ac, mid, n2, cq, ca, lse, kc, vc, frames, so, ci, co, vecs, pieces):
    rows, width = gt.shape
    tile = 256
    nf = frames.shape[0]
    row = pl.BlockSpec((tile, width), lambda i, m: (i, 0))
    row4 = pl.BlockSpec((tile, 192), lambda i, m: (i, 0))
    sds = jax.ShapeDtypeStruct
    acc = pltpu.VMEM((width, width), F32)
    return pl.pallas_call(
        mid_back_kernel,
        grid_spec=pltpu.PrefetchScalarGridSpec(
            num_scalar_prefetch=1,
            grid=(rows // tile,),
            in_specs=[row] * 7
            + [pl.BlockSpec((16, tile), lambda i, m: (0, i))]
            + [whole(v.shape) for v in (kc, vc, frames, so, ci, co, vecs)]
            + [row4] * 4,
            out_specs=[row] + [row4] * 4
            + [whole((width, width)), whole((3, width, width)), whole((width, width)), whole((nf, width)), whole((24, width))],
            scratch_shapes=[
                pltpu.VMEM((12, nf, 128), BF16), pltpu.VMEM((12, 128, nf), BF16), pltpu.VMEM((12, nf, 128), BF16),
                pltpu.VMEM((nf, width), F32), pltpu.VMEM((nf, width), F32), acc, acc, acc,
            ],
        ),
        out_shape=[sds((rows, width), F32)] + [sds((rows, 192), BF16)] * 4
        + [sds((width, width), BF16), sds((3, width, width), BF16), sds((width, width), BF16), sds((nf, width), BF16), sds((24, width), F32)],
        compiler_params=params(dimension_semantics=("arbitrary",)),
        cost_estimate=cost(22e9, 35e6, 3e6),
        name="middle_back",
    )(meta, gt, og, ac, mid, n2, cq, ca, lse, kc, vc, frames, so, ci, co, vecs, *pieces)


def first_back_kernel(a_ref, b_ref, gm_ref, tok_ref, vec_ref, out_ref, sums_ref):
    @pl.when(pl.program_id(0) == 0)
    def _():
        sums_ref[...] = jnp.zeros_like(sums_ref)

    e = a_ref[...].astype(F32) + b_ref[...].astype(F32)
    back, gain, shift = norm_back(tok_ref[...].astype(F32), e, vec_ref[0:1, :])
    sums_ref[0:1, :] += gain
    sums_ref[1:2, :] += shift
    out_ref[...] = (gm_ref[...] + back).astype(BF16)


def first_back_call(a, b, gm, tok, vecs, part):
    width = a.shape[1]
    base = part * 2
    row = pl.BlockSpec((256, width), lambda i: (i, 0))
    off = pl.BlockSpec((256, width), lambda i: (i + base, 0))
    return pl.pallas_call(
        first_back_kernel,
        grid=(2,),
        in_specs=[row, row, off, off, whole(vecs.shape)],
        out_specs=[row, whole((8, width))],
        out_shape=[jax.ShapeDtypeStruct((512, width), BF16), jax.ShapeDtypeStruct((8, width), F32)],
        compiler_params=params(dimension_semantics=("arbitrary",)),
        cost_estimate=cost(1e7, 6e6),
        name="first_back%d" % part,
    )(a, b, gm, tok, vecs)


def device_pairs(dp_count, move, back=False):
    pairs = []
    for dp in range(dp_count):
        for seq in range(8):
            y, c, z, x = move(dp // 2, dp % 2, seq // 2, seq % 2)
            pair = (dp * 8 + seq, (y * 2 + c) * 8 + z * 2 + x)
            pairs.append(pair[::-1] if back else pair)
    return pairs


def home_body(
    tokens, encoder_states, out_grad, block_map, branch_fork, norm_gain, norm_bias, self_in,
    self_out, self_bias, cross_in, cross_out, cross_bias, up_weight, up_bias, down_weight, down_bias,
):
    dp_count = lax.axis_size("dp")
    dp, seq = lax.axis_index("dp"), lax.axis_index("seq")
    c, z, x = dp & 1, seq >> 1, seq & 1
    y = dp >> 1
    flat = dp * 8 + seq
    hset = 2 * c + x
    parity = z & 1
    rows, width = tokens.shape[1:]
    frames = encoder_states.shape[1]

    def send(v, move, back=False):
        return lax.ppermute(v, AXES, device_pairs(dp_count, move, back))

    def flip(k):
        return lambda y, c, z, x: (y, c ^ (k >> 1), z, x ^ (k & 1))

    def home(p):
        return lambda y, c, z, x: (y, z >> 1, 2 * c + (p ^ (z & 1)), x)

    def pick(v, p):
        return jnp.where(parity == p, v[0], v[1])

    def piece(v, parts):
        return v.reshape(parts, -1).astype(BF16)

    small = jnp.concatenate(
        [v.reshape(-1) for v in (norm_gain, norm_bias, self_bias, cross_bias, down_bias, up_bias)]
    )
    small = jnp.pad(small, (0, 8 * 192 - small.shape[0])).reshape(8, 192)
    shard = self_in.reshape(-1, width)
    options = jnp.stack(
        [jnp.concatenate([shard[:, 192 * j : 192 * j + 192], small]) for j in range(4)]
    )

    def merge(own, other, bit):
        return jnp.stack([jnp.where(bit == 0, own, other), jnp.where(bit == 0, other, own)])

    def option(k):
        return lax.dynamic_index_in_dim(options, hset ^ k, 0, False)

    got = [option(0)] + [send(option(k), flip(k)) for k in (1, 2, 3)]
    tree = merge(merge(got[0], got[1], x), merge(got[2], got[3], x), c)
    tree = merge(tree, send(tree, lambda y, c, z, x: (y, c, z ^ 2, x)), z >> 1)
    tree = merge(tree, send(tree, lambda y, c, z, x: (y, c, z ^ 1, x)), z & 1)
    for bit in range((dp_count // 2).bit_length() - 1):
        tree = merge(
            tree, send(tree, lambda y, c, z, x, bit=bit: (y ^ (1 << bit), c, z, x)), (y >> bit) & 1
        )
    y_count = dp_count // 2
    nw = shard.shape[0] // 3
    tree = tree.reshape(y_count, 2, 2, 2, 2, 3 * nw + 8, 192).transpose(0, 3, 2, 1, 4, 5, 6)
    tree = tree.reshape(dp_count * 8, 3 * nw + 8, 192)
    w2 = jnp.concatenate(
        [tree[:, t * nw : (t + 1) * nw].reshape(width, 192) for t in range(3)], axis=1
    )
    flats = tree[:, 3 * nw :].reshape(dp_count * 8, -1)
    lists = [
        flats[:, i * nw : (i + 1) * nw].reshape(1, width) for i in range(13)
    ]
    tiles = up_weight.shape[1] // width
    ub4 = flats[:, 13 * nw : (13 + tiles) * nw].reshape(tiles, width).astype(F32)
    vecs = jnp.concatenate(lists + [jnp.zeros((3, width), BF16)]).astype(F32)
    own_cols = lambda v: lax.dynamic_slice_in_dim(v, hset * 192, 192, 1)
    zero_row = jnp.zeros((1, 192), F32)
    qkv_bias = jnp.concatenate([own_cols(vecs[6:7]), zero_row, own_cols(vecs[7:8])], axis=1)

    both = jnp.concatenate([tokens, encoder_states], axis=1)
    mine = [send(pick(both, p), home(p)) for p in range(2)]
    across = [send(v, flip(1)) for v in mine]
    near = [send(v, flip(2)) for v in mine]
    far = [send(v, flip(2)) for v in across]
    pieces = mine + across + near + far

    info = jnp.concatenate([block_map, branch_fork], axis=1)
    info = jnp.where((z >> 1) == c, info, send(info, flip(2)))
    info = jnp.where(parity == 0, info[0], info[1])
    place = jnp.arange(32, dtype=jnp.int32)
    k_of, p_of = place >> 3, (place >> 2) & 1
    stored = (2 * (2 * (c ^ (k_of >> 1)) + (p_of ^ parity)) + (x ^ (k_of & 1))) * 4 + (place & 3)
    logical = jnp.sum(jnp.where(stored[:, None] == place[None, :], info[None, :32], 0), axis=1)
    spot = jnp.sum(jnp.where(logical[None, :] == place[:, None], place[None, :], 0), axis=1)
    meta = jnp.concatenate(
        [logical, spot, info[32:40], jnp.full((56,), hset, jnp.int32)]
    ).astype(jnp.int32)

    dense = jnp.concatenate(
        [down_weight]
        + [up_weight[:, j * width : (j + 1) * width] for j in range(tiles)]
        + [self_out, cross_in[0], cross_in[1], cross_in[2], cross_out]
    )
    dense = lax.all_gather(dense, AXES, axis=0)
    nd = down_weight.shape[0]

    def gathered(i):
        at = nd + i * nw
        return dense[:, at : at + nw].reshape(width, width)

    dn4 = dense[:, :nd].reshape(tiles, width, width)
    up4 = jnp.stack([gathered(j) for j in range(tiles)])
    so = gathered(tiles)
    ci = jnp.stack([gathered(tiles + 1 + t) for t in range(3)])
    co = gathered(tiles + 4)

    q, kv, tr, n1 = qkv_call(meta, pieces, w2, vecs, qkv_bias)
    og_pair, _ = lax.optimization_barrier((out_grad, far[1]))
    og = jnp.concatenate([send(pick(og_pair, p), home(p)) for p in range(2)])
    tok = jnp.concatenate([v[:rows] for v in mine])
    all_frames = jnp.concatenate([v[rows:] for v in pieces])

    o, lse = attend_call(meta, q, kv, tr)
    o4 = o.reshape(4, 1024, 192)
    o_home = [o4[0]] + [send(o4[k], flip(k)) for k in (1, 2, 3)]
    mid, ac, n2, n3, cq, ca, lse_c, kc, vc = mid_call(
        meta, tok, o_home, so, ci, co, all_frames, vecs
    )
    res, gt, ug, dg, ubg, dbg = feed_call(n3, og, ac, up4, dn4, ub4, vecs)
    gm, d0, d1, d2, d3, sog, cig, cog, eg, sums = mid_back_call(
        meta, gt, og, ac, mid, n2, cq, ca, lse_c, kc, vc, all_frames, so, ci, co, vecs, o_home
    )
    d_home = [d0] + [send(d, flip(k)) for k, d in ((1, d1), (2, d2), (3, d3))]

    def rows_of(grad):
        return grad.reshape(dp_count * 8, -1, width)

    packed = jnp.concatenate(
        [rows_of(dg)] + [rows_of(ug[j]) for j in range(tiles)]
        + [rows_of(sog), rows_of(cig[0]), rows_of(cig[1]), rows_of(cig[2]), rows_of(cog)],
        axis=1,
    )
    dense_grad = lax.psum_scatter(packed, AXES, scatter_dimension=0, tiled=True)[0].astype(F32)

    dqkv = attend_back_call(meta, q, kv, tr, o, lse, d_home)
    dx3 = dx_call(meta, dqkv, w2, 3)
    near3 = send(dx3, flip(2))
    dx1 = dx_call(meta, dqkv, w2, 1)
    side = (dx1.astype(F32) + near3.astype(F32)).astype(BF16)
    side = [send(side[p * rows : (p + 1) * rows], flip(1)) for p in range(2)]
    dx2 = dx_call(meta, dqkv, w2, 2)
    near2 = send(dx2, flip(2))
    dx0 = dx_call(meta, dqkv, w2, 0)
    own = (dx0.astype(F32) + near2.astype(F32)).astype(BF16)

    wg, colsum = win_call(n1, dqkv)
    wg = wg.reshape(y_count, 2, 4, 2, nw, 576)

    def halve(v, move, bit, axis):
        keep = lax.dynamic_index_in_dim(v, bit, axis, False)
        give = lax.dynamic_index_in_dim(v, 1 - bit, axis, False)
        return (keep.astype(F32) + send(give, move).astype(F32)).astype(BF16)

    for bit in reversed(range((dp_count // 2).bit_length() - 1)):
        half = wg.shape[0] // 2
        wg = halve(
            wg.reshape((2, half) + wg.shape[1:]),
            lambda y, c, z, x, bit=bit: (y ^ (1 << bit), c, z, x), (y >> bit) & 1, 0,
        )
    wg = wg.reshape(2, 2, 2, 2, nw, 576)
    wg = halve(wg, lambda y, c, z, x: (y, c, z ^ 1, x), z & 1, 2)
    wg = halve(wg, lambda y, c, z, x: (y, c, z ^ 2, x), z >> 1, 1)
    wg = wg.reshape(4, nw, 576)

    def shard_for(k):
        return lax.dynamic_index_in_dim(wg, hset ^ k, 0, False)

    parts = jnp.stack([shard_for(0)] + [send(shard_for(k), flip(k)) for k in (1, 2, 3)])
    cols = [lax.dynamic_index_in_dim(parts, hset ^ j, 0, False) for j in range(4)]
    self_in_grad = jnp.stack(
        [jnp.concatenate([v[:, 192 * t : 192 * t + 192] for v in cols], axis=1) for t in range(3)]
    ).astype(F32)

    grads, first_sums = [], None
    for p in range(2):
        tg, s = first_back_call(own[p * rows : (p + 1) * rows], side[p], gm, tok, vecs, p)
        grads.append(send(tg, home(p), True))
        first_sums = s if first_sums is None else first_sums + s
    results = [send(res[p * rows : (p + 1) * rows], home(p), True) for p in range(2)]
    eg4 = eg.reshape(4, 2 * frames, width)
    eg_near = send(eg4[2:4], flip(2)).astype(F32)
    eg_side = (eg4[1].astype(F32) + eg_near[1]).astype(BF16)
    eg_sum = eg4[0].astype(F32) + eg_near[0] + send(eg_side, flip(1)).astype(F32)
    eg_sum = eg_sum.astype(BF16)
    eg_back = [send(eg_sum[p * frames : (p + 1) * frames], home(p), True) for p in range(2)]

    def returned(pair, dtype):
        pair = [v.astype(dtype) for v in pair]
        return jnp.stack([jnp.where(parity == 0, pair[0], pair[1]), jnp.where(parity == 0, pair[1], pair[0])])

    own_bias = lambda v: lax.dynamic_update_slice(
        jnp.zeros((1, width), F32), v, (0, hset * 192)
    )
    ubg = ubg.reshape(tiles, 8, width)[:, 0]
    table = jnp.concatenate(
        [
            first_sums[0:1], sums[1:3], first_sums[1:2], sums[4:6],
            own_bias(colsum[0:1, 0:192]), own_bias(colsum[0:1, 384:576]), sums[8:12],
            dbg[0:1], ubg, jnp.zeros((24 - 13 - tiles, width), F32),
        ]
    )
    for k in (1, 2):
        table = table + send(table, flip(k))
    table = table + send(table, lambda y, c, z, x: (y, c, z ^ 1, x))
    table = table + send(table, lambda y, c, z, x: (y, c, z ^ 2, x))
    for bit in range((dp_count // 2).bit_length() - 1):
        table = table + send(table, lambda y, c, z, x, bit=bit: (y ^ (1 << bit), c, z, x))
    mine_of = lambda v: lax.dynamic_slice_in_dim(v, flat * nw, nw, 1)
    vec_grad = mine_of(table[:13])
    up_bias_grad = lax.dynamic_slice_in_dim(
        table[13 : 13 + tiles].reshape(-1), flat * tiles * nw, tiles * nw, 0
    )

    def shard_grad(i):
        at = nd + i * nw
        return dense_grad[at : at + nw]

    return (
        returned(results, BF16),
        returned(grads, F32),
        returned(eg_back, F32),
        vec_grad[0:3],
        vec_grad[3:6],
        self_in_grad,
        shard_grad(tiles),
        vec_grad[6:9],
        jnp.stack([shard_grad(tiles + 1 + t) for t in range(3)]),
        shard_grad(tiles + 4),
        vec_grad[9:12],
        jnp.concatenate([shard_grad(j) for j in range(tiles)], axis=1),
        up_bias_grad,
        dense_grad[:nd],
        vec_grad[12],
    )


def solution(mesh):
    in_specs = (
        P("dp", "seq", None),
        P("dp", "seq", None),
        P("dp", "seq", None),
        P("dp", None),
        P("dp", None),
        P(None, ("dp", "seq")),
        P(None, ("dp", "seq")),
        P(None, ("dp", "seq"), None),
        P(("dp", "seq"), None),
        P(None, ("dp", "seq")),
        P(None, ("dp", "seq"), None),
        P(("dp", "seq"), None),
        P(None, ("dp", "seq")),
        P(("dp", "seq"), None),
        P(("dp", "seq")),
        P(("dp", "seq"), None),
        P(("dp", "seq")),
    )
    out_specs = (
        P("dp", "seq", None),
        P("dp", "seq", None),
        P("dp", "seq", None),
        P(None, ("dp", "seq")),
        P(None, ("dp", "seq")),
        P(None, ("dp", "seq"), None),
        P(("dp", "seq"), None),
        P(None, ("dp", "seq")),
        P(None, ("dp", "seq"), None),
        P(("dp", "seq"), None),
        P(None, ("dp", "seq")),
        P(("dp", "seq"), None),
        P(("dp", "seq")),
        P(("dp", "seq"), None),
        P(("dp", "seq")),
    )
    sizes = dict(mesh.shape)
    chosen = home_body if sizes["dp"] == 4 and sizes["seq"] == 8 else body
    return jax.shard_map(chosen, mesh=mesh, in_specs=in_specs, out_specs=out_specs, check_vma=False)
```

```python
import functools

import jax
import jax.numpy as jnp
from jax import lax
from jax.experimental import pallas as pl
from jax.experimental.pallas import tpu as pltpu
from jax.sharding import PartitionSpec as P

HEADS = 12
HEAD = 64
PROMPT = 2048
BRANCHES = 8
BLEN = 256
BLOCK = 128


def product(former, latter):
    return jnp.dot(former, latter, preferred_element_type=jnp.float32)


def product_left(former, latter):
    return lax.dot_general(
        former, latter, (((0,), (0,)), ((), ())), preferred_element_type=jnp.float32
    )


def product_right(former, latter):
    return lax.dot_general(
        former, latter, (((1,), (1,)), ((), ())), preferred_element_type=jnp.float32
    )


def column_sum(matrix):
    return jnp.sum(matrix.astype(jnp.float32), axis=0)


def norm_layer(stream, norm_gain, norm_shift):
    center = jnp.mean(stream, axis=-1, keepdims=True)
    centered = stream - center
    spread = jnp.mean(centered * centered, axis=-1, keepdims=True)
    return centered * lax.rsqrt(spread + 1e-05) * norm_gain + norm_shift


def gelu_exact(before):
    return jax.nn.gelu(before, approximate=False)


def token_info(blocks, branch_forks):
    offsets = jnp.arange(BLOCK, dtype=jnp.int32)
    logical = (blocks[:, None] * BLOCK + offsets[None, :]).reshape(-1)
    relative = logical - PROMPT
    in_branch = relative >= 0
    segment = jnp.where(in_branch, relative // BLEN + 1, 0)
    position = jnp.where(in_branch, relative % BLEN, logical)
    labels = jnp.arange(1, BRANCHES + 1, dtype=jnp.int32)
    fork_reach = jnp.sum(
        jnp.where(segment[:, None] == labels[None, :], branch_forks[None, :], 0), axis=1
    )
    return (segment, position, fork_reach)


def allowed(query_info, key_info):
    same = (query_info[0][:, None] == key_info[0][None, :]) & (
        key_info[1][None, :] <= query_info[1][:, None]
    )
    shared = (
        (query_info[0][:, None] > 0)
        & (key_info[0][None, :] == 0)
        & (key_info[1][None, :] < query_info[2][:, None])
    )
    return same | shared


def head_split(matrix):
    return matrix.reshape(matrix.shape[0], HEADS, HEAD)


def score_block(queries, key_rows, key_mask):
    scores = jnp.einsum(
        "rhd,khd->hrk",
        head_split(queries),
        head_split(key_rows),
        preferred_element_type=jnp.float32,
    ) * HEAD ** (-0.5)
    if key_mask is None:
        return scores
    return jnp.where(key_mask[None], scores, -1e30)


def attend_forward(queries, key_rows, value_rows, key_mask):
    scores = score_block(queries, key_rows, key_mask)
    row_max = jnp.max(scores, axis=2, keepdims=True)
    weights = jnp.exp(scores - row_max)
    row_total = jnp.sum(weights, axis=2, keepdims=True)
    shares = (weights / row_total).astype(jnp.bfloat16)
    attended = jnp.einsum(
        "hrk,khd->rhd", shares, head_split(value_rows), preferred_element_type=jnp.float32
    )
    return (attended.reshape(queries.shape[0], -1).astype(jnp.bfloat16), row_max, row_total)


def attend_backward(queries, key_rows, value_rows, key_mask, row_max, row_total, incoming):
    scores = score_block(queries, key_rows, key_mask)
    shares_full = jnp.exp(scores - row_max) / row_total
    shares_low = shares_full.astype(jnp.bfloat16)
    grad_heads = head_split(incoming)
    grad_values = jnp.einsum(
        "hrk,rhd->khd", shares_low, grad_heads, preferred_element_type=jnp.float32
    )
    grad_shares = jnp.einsum(
        "rhd,khd->hrk", grad_heads, head_split(value_rows), preferred_element_type=jnp.float32
    )
    inner_sum = jnp.sum(grad_shares * shares_full, axis=2, keepdims=True)
    grad_scores = (shares_full * (grad_shares - inner_sum)).astype(jnp.bfloat16)
    grad_queries = jnp.einsum(
        "hrk,khd->rhd", grad_scores, head_split(key_rows), preferred_element_type=jnp.float32
    ) * HEAD ** (-0.5)
    grad_keys = jnp.einsum(
        "hrk,rhd->khd", grad_scores, head_split(queries), preferred_element_type=jnp.float32
    ) * HEAD ** (-0.5)
    row_count = queries.shape[0]
    key_count = key_rows.shape[0]
    return (
        grad_queries.reshape(row_count, -1),
        grad_keys.reshape(key_count, -1),
        grad_values.reshape(key_count, -1),
    )


def fetch_self(shards):
    return (
        lax.all_gather(shards[0][0], ("dp", "seq"), axis=0, tiled=True),
        lax.all_gather(shards[1][0], ("dp", "seq"), axis=0, tiled=True),
        lax.all_gather(shards[2], ("dp", "seq"), axis=1, tiled=True),
        lax.all_gather(shards[3], ("dp", "seq"), axis=0, tiled=True),
        lax.all_gather(shards[4], ("dp", "seq"), axis=1, tiled=True),
    )


def fetch_cross(shards):
    return (
        lax.all_gather(shards[0][1], ("dp", "seq"), axis=0, tiled=True),
        lax.all_gather(shards[1][1], ("dp", "seq"), axis=0, tiled=True),
        lax.all_gather(shards[5], ("dp", "seq"), axis=1, tiled=True),
        lax.all_gather(shards[6], ("dp", "seq"), axis=0, tiled=True),
        lax.all_gather(shards[7], ("dp", "seq"), axis=1, tiled=True),
    )


def fetch_feed(shards):
    return (
        lax.all_gather(shards[0][2], ("dp", "seq"), axis=0, tiled=True),
        lax.all_gather(shards[1][2], ("dp", "seq"), axis=0, tiled=True),
        lax.all_gather(shards[8], ("dp", "seq"), axis=0, tiled=True),
        lax.all_gather(shards[9], ("dp", "seq"), axis=0, tiled=True),
        lax.all_gather(shards[10], ("dp", "seq"), axis=0, tiled=True),
        lax.all_gather(shards[11], ("dp", "seq"), axis=0, tiled=True),
    )


def body(
    tokens,
    encoder_states,
    out_grad,
    block_map,
    branch_fork,
    norm_gain,
    norm_bias,
    self_in,
    self_out,
    self_bias,
    cross_in,
    cross_out,
    cross_bias,
    up_weight,
    up_bias,
    down_weight,
    down_bias,
):
    shards = (
        norm_gain,
        norm_bias,
        self_in,
        self_out,
        self_bias,
        cross_in,
        cross_out,
        cross_bias,
        up_weight,
        up_bias,
        down_weight,
        down_bias,
    )
    model_width = tokens.shape[2]
    hidden_width = up_weight.shape[1]
    seq_count = lax.axis_size("seq")
    seq_place = lax.axis_index("seq")

    def micro_step(grad_sums, inputs):
        tokens_in, encoded, cotangent, blocks, branch_forks = inputs
        slot_count = blocks.shape[0] // seq_count
        own_blocks = lax.dynamic_slice_in_dim(blocks, seq_place * slot_count, slot_count)
        query_info = token_info(own_blocks, branch_forks)
        full_info = token_info(blocks, branch_forks)
        key_mask = allowed(query_info, full_info)
        gain_first, shift_first, attend_in, attend_out, attend_bias = fetch_self(shards)
        stream = tokens_in.astype(jnp.float32)
        norm_full, pull_first = jax.vjp(
            norm_layer, stream, gain_first.astype(jnp.float32), shift_first.astype(jnp.float32)
        )
        norm_first = norm_full.astype(jnp.bfloat16)
        queries = (product(norm_first, attend_in[0]) + attend_bias[0].astype(jnp.float32)).astype(
            jnp.bfloat16
        )
        key_local = product(norm_first, attend_in[1]).astype(jnp.bfloat16)
        value_local = (
            product(norm_first, attend_in[2]) + attend_bias[1].astype(jnp.float32)
        ).astype(jnp.bfloat16)
        key_rows, value_rows = (
            lax.all_gather(key_local, "seq", axis=0, tiled=True),
            lax.all_gather(value_local, "seq", axis=0, tiled=True),
        )
        attended, self_max, self_total = attend_forward(queries, key_rows, value_rows, key_mask)
        middle = stream + product(attended, attend_out) + attend_bias[2].astype(jnp.float32)
        gain_second, shift_second, cross_proj, cross_back, cross_shift = fetch_cross(shards)
        cross_key_local = product(encoded, cross_proj[1]).astype(jnp.bfloat16)
        cross_value_local = (
            product(encoded, cross_proj[2]) + cross_shift[1].astype(jnp.float32)
        ).astype(jnp.bfloat16)
        cross_keys, cross_values = (
            lax.all_gather(cross_key_local, "seq", axis=0, tiled=True),
            lax.all_gather(cross_value_local, "seq", axis=0, tiled=True),
        )
        norm_full_second, pull_second = jax.vjp(
            norm_layer, middle, gain_second.astype(jnp.float32), shift_second.astype(jnp.float32)
        )
        norm_second = norm_full_second.astype(jnp.bfloat16)
        cross_queries = (
            product(norm_second, cross_proj[0]) + cross_shift[0].astype(jnp.float32)
        ).astype(jnp.bfloat16)
        cross_attended, cross_max, cross_total = attend_forward(
            cross_queries, cross_keys, cross_values, None
        )
        after_cross = (
            middle + product(cross_attended, cross_back) + cross_shift[2].astype(jnp.float32)
        )
        gain_third, shift_third, feed_up, feed_up_bias, feed_down, feed_down_bias = fetch_feed(
            shards
        )
        norm_full_third, pull_third = jax.vjp(
            norm_layer, after_cross, gain_third.astype(jnp.float32), shift_third.astype(jnp.float32)
        )
        norm_third = norm_full_third.astype(jnp.bfloat16)
        before = product(norm_third, feed_up) + feed_up_bias.astype(jnp.float32)
        activated_full, gelu_pull = jax.vjp(gelu_exact, before)
        activated = activated_full.astype(jnp.bfloat16)
        result = after_cross + product(activated, feed_down) + feed_down_bias.astype(jnp.float32)
        gain_third, shift_third, feed_up, feed_up_bias, feed_down, feed_down_bias = fetch_feed(
            shards
        )
        cot_float = cotangent.astype(jnp.float32)
        grad_act = product_right(cotangent, feed_down)
        grad_down = product_left(activated, cotangent)
        grad_down_bias = jnp.sum(cot_float, axis=0)
        grad_before = gelu_pull(grad_act)[0].astype(jnp.bfloat16)
        grad_up = product_left(norm_third, grad_before)
        grad_up_bias = column_sum(grad_before)
        grad_third = product_right(grad_before, feed_up)
        grad_after_norm, grad_gain_third, grad_shift_third = pull_third(grad_third)
        grad_after = cot_float + grad_after_norm
        gain_second, shift_second, cross_proj, cross_back, cross_shift = fetch_cross(shards)
        grad_after_low = grad_after.astype(jnp.bfloat16)
        grad_cross_back = product_left(cross_attended, grad_after_low)
        grad_cross_out_bias = column_sum(grad_after_low)
        grad_cross_attended = product_right(grad_after_low, cross_back).astype(jnp.bfloat16)
        grad_cross_queries, grad_cross_keys, grad_cross_values = attend_backward(
            cross_queries,
            cross_keys,
            cross_values,
            None,
            cross_max,
            cross_total,
            grad_cross_attended,
        )
        cross_key_part, cross_value_part = (
            lax.psum_scatter(
                grad_cross_keys.astype(jnp.bfloat16), "seq", scatter_dimension=0, tiled=True
            ).astype(jnp.float32),
            lax.psum_scatter(
                grad_cross_values.astype(jnp.bfloat16), "seq", scatter_dimension=0, tiled=True
            ).astype(jnp.float32),
        )
        cross_key_low = cross_key_part.astype(jnp.bfloat16)
        cross_value_low = cross_value_part.astype(jnp.bfloat16)
        cross_query_low = grad_cross_queries.astype(jnp.bfloat16)
        grad_cross_proj = jnp.stack(
            [
                product_left(norm_second, cross_query_low),
                product_left(encoded, cross_key_low),
                product_left(encoded, cross_value_low),
            ]
        )
        grad_cross_shift = jnp.stack(
            [column_sum(cross_query_low), column_sum(cross_value_low), grad_cross_out_bias]
        )
        encoder_grad = product_right(cross_key_low, cross_proj[1]) + product_right(
            cross_value_low, cross_proj[2]
        )
        grad_second = product_right(cross_query_low, cross_proj[0])
        grad_middle_norm, grad_gain_second, grad_shift_second = pull_second(grad_second)
        grad_middle = grad_after + grad_middle_norm
        gain_first, shift_first, attend_in, attend_out, attend_bias = fetch_self(shards)
        grad_middle_low = grad_middle.astype(jnp.bfloat16)
        grad_attend_out = product_left(attended, grad_middle_low)
        grad_out_bias = column_sum(grad_middle_low)
        grad_attended = product_right(grad_middle_low, attend_out).astype(jnp.bfloat16)
        grad_queries, grad_keys, grad_values = attend_backward(
            queries, key_rows, value_rows, key_mask, self_max, self_total, grad_attended
        )
        key_part, value_part = (
            lax.psum_scatter(
                grad_keys.astype(jnp.bfloat16), "seq", scatter_dimension=0, tiled=True
            ).astype(jnp.float32),
            lax.psum_scatter(
                grad_values.astype(jnp.bfloat16), "seq", scatter_dimension=0, tiled=True
            ).astype(jnp.float32),
        )
        key_low = key_part.astype(jnp.bfloat16)
        value_low = value_part.astype(jnp.bfloat16)
        query_low = grad_queries.astype(jnp.bfloat16)
        grad_attend_in = jnp.stack(
            [
                product_left(norm_first, query_low),
                product_left(norm_first, key_low),
                product_left(norm_first, value_low),
            ]
        )
        grad_attend_bias = jnp.stack([column_sum(query_low), column_sum(value_low), grad_out_bias])
        grad_first = (
            product_right(query_low, attend_in[0])
            + product_right(key_low, attend_in[1])
            + product_right(value_low, attend_in[2])
        )
        grad_stream_norm, grad_gain_first, grad_shift_first = pull_first(grad_first)
        tokens_grad = grad_middle + grad_stream_norm
        updates = (
            jnp.stack([grad_gain_first, grad_gain_second, grad_gain_third]),
            jnp.stack([grad_shift_first, grad_shift_second, grad_shift_third]),
            grad_attend_in,
            grad_attend_out,
            grad_attend_bias,
            grad_cross_proj,
            grad_cross_back,
            grad_cross_shift,
            grad_up,
            grad_up_bias,
            grad_down,
            grad_down_bias,
        )
        grad_sums = tuple((former + latter for former, latter in zip(grad_sums, updates)))
        return (grad_sums, (result.astype(jnp.bfloat16), tokens_grad, encoder_grad))

    starting = (
        jnp.zeros((3, model_width), jnp.float32),
        jnp.zeros((3, model_width), jnp.float32),
        jnp.zeros((3, model_width, model_width), jnp.float32),
        jnp.zeros((model_width, model_width), jnp.float32),
        jnp.zeros((3, model_width), jnp.float32),
        jnp.zeros((3, model_width, model_width), jnp.float32),
        jnp.zeros((model_width, model_width), jnp.float32),
        jnp.zeros((3, model_width), jnp.float32),
        jnp.zeros((model_width, hidden_width), jnp.float32),
        jnp.zeros((hidden_width,), jnp.float32),
        jnp.zeros((hidden_width, model_width), jnp.float32),
        jnp.zeros((model_width,), jnp.float32),
    )
    grad_sums, outputs = lax.scan(
        micro_step, starting, (tokens, encoder_states, out_grad, block_map, branch_fork)
    )
    feed_part = (
        lax.psum_scatter(grad_sums[8], ("dp", "seq"), scatter_dimension=0, tiled=True),
        lax.psum_scatter(grad_sums[9], ("dp", "seq"), scatter_dimension=0, tiled=True),
        lax.psum_scatter(grad_sums[10], ("dp", "seq"), scatter_dimension=0, tiled=True),
        lax.psum_scatter(grad_sums[11], ("dp", "seq"), scatter_dimension=0, tiled=True),
    )
    cross_part = (
        lax.psum_scatter(grad_sums[5], ("dp", "seq"), scatter_dimension=1, tiled=True),
        lax.psum_scatter(grad_sums[6], ("dp", "seq"), scatter_dimension=0, tiled=True),
        lax.psum_scatter(grad_sums[7], ("dp", "seq"), scatter_dimension=1, tiled=True),
    )
    self_part = (
        lax.psum_scatter(grad_sums[0], ("dp", "seq"), scatter_dimension=1, tiled=True),
        lax.psum_scatter(grad_sums[1], ("dp", "seq"), scatter_dimension=1, tiled=True),
        lax.psum_scatter(grad_sums[2], ("dp", "seq"), scatter_dimension=1, tiled=True),
        lax.psum_scatter(grad_sums[3], ("dp", "seq"), scatter_dimension=0, tiled=True),
        lax.psum_scatter(grad_sums[4], ("dp", "seq"), scatter_dimension=1, tiled=True),
    )
    return (
        outputs[0],
        outputs[1],
        outputs[2],
        self_part[0],
        self_part[1],
        self_part[2],
        self_part[3],
        self_part[4],
        cross_part[0],
        cross_part[1],
        cross_part[2],
        feed_part[0],
        feed_part[1],
        feed_part[2],
        feed_part[3],
    )


LOG2E = 1.4426950408889634
LN2 = 0.6931471805599453
QSCALE = HEAD ** (-0.5) * LOG2E
AXES = ("dp", "seq")
F32 = jnp.float32
BF16 = jnp.bfloat16
ANY = pl.BlockSpec(memory_space=pl.ANY)
SMEM = pl.BlockSpec(memory_space=pltpu.SMEM)


def nn(a, b):
    return lax.dot_general(a, b, (((1,), (0,)), ((), ())), preferred_element_type=F32)


def nt(a, b):
    return lax.dot_general(a, b, (((1,), (1,)), ((), ())), preferred_element_type=F32)


def tn(a, b):
    return lax.dot_general(a, b, (((0,), (0,)), ((), ())), preferred_element_type=F32)


def whole(shape):
    zeros = (0,) * len(shape)
    return pl.BlockSpec(shape, lambda *_: zeros)


def params(**kw):
    return pltpu.CompilerParams(vmem_limit_bytes=60 * 1024 * 1024, **kw)


def cost(flops, nbytes, trans=0):
    return pl.CostEstimate(flops=int(flops), bytes_accessed=int(nbytes), transcendentals=int(trans))


def stats(v):
    mean = jnp.mean(v, axis=-1, keepdims=True)
    centered = v - mean
    var = jnp.mean(centered * centered, axis=-1, keepdims=True)
    rstd = lax.rsqrt(var + 1e-05)
    return centered * rstd, rstd


def norm_back(v, e, gain):
    z, rstd = stats(v)
    f = e * gain
    grad = rstd * (
        f - jnp.mean(f, axis=-1, keepdims=True) - z * jnp.mean(f * z, axis=-1, keepdims=True)
    )
    return grad, jnp.sum(e * z, axis=0, keepdims=True), jnp.sum(e, axis=0, keepdims=True)


def qkv_kernel(meta, *refs):
    pieces = refs[:8]
    w_ref, vec_ref, bias_ref, q_ref, kv_ref, tr_ref, n1_ref, buf, sem = refs[8:]
    rows = buf.shape[0] // 8
    step = pl.program_id(0)

    @pl.when(step == 0)
    def _():
        copies = [
            pltpu.make_async_copy(pieces[i], buf.at[pl.ds(i * rows, rows), :], sem.at[i])
            for i in range(8)
        ]
        for c in copies:
            c.start()
        for c in copies:
            c.wait()

    gain, shift = vec_ref[0:1, :], vec_ref[3:4, :]
    w = w_ref[...]
    bias = bias_ref[0:1, :]
    for u in range(4):
        b = meta[32 + step * 4 + u]
        off = pl.multiple_of((b // 4) * rows + (b % 4) * 128, 32)
        x = buf[pl.ds(off, 128), :].astype(F32)
        z, _ = stats(x)
        n1 = (z * gain + shift).astype(BF16)
        r = slice(u * 128, (u + 1) * 128)
        n1_ref[r, :] = n1
        y = nn(n1, w) + bias
        kvt = jnp.transpose(y[:, 192:576]).astype(BF16)
        for t in range(2):
            for h in range(3):
                o = (t * 3 + h) * 64
                tr_ref[t * 3 + h, :, r] = kvt[o : o + 64, :]
        yq = (y[:, 0:192] * QSCALE).astype(BF16)
        yk = y[:, 192:576].astype(BF16)
        zero = jnp.zeros((128, 64), BF16)
        for h in range(3):
            q_ref[h, r, :] = jnp.concatenate([yq[:, h * 64 : h * 64 + 64], zero], axis=1)
            kv_ref[h, r, :] = jnp.concatenate(
                [yk[:, h * 64 : h * 64 + 64], yk[:, 192 + h * 64 : 256 + h * 64]], axis=1
            )


def qkv_call(meta, pieces, w2, vecs, bias):
    rows = pieces[0].shape[0]
    grid = (8,)
    return pl.pallas_call(
        qkv_kernel,
        grid_spec=pltpu.PrefetchScalarGridSpec(
            num_scalar_prefetch=1,
            grid=grid,
            in_specs=[ANY] * 8 + [whole(w2.shape), whole(vecs.shape), whole(bias.shape)],
            out_specs=[
                pl.BlockSpec((3, 512, 128), lambda i, m: (0, i, 0)),
                pl.BlockSpec((3, 512, 128), lambda i, m: (0, i, 0)),
                pl.BlockSpec((6, 64, 512), lambda i, m: (0, 0, i)),
                pl.BlockSpec((512, 768), lambda i, m: (i, 0)),
            ],
            scratch_shapes=[pltpu.VMEM((8 * rows, 768), BF16), pltpu.SemaphoreType.DMA((8,))],
        ),
        out_shape=[
            jax.ShapeDtypeStruct((3, 4096, 128), BF16),
            jax.ShapeDtypeStruct((3, 4096, 128), BF16),
            jax.ShapeDtypeStruct((6, 64, 4096), BF16),
            jax.ShapeDtypeStruct((4096, 768), BF16),
        ],
        compiler_params=params(dimension_semantics=("arbitrary",)),
        cost_estimate=cost(2 * 4096 * 768 * 576, 20e6),
        name="qkv",
    )(meta, *pieces, w2, vecs, bias)


def tile_mask(diag, kt, limit):
    key = lax.broadcasted_iota(jnp.int32, (256, 256), 0)
    if diag:
        return key <= lax.broadcasted_iota(jnp.int32, (256, 256), 1)
    return key + kt * 256 < limit


def attend_kernel(meta, q_ref, kv_ref, tr_ref, o_ref, lse_ref, m_ref, l_ref, acc_ref):
    def q_tile(qi, carry):
        branch = qi >= 8
        fork = meta[64 + jnp.maximum(qi - 8, 0)]
        full = jnp.where(branch, fork // 256, qi)
        qs = pl.ds(pl.multiple_of(qi * 256, 256), 256)
        m_ref[...] = jnp.full_like(m_ref, -1e30)
        l_ref[...] = jnp.zeros_like(l_ref)
        acc_ref[...] = jnp.zeros_like(acc_ref)

        def k_tile(kt, mask):
            ks = pl.ds(pl.multiple_of(kt * 256, 256), 256)
            for h in range(3):
                s = nt(kv_ref[h, ks, :], q_ref[h, qs, :])
                if mask is not None:
                    s = jnp.where(mask, s, -1e30)
                old = m_ref[h : h + 1, :]
                new = jnp.maximum(old, jnp.max(s, axis=0, keepdims=True))
                p = jnp.exp2(s - new)
                alpha = jnp.exp2(old - new)
                m_ref[h : h + 1, :] = new
                l_ref[h : h + 1, :] = l_ref[h : h + 1, :] * alpha + jnp.sum(p, axis=0, keepdims=True)
                hs = slice(h * 64, h * 64 + 64)
                acc_ref[hs, :] = acc_ref[hs, :] * alpha + nn(tr_ref[3 + h, :, ks], p.astype(BF16))

        def full_tile(kt, c):
            k_tile(kt, None)
            return c

        lax.fori_loop(0, full, full_tile, 0)

        @pl.when(branch & (fork % 256 != 0))
        def _():
            k_tile(full, tile_mask(False, full, fork))

        k_tile(qi, tile_mask(True, 0, 0))
        for h in range(3):
            hs = slice(h * 64, h * 64 + 64)
            l = l_ref[h : h + 1, :]
            acc_ref[hs, :] = acc_ref[hs, :] * (1.0 / l)
            lse_ref[h : h + 1, qs] = m_ref[h : h + 1, :] + jnp.log2(l)
        out = jnp.transpose(acc_ref[...]).astype(BF16)
        for u in range(2):
            o_ref[meta[32 + qi * 2 + u]] = out[u * 128 : (u + 1) * 128, :]
        return carry

    lax.fori_loop(0, 16, q_tile, 0)


def attend_call(meta, q, kv, tr):
    return pl.pallas_call(
        attend_kernel,
        grid_spec=pltpu.PrefetchScalarGridSpec(
            num_scalar_prefetch=1,
            grid=(1,),
            in_specs=[whole(q.shape), whole(kv.shape), whole(tr.shape)],
            out_specs=[whole((32, 128, 192)), whole((8, 4096))],
            scratch_shapes=[
                pltpu.VMEM((8, 256), F32),
                pltpu.VMEM((8, 256), F32),
                pltpu.VMEM((192, 256), F32),
            ],
        ),
        out_shape=[
            jax.ShapeDtypeStruct((32, 128, 192), BF16),
            jax.ShapeDtypeStruct((8, 4096), F32),
        ],
        compiler_params=params(dimension_semantics=("arbitrary",)),
        cost_estimate=cost(20e9, 10e6, 20e6),
        name="attend",
    )(meta, q, kv, tr)


def attend_back_kernel(
    meta, q_ref, kv_ref, tr_ref, o_ref, lse_ref, d0, d1, d2, d3, w_ref,
    out_ref, x0, x1, x2, x3, do_ref, di_ref, dq_ref, acc_ref,
):
    pieces = (d0, d1, d2, d3)
    zero = jnp.zeros((128, 64), BF16)
    for k in range(4):
        for kk in range(8):
            b = k * 8 + kk
            at = pl.ds(pl.multiple_of(meta[b] * 128, 128), 128)
            do = pieces[k][kk * 128 : (kk + 1) * 128, :]
            prod = jnp.transpose(do.astype(F32) * o_ref[b].astype(F32))
            for h in range(3):
                di_ref[h : h + 1, at] = jnp.sum(prod[h * 64 : h * 64 + 64, :], axis=0, keepdims=True)
                do_ref[h, at, :] = jnp.concatenate([zero, do[:, h * 64 : h * 64 + 64]], axis=1)
    acc_ref[...] = jnp.zeros_like(acc_ref)

    def q_tile(qi, carry):
        branch = qi >= 8
        fork = meta[64 + jnp.maximum(qi - 8, 0)]
        full = jnp.where(branch, fork // 256, qi)
        qs = pl.ds(pl.multiple_of(qi * 256, 256), 256)
        dq_ref[...] = jnp.zeros_like(dq_ref)

        def k_tile(kt, mask):
            ks = pl.ds(pl.multiple_of(kt * 256, 256), 256)
            for h in range(3):
                kv = kv_ref[h, ks, :]
                q, do = q_ref[h, qs, :], do_ref[h, qs, :]
                p = jnp.exp2(nt(kv, q) - lse_ref[h : h + 1, qs])
                if mask is not None:
                    p = jnp.where(mask, p, 0.0)
                ds = (p * (nt(kv, do) - di_ref[h : h + 1, qs])).astype(BF16)
                acc_ref[h, ks, :] += nn(ds, q) + nn(p.astype(BF16), do)
                hs = slice(h * 64, h * 64 + 64)
                dq_ref[hs, :] += nn(tr_ref[h, :, ks], ds)

        def full_tile(kt, c):
            k_tile(kt, None)
            return c

        lax.fori_loop(0, full, full_tile, 0)

        @pl.when(branch & (fork % 256 != 0))
        def _():
            k_tile(full, tile_mask(False, full, fork))

        k_tile(qi, tile_mask(True, 0, 0))
        out_ref[qs, 0:192] = (jnp.transpose(dq_ref[...]) * HEAD ** (-0.5)).astype(BF16)
        return carry

    lax.fori_loop(0, 16, q_tile, 0)

    def finish(t, carry):
        rs = pl.ds(pl.multiple_of(t * 256, 256), 256)
        a = [acc_ref[h, rs, :] for h in range(3)]
        dk = jnp.concatenate([v[:, 0:64] for v in a], axis=1) * LN2
        dv = jnp.concatenate([v[:, 64:128] for v in a], axis=1)
        out_ref[rs, 192:576] = jnp.concatenate([dk, dv], axis=1).astype(BF16)
        return carry

    lax.fori_loop(0, 16, finish, 0)
    for k, x_ref in enumerate((x0, x1, x2, x3)):
        for kk in range(8):
            at = pl.ds(pl.multiple_of(meta[k * 8 + kk] * 128, 128), 128)
            x_ref[kk * 128 : (kk + 1) * 128, :] = nt(out_ref[at, :], w_ref[...]).astype(BF16)


def attend_back_call(meta, q, kv, tr, o, lse, pieces, w2):
    ins = [q, kv, tr, o, lse, *pieces, w2]
    return pl.pallas_call(
        attend_back_kernel,
        grid_spec=pltpu.PrefetchScalarGridSpec(
            num_scalar_prefetch=1,
            grid=(1,),
            in_specs=[whole(v.shape) for v in ins],
            out_specs=[whole((4096, 576))] + [whole((1024, 768))] * 4,
            scratch_shapes=[
                pltpu.VMEM((3, 4096, 128), BF16),
                pltpu.VMEM((8, 4096), F32),
                pltpu.VMEM((192, 256), F32),
                pltpu.VMEM((3, 4096, 128), F32),
            ],
        ),
        out_shape=[jax.ShapeDtypeStruct((4096, 576), BF16)]
        + [jax.ShapeDtypeStruct((1024, 768), BF16)] * 4,
        compiler_params=params(dimension_semantics=("arbitrary",)),
        cost_estimate=cost(50e9, 15e6, 20e6),
        name="attend_back",
    )(meta, *ins)


def win_kernel(n_ref, d_ref, g_ref, s_ref, acc_ref):
    step = pl.program_id(0)

    @pl.when(step == 0)
    def _():
        acc_ref[...] = jnp.zeros_like(acc_ref)
        s_ref[...] = jnp.zeros_like(s_ref)

    d = d_ref[...]
    acc_ref[...] += tn(n_ref[...], d)
    s_ref[0:1, :] += jnp.sum(d.astype(F32), axis=0, keepdims=True)

    @pl.when(step == pl.num_programs(0) - 1)
    def _():
        g_ref[...] = acc_ref[...].astype(BF16)


def win_call(n1, dqkv):
    return pl.pallas_call(
        win_kernel,
        grid=(4,),
        in_specs=[
            pl.BlockSpec((1024, 768), lambda i: (i, 0)),
            pl.BlockSpec((1024, 576), lambda i: (i, 0)),
        ],
        out_specs=[whole((768, 576)), whole((8, 576))],
        out_shape=[
            jax.ShapeDtypeStruct((768, 576), BF16),
            jax.ShapeDtypeStruct((8, 576), F32),
        ],
        scratch_shapes=[pltpu.VMEM((768, 576), F32)],
        compiler_params=params(dimension_semantics=("arbitrary",)),
        cost_estimate=cost(2 * 4096 * 768 * 576, 12e6),
        name="win",
    )(n1, dqkv)


def head_masks(frames):
    lane = lax.broadcasted_iota(jnp.int32, (frames, 128), 1) < 64
    return lane, jnp.logical_not(lane)


def mid_kernel(
    meta, tok_ref, o0, o1, o2, o3, so_ref, ci_ref, co_ref, fr_ref, vec_ref,
    mid_ref, ac_ref, n2_ref, n3_ref, cq_ref, ca_ref, lse_ref, kc_ref, vc_ref,
    km_ref, vmt_ref,
):
    frames = fr_ref.shape[0]
    hset = meta[72]

    @pl.when(pl.program_id(0) == 0)
    def _():
        fr = fr_ref[...]
        kc = nn(fr, ci_ref[1]).astype(BF16)
        vc = (nn(fr, ci_ref[2]) + vec_ref[10:11, :]).astype(BF16)
        kc_ref[...] = kc
        vc_ref[...] = vc
        zero = jnp.zeros((frames, 128), BF16)
        masks = head_masks(frames)
        for hp in range(6):
            ls = slice(hp * 128, hp * 128 + 128)
            for e in range(2):
                km_ref[hp * 2 + e] = jnp.where(masks[e], kc[:, ls], zero)
                vmt_ref[hp * 2 + e] = jnp.transpose(
                    jnp.where(masks[e], vc[:, ls].astype(F32), 0.0)
                ).astype(BF16)

    acc = tok_ref[...].astype(F32) + vec_ref[8:9, :]
    for k, o in enumerate((o0, o1, o2, o3)):
        at = pl.ds(pl.multiple_of((hset ^ k) * 192, 64), 192)
        acc = acc + nn(o[...], so_ref[at, :])
    mid_ref[...] = acc
    z, _ = stats(acc)
    n2 = (z * vec_ref[1:2, :] + vec_ref[4:5, :]).astype(BF16)
    n2_ref[...] = n2
    cq = ((nn(n2, ci_ref[0]) + vec_ref[9:10, :]) * QSCALE).astype(BF16)
    cq_ref[...] = cq
    ca = []
    for hp in range(6):
        qp = cq[:, hp * 128 : hp * 128 + 128]
        out = None
        for e in range(2):
            h = hp * 2 + e
            s = nt(km_ref[h], qp)
            m = jnp.max(s, axis=0, keepdims=True)
            p = jnp.exp2(s - m)
            l = jnp.sum(p, axis=0, keepdims=True)
            lse_ref[h : h + 1, :] = m + jnp.log2(l)
            part = nn(vmt_ref[h], p.astype(BF16)) * (1.0 / l)
            out = part if out is None else out + part
        ca.append(jnp.transpose(out).astype(BF16))
    ca = jnp.concatenate(ca, axis=1)
    ca_ref[...] = ca
    ac = acc + nn(ca, co_ref[...]) + vec_ref[11:12, :]
    ac_ref[...] = ac
    z, _ = stats(ac)
    n3_ref[...] = (z * vec_ref[2:3, :] + vec_ref[5:6, :]).astype(BF16)


def mid_call(meta, tok, pieces, so, ci, co, frames, vecs):
    rows, width = tok.shape
    tile = 256
    nf = frames.shape[0]
    row = pl.BlockSpec((tile, width), lambda i, m: (i, 0))
    row4 = pl.BlockSpec((tile, 192), lambda i, m: (i, 0))
    sds = jax.ShapeDtypeStruct
    return pl.pallas_call(
        mid_kernel,
        grid_spec=pltpu.PrefetchScalarGridSpec(
            num_scalar_prefetch=1,
            grid=(rows // tile,),
            in_specs=[row] + [row4] * 4
            + [whole(so.shape), whole(ci.shape), whole(co.shape), whole(frames.shape), whole(vecs.shape)],
            out_specs=[row] * 6
            + [pl.BlockSpec((16, tile), lambda i, m: (0, i)), whole((nf, width)), whole((nf, width))],
            scratch_shapes=[pltpu.VMEM((12, nf, 128), BF16), pltpu.VMEM((12, 128, nf), BF16)],
        ),
        out_shape=[
            sds((rows, width), F32), sds((rows, width), F32), sds((rows, width), BF16),
            sds((rows, width), BF16), sds((rows, width), BF16), sds((rows, width), BF16),
            sds((16, rows), F32), sds((nf, width), BF16), sds((nf, width), BF16),
        ],
        compiler_params=params(dimension_semantics=("arbitrary",)),
        cost_estimate=cost(8e9, 25e6, 3e6),
        name="middle",
    )(meta, tok, *pieces, so, ci, co, frames, vecs)


def normal_parts(b):
    e = jnp.exp2(b * b * (-0.5 * LOG2E))
    a = jnp.abs(b) * 0.7071067811865476
    t = 1.0 / (1.0 + 0.3275911 * a)
    poly = t * (
        0.254829592 + t * (-0.284496736 + t * (1.421413741 + t * (-1.453152027 + t * 1.061405429)))
    )
    tail = 0.5 * poly * e
    return jnp.where(b < 0.0, tail, 1.0 - tail), e * 0.3989422804014327


def feed_kernel(
    n3_ref, og_ref, ac_ref, up_ref, dn_ref, ub_ref, vec_ref,
    res_ref, gt_ref, ug_ref, dg_ref, ubg_ref, dbg_ref,
    acc_ref, n3t_ref, act_ref, gb_ref,
):
    step = pl.program_id(0)
    rows, width = n3_ref.shape

    @pl.when(step == 0)
    def _():
        acc_ref[...] = ac_ref[...] + vec_ref[12:13, :]
        gt_ref[...] = jnp.zeros_like(gt_ref)
        dbg_ref[...] = jnp.zeros_like(dbg_ref)
        dbg_ref[0:1, :] = jnp.sum(og_ref[...].astype(F32), axis=0, keepdims=True)
        n3t_ref[...] = jnp.transpose(n3_ref[...])

    up = up_ref[...].reshape(width, width)
    dn = dn_ref[...].reshape(width, width)
    ub = ub_ref[pl.ds(step, 1), :]
    total = jnp.zeros((1, width), F32)
    for r in range(rows // 256):
        rs = slice(r * 256, (r + 1) * 256)
        n3 = n3_ref[rs, :]
        og = og_ref[rs, :]
        b = nn(n3, up) + ub
        cdf, pdf = normal_parts(b)
        act = (b * cdf).astype(BF16)
        gb = (nt(og, dn) * (cdf + b * pdf)).astype(BF16)
        act_ref[rs, :] = act
        gb_ref[rs, :] = gb
        total = total + jnp.sum(gb.astype(F32), axis=0, keepdims=True)
        acc_ref[rs, :] += nn(act, dn)
        gt_ref[rs, :] += nt(gb, up)
    ubg_ref[...] = jnp.broadcast_to(total, (8, width))
    ug_ref[...] = nn(n3t_ref[...], gb_ref[...]).astype(BF16).reshape(ug_ref.shape)
    dg_ref[...] = tn(act_ref[...], og_ref[...]).astype(BF16).reshape(dg_ref.shape)

    @pl.when(step == pl.num_programs(0) - 1)
    def _():
        res_ref[...] = acc_ref[...].astype(BF16)


def feed_call(n3, og, ac, up4, dn4, ub4, vecs):
    rows, width = n3.shape
    sds = jax.ShapeDtypeStruct
    tiles = up4.shape[0]
    tile = pl.BlockSpec((1, width, width), lambda i: (i, 0, 0))
    return pl.pallas_call(
        feed_kernel,
        grid=(tiles,),
        in_specs=[whole(n3.shape), whole(og.shape), whole(ac.shape), tile, tile, whole(ub4.shape), whole(vecs.shape)],
        out_specs=[
            whole((rows, width)), whole((rows, width)), tile, tile,
            pl.BlockSpec((8, width), lambda i: (i, 0)), whole((8, width)),
        ],
        out_shape=[
            sds((rows, width), BF16), sds((rows, width), F32),
            sds((tiles, width, width), BF16), sds((tiles, width, width), BF16),
            sds((tiles * 8, width), F32), sds((8, width), F32),
        ],
        scratch_shapes=[
            pltpu.VMEM((rows, width), F32), pltpu.VMEM((width, rows), BF16),
            pltpu.VMEM((rows, width), BF16), pltpu.VMEM((rows, width), BF16),
        ],
        compiler_params=params(dimension_semantics=("arbitrary",)),
        cost_estimate=cost(2 * 6 * rows * width * width * tiles, 35e6, 6e6),
        name="feed",
    )(n3, og, ac, up4, dn4, ub4, vecs)


def mid_back_kernel(
    meta, gt_ref, og_ref, ac_ref, mid_ref, n2_ref, cq_ref, ca_ref, lse_ref, kc_ref, vc_ref,
    fr_ref, so_ref, ci_ref, co_ref, vec_ref, o0, o1, o2, o3,
    gm_ref, do0, do1, do2, do3, sog_ref, cig_ref, cog_ref, eg_ref, sums_ref,
    km_ref, kmt_ref, vm_ref, dk_ref, dv_ref, so_acc, cq_acc, co_acc,
):
    frames = fr_ref.shape[0]
    hset = meta[72]
    step = pl.program_id(0)
    last = pl.num_programs(0) - 1
    masks = head_masks(frames)

    @pl.when(step == 0)
    def _():
        zero = jnp.zeros((frames, 128), BF16)
        for hp in range(6):
            ls = slice(hp * 128, hp * 128 + 128)
            k, v = kc_ref[:, ls], vc_ref[:, ls]
            for e in range(2):
                km_ref[hp * 2 + e] = jnp.where(masks[e], k, zero)
                vm_ref[hp * 2 + e] = jnp.where(masks[e], v, zero)
                kmt_ref[hp * 2 + e] = jnp.transpose(
                    jnp.where(masks[e], k.astype(F32), 0.0)
                ).astype(BF16)
        for ref in (dk_ref, dv_ref, so_acc, cq_acc, co_acc, sums_ref):
            ref[...] = jnp.zeros_like(ref)

    def count(row, value):
        sums_ref[row : row + 1, :] += value

    gt = gt_ref[...]
    back, gain, shift = norm_back(ac_ref[...], gt, vec_ref[2:3, :])
    count(2, gain)
    count(5, shift)
    ga = og_ref[...].astype(F32) + back
    gal = ga.astype(BF16)
    count(11, jnp.sum(gal.astype(F32), axis=0, keepdims=True))
    ca = ca_ref[...]
    co_acc[...] += tn(ca, gal)
    dca = nt(gal, co_ref[...]).astype(BF16)
    cq = cq_ref[...]
    dq = []
    for hp in range(6):
        ls = slice(hp * 128, hp * 128 + 128)
        qp, dp_ = cq[:, ls], dca[:, ls]
        dqt = None
        parts = []
        for e in range(2):
            h = hp * 2 + e
            p = jnp.exp2(nt(km_ref[h], qp) - lse_ref[h : h + 1, :])
            dp = nt(vm_ref[h], dp_)
            inner = jnp.sum(dp * p, axis=0, keepdims=True)
            ds = (p * (dp - inner)).astype(BF16)
            part = nn(kmt_ref[h], ds)
            dqt = part if dqt is None else dqt + part
            parts.append((nn(ds, qp), nn(p.astype(BF16), dp_)))
        dq.append(jnp.transpose(dqt))
        dk_ref[:, ls] += jnp.where(masks[0], parts[0][0], parts[1][0])
        dv_ref[:, ls] += jnp.where(masks[0], parts[0][1], parts[1][1])
    dcq = (jnp.concatenate(dq, axis=1) * HEAD ** (-0.5)).astype(BF16)
    count(9, jnp.sum(dcq.astype(F32), axis=0, keepdims=True))
    cq_acc[...] += tn(n2_ref[...], dcq)
    gs = nt(dcq, ci_ref[0])
    back, gain, shift = norm_back(mid_ref[...], gs, vec_ref[1:2, :])
    count(1, gain)
    count(4, shift)
    gm = ga + back
    gm_ref[...] = gm
    gml = gm.astype(BF16)
    count(8, jnp.sum(gml.astype(F32), axis=0, keepdims=True))
    for k, (o, do) in enumerate(zip((o0, o1, o2, o3), (do0, do1, do2, do3))):
        at = pl.ds(pl.multiple_of((hset ^ k) * 192, 64), 192)
        do[...] = nt(gml, so_ref[at, :]).astype(BF16)
        so_acc[at, :] += tn(o[...], gml)

    @pl.when(step == last)
    def _():
        dk = (dk_ref[...] * LN2).astype(BF16)
        dv = dv_ref[...].astype(BF16)
        count(10, jnp.sum(dv.astype(F32), axis=0, keepdims=True))
        fr = fr_ref[...]
        sog_ref[...] = so_acc[...].astype(BF16)
        cog_ref[...] = co_acc[...].astype(BF16)
        cig_ref[0] = cq_acc[...].astype(BF16)
        cig_ref[1] = tn(fr, dk).astype(BF16)
        cig_ref[2] = tn(fr, dv).astype(BF16)
        eg_ref[...] = (nt(dk, ci_ref[1]) + nt(dv, ci_ref[2])).astype(BF16)


def mid_back_call(meta, gt, og, ac, mid, n2, cq, ca, lse, kc, vc, frames, so, ci, co, vecs, pieces):
    rows, width = gt.shape
    tile = 256
    nf = frames.shape[0]
    row = pl.BlockSpec((tile, width), lambda i, m: (i, 0))
    row4 = pl.BlockSpec((tile, 192), lambda i, m: (i, 0))
    sds = jax.ShapeDtypeStruct
    acc = pltpu.VMEM((width, width), F32)
    return pl.pallas_call(
        mid_back_kernel,
        grid_spec=pltpu.PrefetchScalarGridSpec(
            num_scalar_prefetch=1,
            grid=(rows // tile,),
            in_specs=[row] * 7
            + [pl.BlockSpec((16, tile), lambda i, m: (0, i))]
            + [whole(v.shape) for v in (kc, vc, frames, so, ci, co, vecs)]
            + [row4] * 4,
            out_specs=[row] + [row4] * 4
            + [whole((width, width)), whole((3, width, width)), whole((width, width)), whole((nf, width)), whole((24, width))],
            scratch_shapes=[
                pltpu.VMEM((12, nf, 128), BF16), pltpu.VMEM((12, 128, nf), BF16), pltpu.VMEM((12, nf, 128), BF16),
                pltpu.VMEM((nf, width), F32), pltpu.VMEM((nf, width), F32), acc, acc, acc,
            ],
        ),
        out_shape=[sds((rows, width), F32)] + [sds((rows, 192), BF16)] * 4
        + [sds((width, width), BF16), sds((3, width, width), BF16), sds((width, width), BF16), sds((nf, width), BF16), sds((24, width), F32)],
        compiler_params=params(dimension_semantics=("arbitrary",)),
        cost_estimate=cost(22e9, 35e6, 3e6),
        name="middle_back",
    )(meta, gt, og, ac, mid, n2, cq, ca, lse, kc, vc, frames, so, ci, co, vecs, *pieces)


def first_back_kernel(a_ref, b_ref, c_ref, gm_ref, tok_ref, vec_ref, out_ref, sums_ref):
    @pl.when(pl.program_id(0) == 0)
    def _():
        sums_ref[...] = jnp.zeros_like(sums_ref)

    e = a_ref[...].astype(F32) + b_ref[...].astype(F32) + c_ref[...].astype(F32)
    back, gain, shift = norm_back(tok_ref[...].astype(F32), e, vec_ref[0:1, :])
    sums_ref[0:1, :] += gain
    sums_ref[1:2, :] += shift
    out_ref[...] = (gm_ref[...] + back).astype(BF16)


def first_back_call(a, b, c, gm, tok, vecs, part):
    width = a.shape[1]
    base = part * 2
    row = pl.BlockSpec((256, width), lambda i: (i, 0))
    off = pl.BlockSpec((256, width), lambda i: (i + base, 0))
    return pl.pallas_call(
        first_back_kernel,
        grid=(2,),
        in_specs=[off, off, row, off, off, whole(vecs.shape)],
        out_specs=[row, whole((8, width))],
        out_shape=[jax.ShapeDtypeStruct((512, width), BF16), jax.ShapeDtypeStruct((8, width), F32)],
        compiler_params=params(dimension_semantics=("arbitrary",)),
        cost_estimate=cost(1e7, 6e6),
        name="first_back%d" % part,
    )(a, b, c, gm, tok, vecs)


def device_pairs(dp_count, move, back=False):
    pairs = []
    for dp in range(dp_count):
        for seq in range(8):
            y, c, z, x = move(dp // 2, dp % 2, seq // 2, seq % 2)
            pair = (dp * 8 + seq, (y * 2 + c) * 8 + z * 2 + x)
            pairs.append(pair[::-1] if back else pair)
    return pairs


def home_body(
    tokens, encoder_states, out_grad, block_map, branch_fork, norm_gain, norm_bias, self_in,
    self_out, self_bias, cross_in, cross_out, cross_bias, up_weight, up_bias, down_weight, down_bias,
):
    dp_count = lax.axis_size("dp")
    dp, seq = lax.axis_index("dp"), lax.axis_index("seq")
    c, z, x = dp & 1, seq >> 1, seq & 1
    y = dp >> 1
    flat = dp * 8 + seq
    hset = 2 * c + x
    parity = z & 1
    rows, width = tokens.shape[1:]
    frames = encoder_states.shape[1]

    def send(v, move, back=False):
        return lax.ppermute(v, AXES, device_pairs(dp_count, move, back))

    def flip(k):
        return lambda y, c, z, x: (y, c ^ (k >> 1), z, x ^ (k & 1))

    def home(p):
        return lambda y, c, z, x: (y, z >> 1, 2 * c + (p ^ (z & 1)), x)

    def pick(v, p):
        return jnp.where(parity == p, v[0], v[1])

    def piece(v, parts):
        return v.reshape(parts, -1).astype(BF16)

    small = jnp.concatenate(
        [v.reshape(-1) for v in (norm_gain, norm_bias, self_bias, cross_bias, down_bias, up_bias)]
    )
    small = jnp.pad(small, (0, 8 * 192 - small.shape[0])).reshape(8, 192)
    shard = self_in.reshape(-1, width)
    options = jnp.stack(
        [jnp.concatenate([shard[:, 192 * j : 192 * j + 192], small]) for j in range(4)]
    )

    def merge(own, other, bit):
        return jnp.stack([jnp.where(bit == 0, own, other), jnp.where(bit == 0, other, own)])

    def option(k):
        return lax.dynamic_index_in_dim(options, hset ^ k, 0, False)

    got = [option(0)] + [send(option(k), flip(k)) for k in (1, 2, 3)]
    tree = merge(merge(got[0], got[1], x), merge(got[2], got[3], x), c)
    for bit in range((dp_count // 2).bit_length() - 1):
        tree = merge(
            tree, send(tree, lambda y, c, z, x, bit=bit: (y ^ (1 << bit), c, z, x)), (y >> bit) & 1
        )
    both = jnp.concatenate([tokens, encoder_states], axis=1)
    mine = [send(pick(both, p), home(p)) for p in range(2)]
    tree, mine[0] = lax.optimization_barrier((tree, mine[0]))
    across = [send(v, flip(1)) for v in mine]
    near = [send(v, flip(2)) for v in mine]
    tree = merge(tree, send(tree, lambda y, c, z, x: (y, c, z ^ 2, x)), z >> 1)
    tree = merge(tree, send(tree, lambda y, c, z, x: (y, c, z ^ 1, x)), z & 1)
    y_count = dp_count // 2
    nw = shard.shape[0] // 3
    tree = tree.reshape(2, 2, y_count, 2, 2, 3 * nw + 8, 192).transpose(2, 3, 1, 0, 4, 5, 6)
    tree = tree.reshape(dp_count * 8, 3 * nw + 8, 192)
    w2 = jnp.concatenate(
        [tree[:, t * nw : (t + 1) * nw].reshape(width, 192) for t in range(3)], axis=1
    )
    flats = tree[:, 3 * nw :].reshape(dp_count * 8, -1)
    lists = [
        flats[:, i * nw : (i + 1) * nw].reshape(1, width) for i in range(13)
    ]
    tiles = up_weight.shape[1] // width
    ub4 = flats[:, 13 * nw : (13 + tiles) * nw].reshape(tiles, width).astype(F32)
    vecs = jnp.concatenate(lists + [jnp.zeros((3, width), BF16)]).astype(F32)
    own_cols = lambda v: lax.dynamic_slice_in_dim(v, hset * 192, 192, 1)
    zero_row = jnp.zeros((1, 192), F32)
    qkv_bias = jnp.concatenate([own_cols(vecs[6:7]), zero_row, own_cols(vecs[7:8])], axis=1)

    info = jnp.concatenate([block_map, branch_fork], axis=1)
    info = jnp.where((z >> 1) == c, info, send(info, flip(2)))
    info = jnp.where(parity == 0, info[0], info[1])
    place = jnp.arange(32, dtype=jnp.int32)
    k_of, p_of = place >> 3, (place >> 2) & 1
    stored = (2 * (2 * (c ^ (k_of >> 1)) + (p_of ^ parity)) + (x ^ (k_of & 1))) * 4 + (place & 3)
    logical = jnp.sum(jnp.where(stored[:, None] == place[None, :], info[None, :32], 0), axis=1)
    spot = jnp.sum(jnp.where(logical[None, :] == place[:, None], place[None, :], 0), axis=1)
    meta = jnp.concatenate(
        [logical, spot, info[32:40], jnp.full((56,), hset, jnp.int32)]
    ).astype(jnp.int32)

    dense = jnp.concatenate(
        [down_weight]
        + [up_weight[:, j * width : (j + 1) * width] for j in range(tiles)]
        + [self_out, cross_in[0], cross_in[1], cross_in[2], cross_out]
    )
    dense, w2, *across = lax.optimization_barrier((dense, w2, *across))
    dense = lax.all_gather(dense, AXES, axis=0)
    far = [send(v, flip(2)) for v in across]
    out_grad, far[1] = lax.optimization_barrier((out_grad, far[1]))
    pieces = mine + across + near + far
    nd = down_weight.shape[0]

    def gathered(i):
        at = nd + i * nw
        return dense[:, at : at + nw].reshape(width, width)

    dn4 = dense[:, :nd].reshape(tiles, width, width)
    up4 = jnp.stack([gathered(j) for j in range(tiles)])
    so = gathered(tiles)
    ci = jnp.stack([gathered(tiles + 1 + t) for t in range(3)])
    co = gathered(tiles + 4)

    q, kv, tr, n1 = qkv_call(meta, pieces, w2, vecs, qkv_bias)
    og = jnp.concatenate([send(pick(out_grad, p), home(p)) for p in range(2)])
    tok = jnp.concatenate([v[:rows] for v in mine])
    all_frames = jnp.concatenate([v[rows:] for v in pieces])

    o, lse = attend_call(meta, q, kv, tr)
    o4 = o.reshape(4, 1024, 192)
    o_home = [o4[0]] + [send(o4[k], flip(k)) for k in (1, 2, 3)]
    mid, ac, n2, n3, cq, ca, lse_c, kc, vc = mid_call(
        meta, tok, o_home, so, ci, co, all_frames, vecs
    )
    res, gt, ug, dg, ubg, dbg = feed_call(n3, og, ac, up4, dn4, ub4, vecs)
    gm, d0, d1, d2, d3, sog, cig, cog, eg, sums = mid_back_call(
        meta, gt, og, ac, mid, n2, cq, ca, lse_c, kc, vc, all_frames, so, ci, co, vecs, o_home
    )
    d_home = [d0] + [send(d, flip(k)) for k, d in ((1, d1), (2, d2), (3, d3))]

    def rows_of(grad):
        return grad.reshape(dp_count * 8, -1, width)

    packed = jnp.concatenate(
        [rows_of(dg)] + [rows_of(ug[j]) for j in range(tiles)]
        + [rows_of(sog), rows_of(cig[0]), rows_of(cig[1]), rows_of(cig[2]), rows_of(cog)],
        axis=1,
    )
    packed, *d_home = lax.optimization_barrier((packed, *d_home))
    dense_grad = lax.psum_scatter(packed, AXES, scatter_dimension=0, tiled=True)[0].astype(F32)

    results = [send(res[p * rows : (p + 1) * rows], home(p), True) for p in range(2)]
    eg4 = eg.reshape(4, 2 * frames, width)
    eg_near = send(eg4[2:4], flip(2)).astype(F32)
    eg_side = (eg4[1].astype(F32) + eg_near[1]).astype(BF16)
    eg_sum = eg4[0].astype(F32) + eg_near[0] + send(eg_side, flip(1)).astype(F32)
    eg_sum = eg_sum.astype(BF16)
    eg_back = [send(eg_sum[p * frames : (p + 1) * frames], home(p), True) for p in range(2)]

    dqkv, dx0, dx1, dx2, dx3 = attend_back_call(meta, q, kv, tr, o, lse, d_home, w2)
    dx3, results[0], results[1], eg_back[0], eg_back[1] = lax.optimization_barrier(
        (dx3, *results, *eg_back)
    )
    near3 = send(dx3, flip(2))
    side = (dx1.astype(F32) + near3.astype(F32)).astype(BF16)
    side_parts = [side[p * rows : (p + 1) * rows] for p in range(2)]
    side = [send(v, flip(1)) for v in side_parts]
    near2 = send(dx2, flip(2))
    n1, near3 = lax.optimization_barrier((n1, near3))

    wg, colsum = win_call(n1, dqkv)
    wg = wg.reshape(y_count, 2, 4, 2, nw, 576)

    def halve(v, move, bit, axis):
        keep = lax.dynamic_index_in_dim(v, bit, axis, False)
        give = lax.dynamic_index_in_dim(v, 1 - bit, axis, False)
        return (keep.astype(F32) + send(give, move).astype(F32)).astype(BF16)

    for bit in reversed(range((dp_count // 2).bit_length() - 1)):
        half = wg.shape[0] // 2
        wg = halve(
            wg.reshape((2, half) + wg.shape[1:]),
            lambda y, c, z, x, bit=bit: (y ^ (1 << bit), c, z, x), (y >> bit) & 1, 0,
        )
    wg = wg.reshape(2, 2, 2, 2, nw, 576)
    wg = halve(wg, lambda y, c, z, x: (y, c, z ^ 1, x), z & 1, 2)

    first = [first_back_call(dx0, near2, side[p], gm, tok, vecs, p) for p in range(2)]
    grads = [v[0] for v in first]
    first_sums = first[0][1] + first[1][1]
    wg, grads[0] = lax.optimization_barrier((wg, grads[0]))
    grads = [send(v, home(p), True) for p, v in enumerate(grads)]
    wg = halve(wg, lambda y, c, z, x: (y, c, z ^ 2, x), z >> 1, 1)
    wg = wg.reshape(4, nw, 576)

    def shard_for(k):
        return lax.dynamic_index_in_dim(wg, hset ^ k, 0, False)

    parts = jnp.stack([shard_for(0)] + [send(shard_for(k), flip(k)) for k in (1, 2, 3)])
    cols = [lax.dynamic_index_in_dim(parts, hset ^ j, 0, False) for j in range(4)]
    self_in_grad = jnp.stack(
        [jnp.concatenate([v[:, 192 * t : 192 * t + 192] for v in cols], axis=1) for t in range(3)]
    ).astype(F32)

    def returned(pair, dtype):
        pair = [v.astype(dtype) for v in pair]
        return jnp.stack([jnp.where(parity == 0, pair[0], pair[1]), jnp.where(parity == 0, pair[1], pair[0])])

    own_bias = lambda v: lax.dynamic_update_slice(
        jnp.zeros((1, width), F32), v, (0, hset * 192)
    )
    ubg = ubg.reshape(tiles, 8, width)[:, 0]
    def over_all(table):
        for k in (1, 2):
            table = table + send(table, flip(k))
        table = table + send(table, lambda y, c, z, x: (y, c, z ^ 1, x))
        table = table + send(table, lambda y, c, z, x: (y, c, z ^ 2, x))
        for bit in range((dp_count // 2).bit_length() - 1):
            table = table + send(table, lambda y, c, z, x, bit=bit: (y ^ (1 << bit), c, z, x))
        return table

    table = jnp.concatenate(
        [
            sums[1:3], sums[4:6], sums[8:12],
            own_bias(colsum[0:1, 0:192]), own_bias(colsum[0:1, 384:576]),
            dbg[0:1], ubg, jnp.zeros((16 - 11 - tiles, width), F32),
        ]
    )
    table = over_all(table)
    first_table = over_all(first_sums)
    table = jnp.concatenate(
        [
            first_table[0:1], table[0:2], first_table[1:2], table[2:4],
            table[8:10], table[4:8], table[10 : 11 + tiles],
        ]
    )
    mine_of = lambda v: lax.dynamic_slice_in_dim(v, flat * nw, nw, 1)
    vec_grad = mine_of(table[:13])
    up_bias_grad = lax.dynamic_slice_in_dim(
        table[13 : 13 + tiles].reshape(-1), flat * tiles * nw, tiles * nw, 0
    )

    def shard_grad(i):
        at = nd + i * nw
        return dense_grad[at : at + nw]

    return (
        returned(results, BF16),
        returned(grads, F32),
        returned(eg_back, F32),
        vec_grad[0:3],
        vec_grad[3:6],
        self_in_grad,
        shard_grad(tiles),
        vec_grad[6:9],
        jnp.stack([shard_grad(tiles + 1 + t) for t in range(3)]),
        shard_grad(tiles + 4),
        vec_grad[9:12],
        jnp.concatenate([shard_grad(j) for j in range(tiles)], axis=1),
        up_bias_grad,
        dense_grad[:nd],
        vec_grad[12],
    )


def solution(mesh):
    in_specs = (
        P("dp", "seq", None),
        P("dp", "seq", None),
        P("dp", "seq", None),
        P("dp", None),
        P("dp", None),
        P(None, ("dp", "seq")),
        P(None, ("dp", "seq")),
        P(None, ("dp", "seq"), None),
        P(("dp", "seq"), None),
        P(None, ("dp", "seq")),
        P(None, ("dp", "seq"), None),
        P(("dp", "seq"), None),
        P(None, ("dp", "seq")),
        P(("dp", "seq"), None),
        P(("dp", "seq")),
        P(("dp", "seq"), None),
        P(("dp", "seq")),
    )
    out_specs = (
        P("dp", "seq", None),
        P("dp", "seq", None),
        P("dp", "seq", None),
        P(None, ("dp", "seq")),
        P(None, ("dp", "seq")),
        P(None, ("dp", "seq"), None),
        P(("dp", "seq"), None),
        P(None, ("dp", "seq")),
        P(None, ("dp", "seq"), None),
        P(("dp", "seq"), None),
        P(None, ("dp", "seq")),
        P(("dp", "seq"), None),
        P(("dp", "seq")),
        P(("dp", "seq"), None),
        P(("dp", "seq")),
    )
    sizes = dict(mesh.shape)
    chosen = home_body if sizes["dp"] == 4 and sizes["seq"] == 8 else body
    return jax.shard_map(chosen, mesh=mesh, in_specs=in_specs, out_specs=out_specs, check_vma=False)
```

```python
import functools

import jax
import jax.numpy as jnp
from jax import lax
from jax.experimental import pallas as pl
from jax.experimental.pallas import tpu as pltpu
from jax.sharding import PartitionSpec as P

HEADS = 12
HEAD = 64
PROMPT = 2048
BRANCHES = 8
BLEN = 256
BLOCK = 128


def product(former, latter):
    return jnp.dot(former, latter, preferred_element_type=jnp.float32)


def product_left(former, latter):
    return lax.dot_general(
        former, latter, (((0,), (0,)), ((), ())), preferred_element_type=jnp.float32
    )


def product_right(former, latter):
    return lax.dot_general(
        former, latter, (((1,), (1,)), ((), ())), preferred_element_type=jnp.float32
    )


def column_sum(matrix):
    return jnp.sum(matrix.astype(jnp.float32), axis=0)


def norm_layer(stream, norm_gain, norm_shift):
    center = jnp.mean(stream, axis=-1, keepdims=True)
    centered = stream - center
    spread = jnp.mean(centered * centered, axis=-1, keepdims=True)
    return centered * lax.rsqrt(spread + 1e-05) * norm_gain + norm_shift


def gelu_exact(before):
    return jax.nn.gelu(before, approximate=False)


def token_info(blocks, branch_forks):
    offsets = jnp.arange(BLOCK, dtype=jnp.int32)
    logical = (blocks[:, None] * BLOCK + offsets[None, :]).reshape(-1)
    relative = logical - PROMPT
    in_branch = relative >= 0
    segment = jnp.where(in_branch, relative // BLEN + 1, 0)
    position = jnp.where(in_branch, relative % BLEN, logical)
    labels = jnp.arange(1, BRANCHES + 1, dtype=jnp.int32)
    fork_reach = jnp.sum(
        jnp.where(segment[:, None] == labels[None, :], branch_forks[None, :], 0), axis=1
    )
    return (segment, position, fork_reach)


def allowed(query_info, key_info):
    same = (query_info[0][:, None] == key_info[0][None, :]) & (
        key_info[1][None, :] <= query_info[1][:, None]
    )
    shared = (
        (query_info[0][:, None] > 0)
        & (key_info[0][None, :] == 0)
        & (key_info[1][None, :] < query_info[2][:, None])
    )
    return same | shared


def head_split(matrix):
    return matrix.reshape(matrix.shape[0], HEADS, HEAD)


def score_block(queries, key_rows, key_mask):
    scores = jnp.einsum(
        "rhd,khd->hrk",
        head_split(queries),
        head_split(key_rows),
        preferred_element_type=jnp.float32,
    ) * HEAD ** (-0.5)
    if key_mask is None:
        return scores
    return jnp.where(key_mask[None], scores, -1e30)


def attend_forward(queries, key_rows, value_rows, key_mask):
    scores = score_block(queries, key_rows, key_mask)
    row_max = jnp.max(scores, axis=2, keepdims=True)
    weights = jnp.exp(scores - row_max)
    row_total = jnp.sum(weights, axis=2, keepdims=True)
    shares = (weights / row_total).astype(jnp.bfloat16)
    attended = jnp.einsum(
        "hrk,khd->rhd", shares, head_split(value_rows), preferred_element_type=jnp.float32
    )
    return (attended.reshape(queries.shape[0], -1).astype(jnp.bfloat16), row_max, row_total)


def attend_backward(queries, key_rows, value_rows, key_mask, row_max, row_total, incoming):
    scores = score_block(queries, key_rows, key_mask)
    shares_full = jnp.exp(scores - row_max) / row_total
    shares_low = shares_full.astype(jnp.bfloat16)
    grad_heads = head_split(incoming)
    grad_values = jnp.einsum(
        "hrk,rhd->khd", shares_low, grad_heads, preferred_element_type=jnp.float32
    )
    grad_shares = jnp.einsum(
        "rhd,khd->hrk", grad_heads, head_split(value_rows), preferred_element_type=jnp.float32
    )
    inner_sum = jnp.sum(grad_shares * shares_full, axis=2, keepdims=True)
    grad_scores = (shares_full * (grad_shares - inner_sum)).astype(jnp.bfloat16)
    grad_queries = jnp.einsum(
        "hrk,khd->rhd", grad_scores, head_split(key_rows), preferred_element_type=jnp.float32
    ) * HEAD ** (-0.5)
    grad_keys = jnp.einsum(
        "hrk,rhd->khd", grad_scores, head_split(queries), preferred_element_type=jnp.float32
    ) * HEAD ** (-0.5)
    row_count = queries.shape[0]
    key_count = key_rows.shape[0]
    return (
        grad_queries.reshape(row_count, -1),
        grad_keys.reshape(key_count, -1),
        grad_values.reshape(key_count, -1),
    )


def fetch_self(shards):
    return (
        lax.all_gather(shards[0][0], ("dp", "seq"), axis=0, tiled=True),
        lax.all_gather(shards[1][0], ("dp", "seq"), axis=0, tiled=True),
        lax.all_gather(shards[2], ("dp", "seq"), axis=1, tiled=True),
        lax.all_gather(shards[3], ("dp", "seq"), axis=0, tiled=True),
        lax.all_gather(shards[4], ("dp", "seq"), axis=1, tiled=True),
    )


def fetch_cross(shards):
    return (
        lax.all_gather(shards[0][1], ("dp", "seq"), axis=0, tiled=True),
        lax.all_gather(shards[1][1], ("dp", "seq"), axis=0, tiled=True),
        lax.all_gather(shards[5], ("dp", "seq"), axis=1, tiled=True),
        lax.all_gather(shards[6], ("dp", "seq"), axis=0, tiled=True),
        lax.all_gather(shards[7], ("dp", "seq"), axis=1, tiled=True),
    )


def fetch_feed(shards):
    return (
        lax.all_gather(shards[0][2], ("dp", "seq"), axis=0, tiled=True),
        lax.all_gather(shards[1][2], ("dp", "seq"), axis=0, tiled=True),
        lax.all_gather(shards[8], ("dp", "seq"), axis=0, tiled=True),
        lax.all_gather(shards[9], ("dp", "seq"), axis=0, tiled=True),
        lax.all_gather(shards[10], ("dp", "seq"), axis=0, tiled=True),
        lax.all_gather(shards[11], ("dp", "seq"), axis=0, tiled=True),
    )


def body(
    tokens,
    encoder_states,
    out_grad,
    block_map,
    branch_fork,
    norm_gain,
    norm_bias,
    self_in,
    self_out,
    self_bias,
    cross_in,
    cross_out,
    cross_bias,
    up_weight,
    up_bias,
    down_weight,
    down_bias,
):
    shards = (
        norm_gain,
        norm_bias,
        self_in,
        self_out,
        self_bias,
        cross_in,
        cross_out,
        cross_bias,
        up_weight,
        up_bias,
        down_weight,
        down_bias,
    )
    model_width = tokens.shape[2]
    hidden_width = up_weight.shape[1]
    seq_count = lax.axis_size("seq")
    seq_place = lax.axis_index("seq")

    def micro_step(grad_sums, inputs):
        tokens_in, encoded, cotangent, blocks, branch_forks = inputs
        slot_count = blocks.shape[0] // seq_count
        own_blocks = lax.dynamic_slice_in_dim(blocks, seq_place * slot_count, slot_count)
        query_info = token_info(own_blocks, branch_forks)
        full_info = token_info(blocks, branch_forks)
        key_mask = allowed(query_info, full_info)
        gain_first, shift_first, attend_in, attend_out, attend_bias = fetch_self(shards)
        stream = tokens_in.astype(jnp.float32)
        norm_full, pull_first = jax.vjp(
            norm_layer, stream, gain_first.astype(jnp.float32), shift_first.astype(jnp.float32)
        )
        norm_first = norm_full.astype(jnp.bfloat16)
        queries = (product(norm_first, attend_in[0]) + attend_bias[0].astype(jnp.float32)).astype(
            jnp.bfloat16
        )
        key_local = product(norm_first, attend_in[1]).astype(jnp.bfloat16)
        value_local = (
            product(norm_first, attend_in[2]) + attend_bias[1].astype(jnp.float32)
        ).astype(jnp.bfloat16)
        key_rows, value_rows = (
            lax.all_gather(key_local, "seq", axis=0, tiled=True),
            lax.all_gather(value_local, "seq", axis=0, tiled=True),
        )
        attended, self_max, self_total = attend_forward(queries, key_rows, value_rows, key_mask)
        middle = stream + product(attended, attend_out) + attend_bias[2].astype(jnp.float32)
        gain_second, shift_second, cross_proj, cross_back, cross_shift = fetch_cross(shards)
        cross_key_local = product(encoded, cross_proj[1]).astype(jnp.bfloat16)
        cross_value_local = (
            product(encoded, cross_proj[2]) + cross_shift[1].astype(jnp.float32)
        ).astype(jnp.bfloat16)
        cross_keys, cross_values = (
            lax.all_gather(cross_key_local, "seq", axis=0, tiled=True),
            lax.all_gather(cross_value_local, "seq", axis=0, tiled=True),
        )
        norm_full_second, pull_second = jax.vjp(
            norm_layer, middle, gain_second.astype(jnp.float32), shift_second.astype(jnp.float32)
        )
        norm_second = norm_full_second.astype(jnp.bfloat16)
        cross_queries = (
            product(norm_second, cross_proj[0]) + cross_shift[0].astype(jnp.float32)
        ).astype(jnp.bfloat16)
        cross_attended, cross_max, cross_total = attend_forward(
            cross_queries, cross_keys, cross_values, None
        )
        after_cross = (
            middle + product(cross_attended, cross_back) + cross_shift[2].astype(jnp.float32)
        )
        gain_third, shift_third, feed_up, feed_up_bias, feed_down, feed_down_bias = fetch_feed(
            shards
        )
        norm_full_third, pull_third = jax.vjp(
            norm_layer, after_cross, gain_third.astype(jnp.float32), shift_third.astype(jnp.float32)
        )
        norm_third = norm_full_third.astype(jnp.bfloat16)
        before = product(norm_third, feed_up) + feed_up_bias.astype(jnp.float32)
        activated_full, gelu_pull = jax.vjp(gelu_exact, before)
        activated = activated_full.astype(jnp.bfloat16)
        result = after_cross + product(activated, feed_down) + feed_down_bias.astype(jnp.float32)
        gain_third, shift_third, feed_up, feed_up_bias, feed_down, feed_down_bias = fetch_feed(
            shards
        )
        cot_float = cotangent.astype(jnp.float32)
        grad_act = product_right(cotangent, feed_down)
        grad_down = product_left(activated, cotangent)
        grad_down_bias = jnp.sum(cot_float, axis=0)
        grad_before = gelu_pull(grad_act)[0].astype(jnp.bfloat16)
        grad_up = product_left(norm_third, grad_before)
        grad_up_bias = column_sum(grad_before)
        grad_third = product_right(grad_before, feed_up)
        grad_after_norm, grad_gain_third, grad_shift_third = pull_third(grad_third)
        grad_after = cot_float + grad_after_norm
        gain_second, shift_second, cross_proj, cross_back, cross_shift = fetch_cross(shards)
        grad_after_low = grad_after.astype(jnp.bfloat16)
        grad_cross_back = product_left(cross_attended, grad_after_low)
        grad_cross_out_bias = column_sum(grad_after_low)
        grad_cross_attended = product_right(grad_after_low, cross_back).astype(jnp.bfloat16)
        grad_cross_queries, grad_cross_keys, grad_cross_values = attend_backward(
            cross_queries,
            cross_keys,
            cross_values,
            None,
            cross_max,
            cross_total,
            grad_cross_attended,
        )
        cross_key_part, cross_value_part = (
            lax.psum_scatter(
                grad_cross_keys.astype(jnp.bfloat16), "seq", scatter_dimension=0, tiled=True
            ).astype(jnp.float32),
            lax.psum_scatter(
                grad_cross_values.astype(jnp.bfloat16), "seq", scatter_dimension=0, tiled=True
            ).astype(jnp.float32),
        )
        cross_key_low = cross_key_part.astype(jnp.bfloat16)
        cross_value_low = cross_value_part.astype(jnp.bfloat16)
        cross_query_low = grad_cross_queries.astype(jnp.bfloat16)
        grad_cross_proj = jnp.stack(
            [
                product_left(norm_second, cross_query_low),
                product_left(encoded, cross_key_low),
                product_left(encoded, cross_value_low),
            ]
        )
        grad_cross_shift = jnp.stack(
            [column_sum(cross_query_low), column_sum(cross_value_low), grad_cross_out_bias]
        )
        encoder_grad = product_right(cross_key_low, cross_proj[1]) + product_right(
            cross_value_low, cross_proj[2]
        )
        grad_second = product_right(cross_query_low, cross_proj[0])
        grad_middle_norm, grad_gain_second, grad_shift_second = pull_second(grad_second)
        grad_middle = grad_after + grad_middle_norm
        gain_first, shift_first, attend_in, attend_out, attend_bias = fetch_self(shards)
        grad_middle_low = grad_middle.astype(jnp.bfloat16)
        grad_attend_out = product_left(attended, grad_middle_low)
        grad_out_bias = column_sum(grad_middle_low)
        grad_attended = product_right(grad_middle_low, attend_out).astype(jnp.bfloat16)
        grad_queries, grad_keys, grad_values = attend_backward(
            queries, key_rows, value_rows, key_mask, self_max, self_total, grad_attended
        )
        key_part, value_part = (
            lax.psum_scatter(
                grad_keys.astype(jnp.bfloat16), "seq", scatter_dimension=0, tiled=True
            ).astype(jnp.float32),
            lax.psum_scatter(
                grad_values.astype(jnp.bfloat16), "seq", scatter_dimension=0, tiled=True
            ).astype(jnp.float32),
        )
        key_low = key_part.astype(jnp.bfloat16)
        value_low = value_part.astype(jnp.bfloat16)
        query_low = grad_queries.astype(jnp.bfloat16)
        grad_attend_in = jnp.stack(
            [
                product_left(norm_first, query_low),
                product_left(norm_first, key_low),
                product_left(norm_first, value_low),
            ]
        )
        grad_attend_bias = jnp.stack([column_sum(query_low), column_sum(value_low), grad_out_bias])
        grad_first = (
            product_right(query_low, attend_in[0])
            + product_right(key_low, attend_in[1])
            + product_right(value_low, attend_in[2])
        )
        grad_stream_norm, grad_gain_first, grad_shift_first = pull_first(grad_first)
        tokens_grad = grad_middle + grad_stream_norm
        updates = (
            jnp.stack([grad_gain_first, grad_gain_second, grad_gain_third]),
            jnp.stack([grad_shift_first, grad_shift_second, grad_shift_third]),
            grad_attend_in,
            grad_attend_out,
            grad_attend_bias,
            grad_cross_proj,
            grad_cross_back,
            grad_cross_shift,
            grad_up,
            grad_up_bias,
            grad_down,
            grad_down_bias,
        )
        grad_sums = tuple((former + latter for former, latter in zip(grad_sums, updates)))
        return (grad_sums, (result.astype(jnp.bfloat16), tokens_grad, encoder_grad))

    starting = (
        jnp.zeros((3, model_width), jnp.float32),
        jnp.zeros((3, model_width), jnp.float32),
        jnp.zeros((3, model_width, model_width), jnp.float32),
        jnp.zeros((model_width, model_width), jnp.float32),
        jnp.zeros((3, model_width), jnp.float32),
        jnp.zeros((3, model_width, model_width), jnp.float32),
        jnp.zeros((model_width, model_width), jnp.float32),
        jnp.zeros((3, model_width), jnp.float32),
        jnp.zeros((model_width, hidden_width), jnp.float32),
        jnp.zeros((hidden_width,), jnp.float32),
        jnp.zeros((hidden_width, model_width), jnp.float32),
        jnp.zeros((model_width,), jnp.float32),
    )
    grad_sums, outputs = lax.scan(
        micro_step, starting, (tokens, encoder_states, out_grad, block_map, branch_fork)
    )
    feed_part = (
        lax.psum_scatter(grad_sums[8], ("dp", "seq"), scatter_dimension=0, tiled=True),
        lax.psum_scatter(grad_sums[9], ("dp", "seq"), scatter_dimension=0, tiled=True),
        lax.psum_scatter(grad_sums[10], ("dp", "seq"), scatter_dimension=0, tiled=True),
        lax.psum_scatter(grad_sums[11], ("dp", "seq"), scatter_dimension=0, tiled=True),
    )
    cross_part = (
        lax.psum_scatter(grad_sums[5], ("dp", "seq"), scatter_dimension=1, tiled=True),
        lax.psum_scatter(grad_sums[6], ("dp", "seq"), scatter_dimension=0, tiled=True),
        lax.psum_scatter(grad_sums[7], ("dp", "seq"), scatter_dimension=1, tiled=True),
    )
    self_part = (
        lax.psum_scatter(grad_sums[0], ("dp", "seq"), scatter_dimension=1, tiled=True),
        lax.psum_scatter(grad_sums[1], ("dp", "seq"), scatter_dimension=1, tiled=True),
        lax.psum_scatter(grad_sums[2], ("dp", "seq"), scatter_dimension=1, tiled=True),
        lax.psum_scatter(grad_sums[3], ("dp", "seq"), scatter_dimension=0, tiled=True),
        lax.psum_scatter(grad_sums[4], ("dp", "seq"), scatter_dimension=1, tiled=True),
    )
    return (
        outputs[0],
        outputs[1],
        outputs[2],
        self_part[0],
        self_part[1],
        self_part[2],
        self_part[3],
        self_part[4],
        cross_part[0],
        cross_part[1],
        cross_part[2],
        feed_part[0],
        feed_part[1],
        feed_part[2],
        feed_part[3],
    )


LOG2E = 1.4426950408889634
LN2 = 0.6931471805599453
QSCALE = HEAD ** (-0.5) * LOG2E
AXES = ("dp", "seq")
F32 = jnp.float32
BF16 = jnp.bfloat16
ANY = pl.BlockSpec(memory_space=pl.ANY)
SMEM = pl.BlockSpec(memory_space=pltpu.SMEM)


def nn(a, b):
    return lax.dot_general(a, b, (((1,), (0,)), ((), ())), preferred_element_type=F32)


def nt(a, b):
    return lax.dot_general(a, b, (((1,), (1,)), ((), ())), preferred_element_type=F32)


def tn(a, b):
    return lax.dot_general(a, b, (((0,), (0,)), ((), ())), preferred_element_type=F32)


def whole(shape):
    zeros = (0,) * len(shape)
    return pl.BlockSpec(shape, lambda *_: zeros)


def params(**kw):
    return pltpu.CompilerParams(vmem_limit_bytes=60 * 1024 * 1024, **kw)


def cost(flops, nbytes, trans=0):
    return pl.CostEstimate(flops=int(flops), bytes_accessed=int(nbytes), transcendentals=int(trans))


def stats(v):
    mean = jnp.mean(v, axis=-1, keepdims=True)
    centered = v - mean
    var = jnp.mean(centered * centered, axis=-1, keepdims=True)
    rstd = lax.rsqrt(var + 1e-05)
    return centered * rstd, rstd


def norm_back(v, e, gain):
    z, rstd = stats(v)
    f = e * gain
    grad = rstd * (
        f - jnp.mean(f, axis=-1, keepdims=True) - z * jnp.mean(f * z, axis=-1, keepdims=True)
    )
    return grad, jnp.sum(e * z, axis=0, keepdims=True), jnp.sum(e, axis=0, keepdims=True)


def qkv_kernel(meta, *refs):
    pieces = refs[:8]
    w_ref, vec_ref, bias_ref, q_ref, kv_ref, tr_ref, n1_ref, buf, sem = refs[8:]
    rows = buf.shape[0] // 8
    step = pl.program_id(0)

    @pl.when(step == 0)
    def _():
        copies = [
            pltpu.make_async_copy(pieces[i], buf.at[pl.ds(i * rows, rows), :], sem.at[i])
            for i in range(8)
        ]
        for c in copies:
            c.start()
        for c in copies:
            c.wait()

    gain, shift = vec_ref[0:1, :], vec_ref[3:4, :]
    w = w_ref[...]
    bias = bias_ref[0:1, :]
    for u in range(4):
        b = meta[32 + step * 4 + u]
        off = pl.multiple_of((b // 4) * rows + (b % 4) * 128, 32)
        x = buf[pl.ds(off, 128), :].astype(F32)
        z, _ = stats(x)
        n1 = (z * gain + shift).astype(BF16)
        r = slice(u * 128, (u + 1) * 128)
        n1_ref[r, :] = n1
        y = nn(n1, w) + bias
        kvt = jnp.transpose(y[:, 192:576]).astype(BF16)
        for t in range(2):
            for h in range(3):
                o = (t * 3 + h) * 64
                tr_ref[t * 3 + h, :, r] = kvt[o : o + 64, :]
        yq = (y[:, 0:192] * QSCALE).astype(BF16)
        yk = y[:, 192:576].astype(BF16)
        zero = jnp.zeros((128, 64), BF16)
        for h in range(3):
            q_ref[h, r, :] = jnp.concatenate([yq[:, h * 64 : h * 64 + 64], zero], axis=1)
            kv_ref[h, r, :] = jnp.concatenate(
                [yk[:, h * 64 : h * 64 + 64], yk[:, 192 + h * 64 : 256 + h * 64]], axis=1
            )


def qkv_call(meta, pieces, w2, vecs, bias):
    rows = pieces[0].shape[0]
    grid = (8,)
    return pl.pallas_call(
        qkv_kernel,
        grid_spec=pltpu.PrefetchScalarGridSpec(
            num_scalar_prefetch=1,
            grid=grid,
            in_specs=[ANY] * 8 + [whole(w2.shape), whole(vecs.shape), whole(bias.shape)],
            out_specs=[
                pl.BlockSpec((3, 512, 128), lambda i, m: (0, i, 0)),
                pl.BlockSpec((3, 512, 128), lambda i, m: (0, i, 0)),
                pl.BlockSpec((6, 64, 512), lambda i, m: (0, 0, i)),
                pl.BlockSpec((512, 768), lambda i, m: (i, 0)),
            ],
            scratch_shapes=[pltpu.VMEM((8 * rows, 768), BF16), pltpu.SemaphoreType.DMA((8,))],
        ),
        out_shape=[
            jax.ShapeDtypeStruct((3, 4096, 128), BF16),
            jax.ShapeDtypeStruct((3, 4096, 128), BF16),
            jax.ShapeDtypeStruct((6, 64, 4096), BF16),
            jax.ShapeDtypeStruct((4096, 768), BF16),
        ],
        compiler_params=params(dimension_semantics=("arbitrary",)),
        cost_estimate=cost(2 * 4096 * 768 * 576, 20e6),
        name="qkv",
    )(meta, *pieces, w2, vecs, bias)


def tile_plan(meta, qi):
    branch = qi >= 8
    fork = meta[64 + jnp.maximum(qi - 8, 0)]
    count = jnp.where(branch, (fork + 255) // 256, qi) + 1
    reach = jnp.where(branch, fork, 4096)

    def tile(t, own):
        if own:
            kt = qi
        else:
            kt = jnp.where(t == count - 1, qi, t)
        key = lax.broadcasted_iota(jnp.int32, (256, 256), 0)
        query = lax.broadcasted_iota(jnp.int32, (256, 256), 1)
        if own:
            mask = key <= query
        else:
            limit = jnp.where(t == count - 1, 0, jnp.minimum(reach - t * 256, 256) - 1)
            slope = jnp.where(t == count - 1, 1, 0)
            mask = key <= query[0:1, :] * slope + limit
        return pl.ds(pl.multiple_of(kt * 256, 256), 256), mask

    return count, tile


def tile_pairs(count, step):
    def pair(i, carry):
        step(i * 2, False)
        step(i * 2 + 1, False)
        return carry

    lax.fori_loop(0, count // 2, pair, 0)

    @pl.when(count % 2 == 1)
    def _():
        step(count - 1, True)


def attend_kernel(meta, q_ref, kv_ref, tr_ref, o_ref, lse_ref, m_ref, l_ref, acc_ref):
    def q_tile(qi, carry):
        count, tile = tile_plan(meta, qi)
        qs = pl.ds(pl.multiple_of(qi * 256, 256), 256)
        m_ref[...] = jnp.full_like(m_ref, -1e30)
        l_ref[...] = jnp.zeros_like(l_ref)
        acc_ref[...] = jnp.zeros_like(acc_ref)

        def k_tile(t, own):
            ks, mask = tile(t, own)
            s = [nt(kv_ref[h, ks, :], q_ref[h, qs, :]) for h in range(3)]
            s = [jnp.where(mask, v, -1e30) for v in s]
            old = [m_ref[h : h + 1, :] for h in range(3)]
            new = [jnp.maximum(old[h], jnp.max(s[h], axis=0, keepdims=True)) for h in range(3)]
            p = [jnp.exp2(s[h] - new[h]) for h in range(3)]
            out = [nn(tr_ref[3 + h, :, ks], p[h].astype(BF16)) for h in range(3)]
            for h in range(3):
                alpha = jnp.exp2(old[h] - new[h])
                m_ref[h : h + 1, :] = new[h]
                l_ref[h : h + 1, :] = l_ref[h : h + 1, :] * alpha + jnp.sum(p[h], axis=0, keepdims=True)
                hs = slice(h * 64, h * 64 + 64)
                acc_ref[hs, :] = acc_ref[hs, :] * alpha + out[h]

        tile_pairs(count, k_tile)
        for h in range(3):
            hs = slice(h * 64, h * 64 + 64)
            l = l_ref[h : h + 1, :]
            acc_ref[hs, :] = acc_ref[hs, :] * (1.0 / l)
            lse_ref[h : h + 1, qs] = m_ref[h : h + 1, :] + jnp.log2(l)
        out = jnp.transpose(acc_ref[...]).astype(BF16)
        for u in range(2):
            o_ref[meta[32 + qi * 2 + u]] = out[u * 128 : (u + 1) * 128, :]
        return carry

    lax.fori_loop(0, 16, q_tile, 0)


def attend_call(meta, q, kv, tr):
    return pl.pallas_call(
        attend_kernel,
        grid_spec=pltpu.PrefetchScalarGridSpec(
            num_scalar_prefetch=1,
            grid=(1,),
            in_specs=[whole(q.shape), whole(kv.shape), whole(tr.shape)],
            out_specs=[whole((32, 128, 192)), whole((8, 4096))],
            scratch_shapes=[
                pltpu.VMEM((8, 256), F32),
                pltpu.VMEM((8, 256), F32),
                pltpu.VMEM((192, 256), F32),
            ],
        ),
        out_shape=[
            jax.ShapeDtypeStruct((32, 128, 192), BF16),
            jax.ShapeDtypeStruct((8, 4096), F32),
        ],
        compiler_params=params(dimension_semantics=("arbitrary",)),
        cost_estimate=cost(20e9, 10e6, 20e6),
        name="attend",
    )(meta, q, kv, tr)


def attend_back_kernel(
    meta, q_ref, kv_ref, tr_ref, o_ref, lse_ref, d0, d1, d2, d3, w_ref,
    out_ref, x0, x1, x2, x3, do_ref, di_ref, dq_ref, acc_ref, wt_ref,
):
    pieces = (d0, d1, d2, d3)
    zero = jnp.zeros((128, 64), BF16)
    head = lax.broadcasted_iota(jnp.int32, (8, 192), 0) * 64
    lane = lax.broadcasted_iota(jnp.int32, (8, 192), 1)
    pick = jnp.where((lane >= head) & (lane < head + 64), 1.0, 0.0).astype(BF16)

    def arrange(kk, carry):
        rs = pl.ds(pl.multiple_of(kk * 128, 128), 128)
        for k in range(4):
            b = k * 8 + kk
            at = pl.ds(pl.multiple_of(meta[b] * 128, 128), 128)
            do = pieces[k][rs, :]
            prod = do.astype(F32) * o_ref[b].astype(F32)
            high = prod.astype(BF16)
            low = (prod - high.astype(F32)).astype(BF16)
            di_ref[:, at] = nt(pick, high) + nt(pick, low)
            for h in range(3):
                do_ref[h, at, :] = jnp.concatenate([zero, do[:, h * 64 : h * 64 + 64]], axis=1)
        return carry

    lax.fori_loop(0, 8, arrange, 0)
    acc_ref[...] = jnp.zeros_like(acc_ref)

    def q_tile(qi, carry):
        count, tile = tile_plan(meta, qi)
        qs = pl.ds(pl.multiple_of(qi * 256, 256), 256)
        dq_ref[...] = jnp.zeros_like(dq_ref)

        def k_tile(t, own):
            ks, mask = tile(t, own)
            q = [q_ref[h, qs, :] for h in range(3)]
            do = [do_ref[h, qs, :] for h in range(3)]
            kv = [kv_ref[h, ks, :] for h in range(3)]
            s = [nt(kv[h], q[h]) for h in range(3)]
            dp = [nt(kv[h], do[h]) for h in range(3)]
            p, ds = [], []
            for h in range(3):
                e = jnp.where(mask, jnp.exp2(s[h] - lse_ref[h : h + 1, qs]), 0.0)
                p.append(e.astype(BF16))
                ds.append((e * (dp[h] - di_ref[h : h + 1, qs])).astype(BF16))
            for h in range(3):
                acc_ref[h, ks, :] += nn(ds[h], q[h]) + nn(p[h], do[h])
                hs = slice(h * 64, h * 64 + 64)
                dq_ref[hs, :] += nn(tr_ref[h, :, ks], ds[h])

        tile_pairs(count, k_tile)
        out_ref[qs, 0:192] = (jnp.transpose(dq_ref[...]) * HEAD ** (-0.5)).astype(BF16)
        return carry

    lax.fori_loop(0, 16, q_tile, 0)

    def finish(t, carry):
        rs = pl.ds(pl.multiple_of(t * 256, 256), 256)
        a = [acc_ref[h, rs, :] for h in range(3)]
        dk = jnp.concatenate([v[:, 0:64] for v in a], axis=1) * LN2
        dv = jnp.concatenate([v[:, 64:128] for v in a], axis=1)
        out_ref[rs, 192:576] = jnp.concatenate([dk, dv], axis=1).astype(BF16)
        return carry

    lax.fori_loop(0, 16, finish, 0)
    wt = jnp.transpose(w_ref[...])
    wt_ref[...] = wt

    def spread(i, carry):
        rs = pl.ds(pl.multiple_of(i * 512, 512), 512)
        for k, x_ref in enumerate((x0, x1, x2, x3)):
            rows = [
                out_ref[pl.ds(pl.multiple_of(meta[k * 8 + i * 4 + u] * 128, 128), 128), :]
                for u in range(4)
            ]
            x_ref[rs, :] = nn(jnp.concatenate(rows, axis=0), wt_ref[...]).astype(BF16)
        return carry

    lax.fori_loop(0, 2, spread, 0)


def attend_back_call(meta, q, kv, tr, o, lse, pieces, w2):
    ins = [q, kv, tr, o, lse, *pieces, w2]
    return pl.pallas_call(
        attend_back_kernel,
        grid_spec=pltpu.PrefetchScalarGridSpec(
            num_scalar_prefetch=1,
            grid=(1,),
            in_specs=[whole(v.shape) for v in ins],
            out_specs=[whole((4096, 576))] + [whole((1024, 768))] * 4,
            scratch_shapes=[
                pltpu.VMEM((3, 4096, 128), BF16),
                pltpu.VMEM((8, 4096), F32),
                pltpu.VMEM((192, 256), F32),
                pltpu.VMEM((3, 4096, 128), F32),
                pltpu.VMEM((576, 768), BF16),
            ],
        ),
        out_shape=[jax.ShapeDtypeStruct((4096, 576), BF16)]
        + [jax.ShapeDtypeStruct((1024, 768), BF16)] * 4,
        compiler_params=params(dimension_semantics=("arbitrary",)),
        cost_estimate=cost(50e9, 15e6, 20e6),
        name="attend_back",
    )(meta, *ins)


def win_kernel(n_ref, d_ref, g_ref, s_ref, acc_ref):
    step = pl.program_id(0)

    @pl.when(step == 0)
    def _():
        acc_ref[...] = jnp.zeros_like(acc_ref)
        s_ref[...] = jnp.zeros_like(s_ref)

    d = d_ref[...]
    acc_ref[...] += tn(n_ref[...], d)
    s_ref[0:1, :] += jnp.sum(d.astype(F32), axis=0, keepdims=True)

    @pl.when(step == pl.num_programs(0) - 1)
    def _():
        g_ref[...] = acc_ref[...].astype(BF16)


def win_call(n1, dqkv):
    return pl.pallas_call(
        win_kernel,
        grid=(4,),
        in_specs=[
            pl.BlockSpec((1024, 768), lambda i: (i, 0)),
            pl.BlockSpec((1024, 576), lambda i: (i, 0)),
        ],
        out_specs=[whole((768, 576)), whole((8, 576))],
        out_shape=[
            jax.ShapeDtypeStruct((768, 576), BF16),
            jax.ShapeDtypeStruct((8, 576), F32),
        ],
        scratch_shapes=[pltpu.VMEM((768, 576), F32)],
        compiler_params=params(dimension_semantics=("arbitrary",)),
        cost_estimate=cost(2 * 4096 * 768 * 576, 12e6),
        name="win",
    )(n1, dqkv)


def head_masks(frames):
    lane = lax.broadcasted_iota(jnp.int32, (frames, 128), 1) < 64
    return lane, jnp.logical_not(lane)


def mid_kernel(
    meta, tok_ref, o0, o1, o2, o3, so_ref, ci_ref, co_ref, fr_ref, vec_ref,
    mid_ref, ac_ref, n2_ref, n3_ref, cq_ref, ca_ref, lse_ref, kc_ref, vc_ref,
    km_ref, vmt_ref,
):
    frames = fr_ref.shape[0]
    hset = meta[72]

    @pl.when(pl.program_id(0) == 0)
    def _():
        fr = fr_ref[...]
        kc = nn(fr, ci_ref[1]).astype(BF16)
        vc = (nn(fr, ci_ref[2]) + vec_ref[10:11, :]).astype(BF16)
        kc_ref[...] = kc
        vc_ref[...] = vc
        zero = jnp.zeros((frames, 128), BF16)
        masks = head_masks(frames)
        for hp in range(6):
            ls = slice(hp * 128, hp * 128 + 128)
            for e in range(2):
                km_ref[hp * 2 + e] = jnp.where(masks[e], kc[:, ls], zero)
                vmt_ref[hp * 2 + e] = jnp.transpose(
                    jnp.where(masks[e], vc[:, ls].astype(F32), 0.0)
                ).astype(BF16)

    acc = tok_ref[...].astype(F32) + vec_ref[8:9, :]
    for k, o in enumerate((o0, o1, o2, o3)):
        at = pl.ds(pl.multiple_of((hset ^ k) * 192, 64), 192)
        acc = acc + nn(o[...], so_ref[at, :])
    mid_ref[...] = acc
    z, _ = stats(acc)
    n2 = (z * vec_ref[1:2, :] + vec_ref[4:5, :]).astype(BF16)
    n2_ref[...] = n2
    cq = ((nn(n2, ci_ref[0]) + vec_ref[9:10, :]) * QSCALE).astype(BF16)
    cq_ref[...] = cq
    ca = []
    for hp in range(6):
        qp = cq[:, hp * 128 : hp * 128 + 128]
        out = None
        for e in range(2):
            h = hp * 2 + e
            s = nt(km_ref[h], qp)
            m = jnp.max(s, axis=0, keepdims=True)
            p = jnp.exp2(s - m)
            l = jnp.sum(p, axis=0, keepdims=True)
            lse_ref[h : h + 1, :] = m + jnp.log2(l)
            part = nn(vmt_ref[h], p.astype(BF16)) * (1.0 / l)
            out = part if out is None else out + part
        ca.append(jnp.transpose(out).astype(BF16))
    ca = jnp.concatenate(ca, axis=1)
    ca_ref[...] = ca
    ac = acc + nn(ca, co_ref[...]) + vec_ref[11:12, :]
    ac_ref[...] = ac
    z, _ = stats(ac)
    n3_ref[...] = (z * vec_ref[2:3, :] + vec_ref[5:6, :]).astype(BF16)


def mid_call(meta, tok, pieces, so, ci, co, frames, vecs):
    rows, width = tok.shape
    tile = 256
    nf = frames.shape[0]
    row = pl.BlockSpec((tile, width), lambda i, m: (i, 0))
    row4 = pl.BlockSpec((tile, 192), lambda i, m: (i, 0))
    sds = jax.ShapeDtypeStruct
    return pl.pallas_call(
        mid_kernel,
        grid_spec=pltpu.PrefetchScalarGridSpec(
            num_scalar_prefetch=1,
            grid=(rows // tile,),
            in_specs=[row] + [row4] * 4
            + [whole(so.shape), whole(ci.shape), whole(co.shape), whole(frames.shape), whole(vecs.shape)],
            out_specs=[row] * 6
            + [pl.BlockSpec((16, tile), lambda i, m: (0, i)), whole((nf, width)), whole((nf, width))],
            scratch_shapes=[pltpu.VMEM((12, nf, 128), BF16), pltpu.VMEM((12, 128, nf), BF16)],
        ),
        out_shape=[
            sds((rows, width), F32), sds((rows, width), F32), sds((rows, width), BF16),
            sds((rows, width), BF16), sds((rows, width), BF16), sds((rows, width), BF16),
            sds((16, rows), F32), sds((nf, width), BF16), sds((nf, width), BF16),
        ],
        compiler_params=params(dimension_semantics=("arbitrary",)),
        cost_estimate=cost(8e9, 25e6, 3e6),
        name="middle",
    )(meta, tok, *pieces, so, ci, co, frames, vecs)


def normal_parts(b):
    e = jnp.exp2(b * b * (-0.5 * LOG2E))
    a = jnp.abs(b) * 0.7071067811865476
    t = 1.0 / (1.0 + 0.3275911 * a)
    poly = t * (
        0.254829592 + t * (-0.284496736 + t * (1.421413741 + t * (-1.453152027 + t * 1.061405429)))
    )
    tail = 0.5 * poly * e
    return jnp.where(b < 0.0, tail, 1.0 - tail), e * 0.3989422804014327


def feed_kernel(
    n3_ref, og_ref, ac_ref, up_ref, dn_ref, ub_ref, vec_ref,
    res_ref, gt_ref, ug_ref, dg_ref, ubg_ref, dbg_ref,
    acc_ref, n3t_ref, act_ref, gb_ref,
):
    step = pl.program_id(0)
    rows, width = n3_ref.shape

    @pl.when(step == 0)
    def _():
        acc_ref[...] = ac_ref[...] + vec_ref[12:13, :]
        gt_ref[...] = jnp.zeros_like(gt_ref)
        dbg_ref[...] = jnp.zeros_like(dbg_ref)
        dbg_ref[0:1, :] = jnp.sum(og_ref[...].astype(F32), axis=0, keepdims=True)
        n3t_ref[...] = jnp.transpose(n3_ref[...])

    up = up_ref[...].reshape(width, width)
    dn = dn_ref[...].reshape(width, width)
    ub = ub_ref[pl.ds(step, 1), :]
    total = jnp.zeros((1, width), F32)
    for r in range(rows // 256):
        rs = slice(r * 256, (r + 1) * 256)
        n3 = n3_ref[rs, :]
        og = og_ref[rs, :]
        b = nn(n3, up) + ub
        cdf, pdf = normal_parts(b)
        act = (b * cdf).astype(BF16)
        gb = (nt(og, dn) * (cdf + b * pdf)).astype(BF16)
        act_ref[rs, :] = act
        gb_ref[rs, :] = gb
        total = total + jnp.sum(gb.astype(F32), axis=0, keepdims=True)
        acc_ref[rs, :] += nn(act, dn)
        gt_ref[rs, :] += nt(gb, up)
    ubg_ref[...] = jnp.broadcast_to(total, (8, width))
    ug_ref[...] = nn(n3t_ref[...], gb_ref[...]).astype(BF16).reshape(ug_ref.shape)
    dg_ref[...] = tn(act_ref[...], og_ref[...]).astype(BF16).reshape(dg_ref.shape)

    @pl.when(step == pl.num_programs(0) - 1)
    def _():
        res_ref[...] = acc_ref[...].astype(BF16)


def feed_call(n3, og, ac, up4, dn4, ub4, vecs):
    rows, width = n3.shape
    sds = jax.ShapeDtypeStruct
    tiles = up4.shape[0]
    tile = pl.BlockSpec((1, width, width), lambda i: (i, 0, 0))
    return pl.pallas_call(
        feed_kernel,
        grid=(tiles,),
        in_specs=[whole(n3.shape), whole(og.shape), whole(ac.shape), tile, tile, whole(ub4.shape), whole(vecs.shape)],
        out_specs=[
            whole((rows, width)), whole((rows, width)), tile, tile,
            pl.BlockSpec((8, width), lambda i: (i, 0)), whole((8, width)),
        ],
        out_shape=[
            sds((rows, width), BF16), sds((rows, width), F32),
            sds((tiles, width, width), BF16), sds((tiles, width, width), BF16),
            sds((tiles * 8, width), F32), sds((8, width), F32),
        ],
        scratch_shapes=[
            pltpu.VMEM((rows, width), F32), pltpu.VMEM((width, rows), BF16),
            pltpu.VMEM((rows, width), BF16), pltpu.VMEM((rows, width), BF16),
        ],
        compiler_params=params(dimension_semantics=("arbitrary",)),
        cost_estimate=cost(2 * 6 * rows * width * width * tiles, 35e6, 6e6),
        name="feed",
    )(n3, og, ac, up4, dn4, ub4, vecs)


def mid_back_kernel(
    meta, gt_ref, og_ref, ac_ref, mid_ref, n2_ref, cq_ref, ca_ref, lse_ref, kc_ref, vc_ref,
    fr_ref, so_ref, ci_ref, co_ref, vec_ref, o0, o1, o2, o3,
    gm_ref, do0, do1, do2, do3, sog_ref, cig_ref, cog_ref, eg_ref, sums_ref,
    km_ref, kmt_ref, vm_ref, dk_ref, dv_ref, so_acc, cq_acc, co_acc,
):
    frames = fr_ref.shape[0]
    hset = meta[72]
    step = pl.program_id(0)
    last = pl.num_programs(0) - 1
    masks = head_masks(frames)

    @pl.when(step == 0)
    def _():
        zero = jnp.zeros((frames, 128), BF16)
        for hp in range(6):
            ls = slice(hp * 128, hp * 128 + 128)
            k, v = kc_ref[:, ls], vc_ref[:, ls]
            for e in range(2):
                km_ref[hp * 2 + e] = jnp.where(masks[e], k, zero)
                vm_ref[hp * 2 + e] = jnp.where(masks[e], v, zero)
                kmt_ref[hp * 2 + e] = jnp.transpose(
                    jnp.where(masks[e], k.astype(F32), 0.0)
                ).astype(BF16)
        for ref in (dk_ref, dv_ref, so_acc, cq_acc, co_acc, sums_ref):
            ref[...] = jnp.zeros_like(ref)

    def count(row, value):
        sums_ref[row : row + 1, :] += value

    gt = gt_ref[...]
    back, gain, shift = norm_back(ac_ref[...], gt, vec_ref[2:3, :])
    count(2, gain)
    count(5, shift)
    ga = og_ref[...].astype(F32) + back
    gal = ga.astype(BF16)
    count(11, jnp.sum(gal.astype(F32), axis=0, keepdims=True))
    ca = ca_ref[...]
    co_acc[...] += tn(ca, gal)
    dca = nt(gal, co_ref[...]).astype(BF16)
    cq = cq_ref[...]
    dq = []
    for hp in range(6):
        ls = slice(hp * 128, hp * 128 + 128)
        qp, dp_ = cq[:, ls], dca[:, ls]
        dqt = None
        parts = []
        for e in range(2):
            h = hp * 2 + e
            p = jnp.exp2(nt(km_ref[h], qp) - lse_ref[h : h + 1, :])
            dp = nt(vm_ref[h], dp_)
            inner = jnp.sum(dp * p, axis=0, keepdims=True)
            ds = (p * (dp - inner)).astype(BF16)
            part = nn(kmt_ref[h], ds)
            dqt = part if dqt is None else dqt + part
            parts.append((nn(ds, qp), nn(p.astype(BF16), dp_)))
        dq.append(jnp.transpose(dqt))
        dk_ref[:, ls] += jnp.where(masks[0], parts[0][0], parts[1][0])
        dv_ref[:, ls] += jnp.where(masks[0], parts[0][1], parts[1][1])
    dcq = (jnp.concatenate(dq, axis=1) * HEAD ** (-0.5)).astype(BF16)
    count(9, jnp.sum(dcq.astype(F32), axis=0, keepdims=True))
    cq_acc[...] += tn(n2_ref[...], dcq)
    gs = nt(dcq, ci_ref[0])
    back, gain, shift = norm_back(mid_ref[...], gs, vec_ref[1:2, :])
    count(1, gain)
    count(4, shift)
    gm = ga + back
    gm_ref[...] = gm
    gml = gm.astype(BF16)
    count(8, jnp.sum(gml.astype(F32), axis=0, keepdims=True))
    for k, (o, do) in enumerate(zip((o0, o1, o2, o3), (do0, do1, do2, do3))):
        at = pl.ds(pl.multiple_of((hset ^ k) * 192, 64), 192)
        do[...] = nt(gml, so_ref[at, :]).astype(BF16)
        so_acc[at, :] += tn(o[...], gml)

    @pl.when(step == last)
    def _():
        dk = (dk_ref[...] * LN2).astype(BF16)
        dv = dv_ref[...].astype(BF16)
        count(10, jnp.sum(dv.astype(F32), axis=0, keepdims=True))
        fr = fr_ref[...]
        sog_ref[...] = so_acc[...].astype(BF16)
        cog_ref[...] = co_acc[...].astype(BF16)
        cig_ref[0] = cq_acc[...].astype(BF16)
        cig_ref[1] = tn(fr, dk).astype(BF16)
        cig_ref[2] = tn(fr, dv).astype(BF16)
        eg_ref[...] = (nt(dk, ci_ref[1]) + nt(dv, ci_ref[2])).astype(BF16)


def mid_back_call(meta, gt, og, ac, mid, n2, cq, ca, lse, kc, vc, frames, so, ci, co, vecs, pieces):
    rows, width = gt.shape
    tile = 256
    nf = frames.shape[0]
    row = pl.BlockSpec((tile, width), lambda i, m: (i, 0))
    row4 = pl.BlockSpec((tile, 192), lambda i, m: (i, 0))
    sds = jax.ShapeDtypeStruct
    acc = pltpu.VMEM((width, width), F32)
    return pl.pallas_call(
        mid_back_kernel,
        grid_spec=pltpu.PrefetchScalarGridSpec(
            num_scalar_prefetch=1,
            grid=(rows // tile,),
            in_specs=[row] * 7
            + [pl.BlockSpec((16, tile), lambda i, m: (0, i))]
            + [whole(v.shape) for v in (kc, vc, frames, so, ci, co, vecs)]
            + [row4] * 4,
            out_specs=[row] + [row4] * 4
            + [whole((width, width)), whole((3, width, width)), whole((width, width)), whole((nf, width)), whole((24, width))],
            scratch_shapes=[
                pltpu.VMEM((12, nf, 128), BF16), pltpu.VMEM((12, 128, nf), BF16), pltpu.VMEM((12, nf, 128), BF16),
                pltpu.VMEM((nf, width), F32), pltpu.VMEM((nf, width), F32), acc, acc, acc,
            ],
        ),
        out_shape=[sds((rows, width), F32)] + [sds((rows, 192), BF16)] * 4
        + [sds((width, width), BF16), sds((3, width, width), BF16), sds((width, width), BF16), sds((nf, width), BF16), sds((24, width), F32)],
        compiler_params=params(dimension_semantics=("arbitrary",)),
        cost_estimate=cost(22e9, 35e6, 3e6),
        name="middle_back",
    )(meta, gt, og, ac, mid, n2, cq, ca, lse, kc, vc, frames, so, ci, co, vecs, *pieces)


def first_back_kernel(a_ref, b_ref, c_ref, gm_ref, tok_ref, vec_ref, out_ref, sums_ref):
    @pl.when(pl.program_id(0) == 0)
    def _():
        sums_ref[...] = jnp.zeros_like(sums_ref)

    e = a_ref[...].astype(F32) + b_ref[...].astype(F32) + c_ref[...].astype(F32)
    back, gain, shift = norm_back(tok_ref[...].astype(F32), e, vec_ref[0:1, :])
    sums_ref[0:1, :] += gain
    sums_ref[1:2, :] += shift
    out_ref[...] = (gm_ref[...] + back).astype(BF16)


def first_back_call(a, b, c, gm, tok, vecs, part):
    width = a.shape[1]
    base = part * 2
    row = pl.BlockSpec((256, width), lambda i: (i, 0))
    off = pl.BlockSpec((256, width), lambda i: (i + base, 0))
    return pl.pallas_call(
        first_back_kernel,
        grid=(2,),
        in_specs=[off, off, row, off, off, whole(vecs.shape)],
        out_specs=[row, whole((8, width))],
        out_shape=[jax.ShapeDtypeStruct((512, width), BF16), jax.ShapeDtypeStruct((8, width), F32)],
        compiler_params=params(dimension_semantics=("arbitrary",)),
        cost_estimate=cost(1e7, 6e6),
        name="first_back%d" % part,
    )(a, b, c, gm, tok, vecs)


def device_pairs(dp_count, move, back=False):
    pairs = []
    for dp in range(dp_count):
        for seq in range(8):
            y, c, z, x = move(dp // 2, dp % 2, seq // 2, seq % 2)
            pair = (dp * 8 + seq, (y * 2 + c) * 8 + z * 2 + x)
            pairs.append(pair[::-1] if back else pair)
    return pairs


def home_body(
    tokens, encoder_states, out_grad, block_map, branch_fork, norm_gain, norm_bias, self_in,
    self_out, self_bias, cross_in, cross_out, cross_bias, up_weight, up_bias, down_weight, down_bias,
):
    dp_count = lax.axis_size("dp")
    dp, seq = lax.axis_index("dp"), lax.axis_index("seq")
    c, z, x = dp & 1, seq >> 1, seq & 1
    y = dp >> 1
    flat = dp * 8 + seq
    hset = 2 * c + x
    parity = z & 1
    rows, width = tokens.shape[1:]
    frames = encoder_states.shape[1]

    def send(v, move, back=False):
        return lax.ppermute(v, AXES, device_pairs(dp_count, move, back))

    def flip(k):
        return lambda y, c, z, x: (y, c ^ (k >> 1), z, x ^ (k & 1))

    def home(p):
        return lambda y, c, z, x: (y, z >> 1, 2 * c + (p ^ (z & 1)), x)

    def pick(v, p):
        return jnp.where(parity == p, v[0], v[1])

    def piece(v, parts):
        return v.reshape(parts, -1).astype(BF16)

    small = jnp.concatenate(
        [v.reshape(-1) for v in (norm_gain, norm_bias, self_bias, cross_bias, down_bias, up_bias)]
    )
    small = jnp.pad(small, (0, 8 * 192 - small.shape[0])).reshape(8, 192)
    shard = self_in.reshape(-1, width)
    options = jnp.stack(
        [jnp.concatenate([shard[:, 192 * j : 192 * j + 192], small]) for j in range(4)]
    )

    def merge(own, other, bit):
        return jnp.stack([jnp.where(bit == 0, own, other), jnp.where(bit == 0, other, own)])

    def option(k):
        return lax.dynamic_index_in_dim(options, hset ^ k, 0, False)

    got = [option(0)] + [send(option(k), flip(k)) for k in (1, 2, 3)]
    tree = merge(merge(got[0], got[1], x), merge(got[2], got[3], x), c)
    for bit in range((dp_count // 2).bit_length() - 1):
        tree = merge(
            tree, send(tree, lambda y, c, z, x, bit=bit: (y ^ (1 << bit), c, z, x)), (y >> bit) & 1
        )
    both = jnp.concatenate([tokens, encoder_states], axis=1)
    mine = [send(pick(both, p), home(p)) for p in range(2)]
    tree, mine[0] = lax.optimization_barrier((tree, mine[0]))
    across = [send(v, flip(1)) for v in mine]
    near = [send(v, flip(2)) for v in mine]
    tree = merge(tree, send(tree, lambda y, c, z, x: (y, c, z ^ 2, x)), z >> 1)
    tree = merge(tree, send(tree, lambda y, c, z, x: (y, c, z ^ 1, x)), z & 1)
    y_count = dp_count // 2
    nw = shard.shape[0] // 3
    tree = tree.reshape(2, 2, y_count, 2, 2, 3 * nw + 8, 192).transpose(2, 3, 1, 0, 4, 5, 6)
    tree = tree.reshape(dp_count * 8, 3 * nw + 8, 192)
    w2 = jnp.concatenate(
        [tree[:, t * nw : (t + 1) * nw].reshape(width, 192) for t in range(3)], axis=1
    )
    flats = tree[:, 3 * nw :].reshape(dp_count * 8, -1)
    lists = [
        flats[:, i * nw : (i + 1) * nw].reshape(1, width) for i in range(13)
    ]
    tiles = up_weight.shape[1] // width
    ub4 = flats[:, 13 * nw : (13 + tiles) * nw].reshape(tiles, width).astype(F32)
    vecs = jnp.concatenate(lists + [jnp.zeros((3, width), BF16)]).astype(F32)
    own_cols = lambda v: lax.dynamic_slice_in_dim(v, hset * 192, 192, 1)
    zero_row = jnp.zeros((1, 192), F32)
    qkv_bias = jnp.concatenate([own_cols(vecs[6:7]), zero_row, own_cols(vecs[7:8])], axis=1)

    info = jnp.concatenate([block_map, branch_fork], axis=1)
    info = jnp.where((z >> 1) == c, info, send(info, flip(2)))
    info = jnp.where(parity == 0, info[0], info[1])
    place = jnp.arange(32, dtype=jnp.int32)
    k_of, p_of = place >> 3, (place >> 2) & 1
    stored = (2 * (2 * (c ^ (k_of >> 1)) + (p_of ^ parity)) + (x ^ (k_of & 1))) * 4 + (place & 3)
    logical = jnp.sum(jnp.where(stored[:, None] == place[None, :], info[None, :32], 0), axis=1)
    spot = jnp.sum(jnp.where(logical[None, :] == place[:, None], place[None, :], 0), axis=1)
    meta = jnp.concatenate(
        [logical, spot, info[32:40], jnp.full((56,), hset, jnp.int32)]
    ).astype(jnp.int32)

    dense = jnp.concatenate(
        [down_weight]
        + [up_weight[:, j * width : (j + 1) * width] for j in range(tiles)]
        + [self_out, cross_in[0], cross_in[1], cross_in[2], cross_out]
    )
    dense, w2, *across = lax.optimization_barrier((dense, w2, *across))
    dense = lax.all_gather(dense, AXES, axis=0)
    far = [send(v, flip(2)) for v in across]
    out_grad, far[1] = lax.optimization_barrier((out_grad, far[1]))
    pieces = mine + across + near + far
    nd = down_weight.shape[0]

    def gathered(i):
        at = nd + i * nw
        return dense[:, at : at + nw].reshape(width, width)

    dn4 = dense[:, :nd].reshape(tiles, width, width)
    up4 = jnp.stack([gathered(j) for j in range(tiles)])
    so = gathered(tiles)
    ci = jnp.stack([gathered(tiles + 1 + t) for t in range(3)])
    co = gathered(tiles + 4)

    q, kv, tr, n1 = qkv_call(meta, pieces, w2, vecs, qkv_bias)
    og = jnp.concatenate([send(pick(out_grad, p), home(p)) for p in range(2)])
    tok = jnp.concatenate([v[:rows] for v in mine])
    all_frames = jnp.concatenate([v[rows:] for v in pieces])

    o, lse = attend_call(meta, q, kv, tr)
    o4 = o.reshape(4, 1024, 192)
    o_home = [o4[0]] + [send(o4[k], flip(k)) for k in (1, 2, 3)]
    mid, ac, n2, n3, cq, ca, lse_c, kc, vc = mid_call(
        meta, tok, o_home, so, ci, co, all_frames, vecs
    )
    res, gt, ug, dg, ubg, dbg = feed_call(n3, og, ac, up4, dn4, ub4, vecs)
    gm, d0, d1, d2, d3, sog, cig, cog, eg, sums = mid_back_call(
        meta, gt, og, ac, mid, n2, cq, ca, lse_c, kc, vc, all_frames, so, ci, co, vecs, o_home
    )
    d_home = [d0] + [send(d, flip(k)) for k, d in ((1, d1), (2, d2), (3, d3))]

    def rows_of(grad):
        return grad.reshape(dp_count * 8, -1, width)

    packed = jnp.concatenate(
        [rows_of(dg)] + [rows_of(ug[j]) for j in range(tiles)]
        + [rows_of(sog), rows_of(cig[0]), rows_of(cig[1]), rows_of(cig[2]), rows_of(cog)],
        axis=1,
    )
    packed, *d_home = lax.optimization_barrier((packed, *d_home))
    dense_grad = lax.psum_scatter(packed, AXES, scatter_dimension=0, tiled=True)[0].astype(F32)

    results = [send(res[p * rows : (p + 1) * rows], home(p), True) for p in range(2)]
    eg4 = eg.reshape(4, 2 * frames, width)
    eg_near = send(eg4[2:4], flip(2)).astype(F32)
    eg_side = (eg4[1].astype(F32) + eg_near[1]).astype(BF16)
    eg_sum = eg4[0].astype(F32) + eg_near[0] + send(eg_side, flip(1)).astype(F32)
    eg_sum = eg_sum.astype(BF16)
    eg_back = [send(eg_sum[p * frames : (p + 1) * frames], home(p), True) for p in range(2)]

    dqkv, dx0, dx1, dx2, dx3 = attend_back_call(meta, q, kv, tr, o, lse, d_home, w2)
    dx3, results[0], results[1], eg_back[0], eg_back[1] = lax.optimization_barrier(
        (dx3, *results, *eg_back)
    )
    near3 = send(dx3, flip(2))
    side = (dx1.astype(F32) + near3.astype(F32)).astype(BF16)
    side_parts = [side[p * rows : (p + 1) * rows] for p in range(2)]
    side = [send(v, flip(1)) for v in side_parts]
    near2 = send(dx2, flip(2))
    n1, near3 = lax.optimization_barrier((n1, near3))

    wg, colsum = win_call(n1, dqkv)
    wg = wg.reshape(y_count, 2, 4, 2, nw, 576)

    def halve(v, move, bit, axis):
        keep = lax.dynamic_index_in_dim(v, bit, axis, False)
        give = lax.dynamic_index_in_dim(v, 1 - bit, axis, False)
        return (keep.astype(F32) + send(give, move).astype(F32)).astype(BF16)

    for bit in reversed(range((dp_count // 2).bit_length() - 1)):
        half = wg.shape[0] // 2
        wg = halve(
            wg.reshape((2, half) + wg.shape[1:]),
            lambda y, c, z, x, bit=bit: (y ^ (1 << bit), c, z, x), (y >> bit) & 1, 0,
        )
    wg = wg.reshape(2, 2, 2, 2, nw, 576)
    wg = halve(wg, lambda y, c, z, x: (y, c, z ^ 1, x), z & 1, 2)

    first = [first_back_call(dx0, near2, side[p], gm, tok, vecs, p) for p in range(2)]
    grads = [v[0] for v in first]
    first_sums = first[0][1] + first[1][1]
    wg, grads[0] = lax.optimization_barrier((wg, grads[0]))
    grads = [send(v, home(p), True) for p, v in enumerate(grads)]
    wg = halve(wg, lambda y, c, z, x: (y, c, z ^ 2, x), z >> 1, 1)
    wg = wg.reshape(4, nw, 576)

    def shard_for(k):
        return lax.dynamic_index_in_dim(wg, hset ^ k, 0, False)

    parts = jnp.stack([shard_for(0)] + [send(shard_for(k), flip(k)) for k in (1, 2, 3)])
    cols = [lax.dynamic_index_in_dim(parts, hset ^ j, 0, False) for j in range(4)]
    self_in_grad = jnp.stack(
        [jnp.concatenate([v[:, 192 * t : 192 * t + 192] for v in cols], axis=1) for t in range(3)]
    ).astype(F32)

    def returned(pair, dtype):
        pair = [v.astype(dtype) for v in pair]
        return jnp.stack([jnp.where(parity == 0, pair[0], pair[1]), jnp.where(parity == 0, pair[1], pair[0])])

    own_bias = lambda v: lax.dynamic_update_slice(
        jnp.zeros((1, width), F32), v, (0, hset * 192)
    )
    ubg = ubg.reshape(tiles, 8, width)[:, 0]
    def over_all(table):
        for k in (1, 2):
            table = table + send(table, flip(k))
        table = table + send(table, lambda y, c, z, x: (y, c, z ^ 1, x))
        table = table + send(table, lambda y, c, z, x: (y, c, z ^ 2, x))
        for bit in range((dp_count // 2).bit_length() - 1):
            table = table + send(table, lambda y, c, z, x, bit=bit: (y ^ (1 << bit), c, z, x))
        return table

    table = jnp.concatenate(
        [
            sums[1:3], sums[4:6], sums[8:12],
            own_bias(colsum[0:1, 0:192]), own_bias(colsum[0:1, 384:576]),
            dbg[0:1], ubg, jnp.zeros((16 - 11 - tiles, width), F32),
        ]
    )
    table = over_all(table)
    first_table = over_all(first_sums)
    table = jnp.concatenate(
        [
            first_table[0:1], table[0:2], first_table[1:2], table[2:4],
            table[8:10], table[4:8], table[10 : 11 + tiles],
        ]
    )
    mine_of = lambda v: lax.dynamic_slice_in_dim(v, flat * nw, nw, 1)
    vec_grad = mine_of(table[:13])
    up_bias_grad = lax.dynamic_slice_in_dim(
        table[13 : 13 + tiles].reshape(-1), flat * tiles * nw, tiles * nw, 0
    )

    def shard_grad(i):
        at = nd + i * nw
        return dense_grad[at : at + nw]

    return (
        returned(results, BF16),
        returned(grads, F32),
        returned(eg_back, F32),
        vec_grad[0:3],
        vec_grad[3:6],
        self_in_grad,
        shard_grad(tiles),
        vec_grad[6:9],
        jnp.stack([shard_grad(tiles + 1 + t) for t in range(3)]),
        shard_grad(tiles + 4),
        vec_grad[9:12],
        jnp.concatenate([shard_grad(j) for j in range(tiles)], axis=1),
        up_bias_grad,
        dense_grad[:nd],
        vec_grad[12],
    )


def solution(mesh):
    in_specs = (
        P("dp", "seq", None),
        P("dp", "seq", None),
        P("dp", "seq", None),
        P("dp", None),
        P("dp", None),
        P(None, ("dp", "seq")),
        P(None, ("dp", "seq")),
        P(None, ("dp", "seq"), None),
        P(("dp", "seq"), None),
        P(None, ("dp", "seq")),
        P(None, ("dp", "seq"), None),
        P(("dp", "seq"), None),
        P(None, ("dp", "seq")),
        P(("dp", "seq"), None),
        P(("dp", "seq")),
        P(("dp", "seq"), None),
        P(("dp", "seq")),
    )
    out_specs = (
        P("dp", "seq", None),
        P("dp", "seq", None),
        P("dp", "seq", None),
        P(None, ("dp", "seq")),
        P(None, ("dp", "seq")),
        P(None, ("dp", "seq"), None),
        P(("dp", "seq"), None),
        P(None, ("dp", "seq")),
        P(None, ("dp", "seq"), None),
        P(("dp", "seq"), None),
        P(None, ("dp", "seq")),
        P(("dp", "seq"), None),
        P(("dp", "seq")),
        P(("dp", "seq"), None),
        P(("dp", "seq")),
    )
    sizes = dict(mesh.shape)
    chosen = home_body if sizes["dp"] == 4 and sizes["seq"] == 8 else body
    return jax.shard_map(chosen, mesh=mesh, in_specs=in_specs, out_specs=out_specs, check_vma=False)
```

```python
import functools

import jax
import jax.numpy as jnp
from jax import lax
from jax.experimental import pallas as pl
from jax.experimental.pallas import tpu as pltpu
from jax.sharding import PartitionSpec as P

HEADS = 12
HEAD = 64
PROMPT = 2048
BRANCHES = 8
BLEN = 256
BLOCK = 128


def product(former, latter):
    return jnp.dot(former, latter, preferred_element_type=jnp.float32)


def product_left(former, latter):
    return lax.dot_general(
        former, latter, (((0,), (0,)), ((), ())), preferred_element_type=jnp.float32
    )


def product_right(former, latter):
    return lax.dot_general(
        former, latter, (((1,), (1,)), ((), ())), preferred_element_type=jnp.float32
    )


def column_sum(matrix):
    return jnp.sum(matrix.astype(jnp.float32), axis=0)


def norm_layer(stream, norm_gain, norm_shift):
    center = jnp.mean(stream, axis=-1, keepdims=True)
    centered = stream - center
    spread = jnp.mean(centered * centered, axis=-1, keepdims=True)
    return centered * lax.rsqrt(spread + 1e-05) * norm_gain + norm_shift


def gelu_exact(before):
    return jax.nn.gelu(before, approximate=False)


def token_info(blocks, branch_forks):
    offsets = jnp.arange(BLOCK, dtype=jnp.int32)
    logical = (blocks[:, None] * BLOCK + offsets[None, :]).reshape(-1)
    relative = logical - PROMPT
    in_branch = relative >= 0
    segment = jnp.where(in_branch, relative // BLEN + 1, 0)
    position = jnp.where(in_branch, relative % BLEN, logical)
    labels = jnp.arange(1, BRANCHES + 1, dtype=jnp.int32)
    fork_reach = jnp.sum(
        jnp.where(segment[:, None] == labels[None, :], branch_forks[None, :], 0), axis=1
    )
    return (segment, position, fork_reach)


def allowed(query_info, key_info):
    same = (query_info[0][:, None] == key_info[0][None, :]) & (
        key_info[1][None, :] <= query_info[1][:, None]
    )
    shared = (
        (query_info[0][:, None] > 0)
        & (key_info[0][None, :] == 0)
        & (key_info[1][None, :] < query_info[2][:, None])
    )
    return same | shared


def head_split(matrix):
    return matrix.reshape(matrix.shape[0], HEADS, HEAD)


def score_block(queries, key_rows, key_mask):
    scores = jnp.einsum(
        "rhd,khd->hrk",
        head_split(queries),
        head_split(key_rows),
        preferred_element_type=jnp.float32,
    ) * HEAD ** (-0.5)
    if key_mask is None:
        return scores
    return jnp.where(key_mask[None], scores, -1e30)


def attend_forward(queries, key_rows, value_rows, key_mask):
    scores = score_block(queries, key_rows, key_mask)
    row_max = jnp.max(scores, axis=2, keepdims=True)
    weights = jnp.exp(scores - row_max)
    row_total = jnp.sum(weights, axis=2, keepdims=True)
    shares = (weights / row_total).astype(jnp.bfloat16)
    attended = jnp.einsum(
        "hrk,khd->rhd", shares, head_split(value_rows), preferred_element_type=jnp.float32
    )
    return (attended.reshape(queries.shape[0], -1).astype(jnp.bfloat16), row_max, row_total)


def attend_backward(queries, key_rows, value_rows, key_mask, row_max, row_total, incoming):
    scores = score_block(queries, key_rows, key_mask)
    shares_full = jnp.exp(scores - row_max) / row_total
    shares_low = shares_full.astype(jnp.bfloat16)
    grad_heads = head_split(incoming)
    grad_values = jnp.einsum(
        "hrk,rhd->khd", shares_low, grad_heads, preferred_element_type=jnp.float32
    )
    grad_shares = jnp.einsum(
        "rhd,khd->hrk", grad_heads, head_split(value_rows), preferred_element_type=jnp.float32
    )
    inner_sum = jnp.sum(grad_shares * shares_full, axis=2, keepdims=True)
    grad_scores = (shares_full * (grad_shares - inner_sum)).astype(jnp.bfloat16)
    grad_queries = jnp.einsum(
        "hrk,khd->rhd", grad_scores, head_split(key_rows), preferred_element_type=jnp.float32
    ) * HEAD ** (-0.5)
    grad_keys = jnp.einsum(
        "hrk,rhd->khd", grad_scores, head_split(queries), preferred_element_type=jnp.float32
    ) * HEAD ** (-0.5)
    row_count = queries.shape[0]
    key_count = key_rows.shape[0]
    return (
        grad_queries.reshape(row_count, -1),
        grad_keys.reshape(key_count, -1),
        grad_values.reshape(key_count, -1),
    )


def fetch_self(shards):
    return (
        lax.all_gather(shards[0][0], ("dp", "seq"), axis=0, tiled=True),
        lax.all_gather(shards[1][0], ("dp", "seq"), axis=0, tiled=True),
        lax.all_gather(shards[2], ("dp", "seq"), axis=1, tiled=True),
        lax.all_gather(shards[3], ("dp", "seq"), axis=0, tiled=True),
        lax.all_gather(shards[4], ("dp", "seq"), axis=1, tiled=True),
    )


def fetch_cross(shards):
    return (
        lax.all_gather(shards[0][1], ("dp", "seq"), axis=0, tiled=True),
        lax.all_gather(shards[1][1], ("dp", "seq"), axis=0, tiled=True),
        lax.all_gather(shards[5], ("dp", "seq"), axis=1, tiled=True),
        lax.all_gather(shards[6], ("dp", "seq"), axis=0, tiled=True),
        lax.all_gather(shards[7], ("dp", "seq"), axis=1, tiled=True),
    )


def fetch_feed(shards):
    return (
        lax.all_gather(shards[0][2], ("dp", "seq"), axis=0, tiled=True),
        lax.all_gather(shards[1][2], ("dp", "seq"), axis=0, tiled=True),
        lax.all_gather(shards[8], ("dp", "seq"), axis=0, tiled=True),
        lax.all_gather(shards[9], ("dp", "seq"), axis=0, tiled=True),
        lax.all_gather(shards[10], ("dp", "seq"), axis=0, tiled=True),
        lax.all_gather(shards[11], ("dp", "seq"), axis=0, tiled=True),
    )


def body(
    tokens,
    encoder_states,
    out_grad,
    block_map,
    branch_fork,
    norm_gain,
    norm_bias,
    self_in,
    self_out,
    self_bias,
    cross_in,
    cross_out,
    cross_bias,
    up_weight,
    up_bias,
    down_weight,
    down_bias,
):
    shards = (
        norm_gain,
        norm_bias,
        self_in,
        self_out,
        self_bias,
        cross_in,
        cross_out,
        cross_bias,
        up_weight,
        up_bias,
        down_weight,
        down_bias,
    )
    model_width = tokens.shape[2]
    hidden_width = up_weight.shape[1]
    seq_count = lax.axis_size("seq")
    seq_place = lax.axis_index("seq")

    def micro_step(grad_sums, inputs):
        tokens_in, encoded, cotangent, blocks, branch_forks = inputs
        slot_count = blocks.shape[0] // seq_count
        own_blocks = lax.dynamic_slice_in_dim(blocks, seq_place * slot_count, slot_count)
        query_info = token_info(own_blocks, branch_forks)
        full_info = token_info(blocks, branch_forks)
        key_mask = allowed(query_info, full_info)
        gain_first, shift_first, attend_in, attend_out, attend_bias = fetch_self(shards)
        stream = tokens_in.astype(jnp.float32)
        norm_full, pull_first = jax.vjp(
            norm_layer, stream, gain_first.astype(jnp.float32), shift_first.astype(jnp.float32)
        )
        norm_first = norm_full.astype(jnp.bfloat16)
        queries = (product(norm_first, attend_in[0]) + attend_bias[0].astype(jnp.float32)).astype(
            jnp.bfloat16
        )
        key_local = product(norm_first, attend_in[1]).astype(jnp.bfloat16)
        value_local = (
            product(norm_first, attend_in[2]) + attend_bias[1].astype(jnp.float32)
        ).astype(jnp.bfloat16)
        key_rows, value_rows = (
            lax.all_gather(key_local, "seq", axis=0, tiled=True),
            lax.all_gather(value_local, "seq", axis=0, tiled=True),
        )
        attended, self_max, self_total = attend_forward(queries, key_rows, value_rows, key_mask)
        middle = stream + product(attended, attend_out) + attend_bias[2].astype(jnp.float32)
        gain_second, shift_second, cross_proj, cross_back, cross_shift = fetch_cross(shards)
        cross_key_local = product(encoded, cross_proj[1]).astype(jnp.bfloat16)
        cross_value_local = (
            product(encoded, cross_proj[2]) + cross_shift[1].astype(jnp.float32)
        ).astype(jnp.bfloat16)
        cross_keys, cross_values = (
            lax.all_gather(cross_key_local, "seq", axis=0, tiled=True),
            lax.all_gather(cross_value_local, "seq", axis=0, tiled=True),
        )
        norm_full_second, pull_second = jax.vjp(
            norm_layer, middle, gain_second.astype(jnp.float32), shift_second.astype(jnp.float32)
        )
        norm_second = norm_full_second.astype(jnp.bfloat16)
        cross_queries = (
            product(norm_second, cross_proj[0]) + cross_shift[0].astype(jnp.float32)
        ).astype(jnp.bfloat16)
        cross_attended, cross_max, cross_total = attend_forward(
            cross_queries, cross_keys, cross_values, None
        )
        after_cross = (
            middle + product(cross_attended, cross_back) + cross_shift[2].astype(jnp.float32)
        )
        gain_third, shift_third, feed_up, feed_up_bias, feed_down, feed_down_bias = fetch_feed(
            shards
        )
        norm_full_third, pull_third = jax.vjp(
            norm_layer, after_cross, gain_third.astype(jnp.float32), shift_third.astype(jnp.float32)
        )
        norm_third = norm_full_third.astype(jnp.bfloat16)
        before = product(norm_third, feed_up) + feed_up_bias.astype(jnp.float32)
        activated_full, gelu_pull = jax.vjp(gelu_exact, before)
        activated = activated_full.astype(jnp.bfloat16)
        result = after_cross + product(activated, feed_down) + feed_down_bias.astype(jnp.float32)
        gain_third, shift_third, feed_up, feed_up_bias, feed_down, feed_down_bias = fetch_feed(
            shards
        )
        cot_float = cotangent.astype(jnp.float32)
        grad_act = product_right(cotangent, feed_down)
        grad_down = product_left(activated, cotangent)
        grad_down_bias = jnp.sum(cot_float, axis=0)
        grad_before = gelu_pull(grad_act)[0].astype(jnp.bfloat16)
        grad_up = product_left(norm_third, grad_before)
        grad_up_bias = column_sum(grad_before)
        grad_third = product_right(grad_before, feed_up)
        grad_after_norm, grad_gain_third, grad_shift_third = pull_third(grad_third)
        grad_after = cot_float + grad_after_norm
        gain_second, shift_second, cross_proj, cross_back, cross_shift = fetch_cross(shards)
        grad_after_low = grad_after.astype(jnp.bfloat16)
        grad_cross_back = product_left(cross_attended, grad_after_low)
        grad_cross_out_bias = column_sum(grad_after_low)
        grad_cross_attended = product_right(grad_after_low, cross_back).astype(jnp.bfloat16)
        grad_cross_queries, grad_cross_keys, grad_cross_values = attend_backward(
            cross_queries,
            cross_keys,
            cross_values,
            None,
            cross_max,
            cross_total,
            grad_cross_attended,
        )
        cross_key_part, cross_value_part = (
            lax.psum_scatter(
                grad_cross_keys.astype(jnp.bfloat16), "seq", scatter_dimension=0, tiled=True
            ).astype(jnp.float32),
            lax.psum_scatter(
                grad_cross_values.astype(jnp.bfloat16), "seq", scatter_dimension=0, tiled=True
            ).astype(jnp.float32),
        )
        cross_key_low = cross_key_part.astype(jnp.bfloat16)
        cross_value_low = cross_value_part.astype(jnp.bfloat16)
        cross_query_low = grad_cross_queries.astype(jnp.bfloat16)
        grad_cross_proj = jnp.stack(
            [
                product_left(norm_second, cross_query_low),
                product_left(encoded, cross_key_low),
                product_left(encoded, cross_value_low),
            ]
        )
        grad_cross_shift = jnp.stack(
            [column_sum(cross_query_low), column_sum(cross_value_low), grad_cross_out_bias]
        )
        encoder_grad = product_right(cross_key_low, cross_proj[1]) + product_right(
            cross_value_low, cross_proj[2]
        )
        grad_second = product_right(cross_query_low, cross_proj[0])
        grad_middle_norm, grad_gain_second, grad_shift_second = pull_second(grad_second)
        grad_middle = grad_after + grad_middle_norm
        gain_first, shift_first, attend_in, attend_out, attend_bias = fetch_self(shards)
        grad_middle_low = grad_middle.astype(jnp.bfloat16)
        grad_attend_out = product_left(attended, grad_middle_low)
        grad_out_bias = column_sum(grad_middle_low)
        grad_attended = product_right(grad_middle_low, attend_out).astype(jnp.bfloat16)
        grad_queries, grad_keys, grad_values = attend_backward(
            queries, key_rows, value_rows, key_mask, self_max, self_total, grad_attended
        )
        key_part, value_part = (
            lax.psum_scatter(
                grad_keys.astype(jnp.bfloat16), "seq", scatter_dimension=0, tiled=True
            ).astype(jnp.float32),
            lax.psum_scatter(
                grad_values.astype(jnp.bfloat16), "seq", scatter_dimension=0, tiled=True
            ).astype(jnp.float32),
        )
        key_low = key_part.astype(jnp.bfloat16)
        value_low = value_part.astype(jnp.bfloat16)
        query_low = grad_queries.astype(jnp.bfloat16)
        grad_attend_in = jnp.stack(
            [
                product_left(norm_first, query_low),
                product_left(norm_first, key_low),
                product_left(norm_first, value_low),
            ]
        )
        grad_attend_bias = jnp.stack([column_sum(query_low), column_sum(value_low), grad_out_bias])
        grad_first = (
            product_right(query_low, attend_in[0])
            + product_right(key_low, attend_in[1])
            + product_right(value_low, attend_in[2])
        )
        grad_stream_norm, grad_gain_first, grad_shift_first = pull_first(grad_first)
        tokens_grad = grad_middle + grad_stream_norm
        updates = (
            jnp.stack([grad_gain_first, grad_gain_second, grad_gain_third]),
            jnp.stack([grad_shift_first, grad_shift_second, grad_shift_third]),
            grad_attend_in,
            grad_attend_out,
            grad_attend_bias,
            grad_cross_proj,
            grad_cross_back,
            grad_cross_shift,
            grad_up,
            grad_up_bias,
            grad_down,
            grad_down_bias,
        )
        grad_sums = tuple((former + latter for former, latter in zip(grad_sums, updates)))
        return (grad_sums, (result.astype(jnp.bfloat16), tokens_grad, encoder_grad))

    starting = (
        jnp.zeros((3, model_width), jnp.float32),
        jnp.zeros((3, model_width), jnp.float32),
        jnp.zeros((3, model_width, model_width), jnp.float32),
        jnp.zeros((model_width, model_width), jnp.float32),
        jnp.zeros((3, model_width), jnp.float32),
        jnp.zeros((3, model_width, model_width), jnp.float32),
        jnp.zeros((model_width, model_width), jnp.float32),
        jnp.zeros((3, model_width), jnp.float32),
        jnp.zeros((model_width, hidden_width), jnp.float32),
        jnp.zeros((hidden_width,), jnp.float32),
        jnp.zeros((hidden_width, model_width), jnp.float32),
        jnp.zeros((model_width,), jnp.float32),
    )
    grad_sums, outputs = lax.scan(
        micro_step, starting, (tokens, encoder_states, out_grad, block_map, branch_fork)
    )
    feed_part = (
        lax.psum_scatter(grad_sums[8], ("dp", "seq"), scatter_dimension=0, tiled=True),
        lax.psum_scatter(grad_sums[9], ("dp", "seq"), scatter_dimension=0, tiled=True),
        lax.psum_scatter(grad_sums[10], ("dp", "seq"), scatter_dimension=0, tiled=True),
        lax.psum_scatter(grad_sums[11], ("dp", "seq"), scatter_dimension=0, tiled=True),
    )
    cross_part = (
        lax.psum_scatter(grad_sums[5], ("dp", "seq"), scatter_dimension=1, tiled=True),
        lax.psum_scatter(grad_sums[6], ("dp", "seq"), scatter_dimension=0, tiled=True),
        lax.psum_scatter(grad_sums[7], ("dp", "seq"), scatter_dimension=1, tiled=True),
    )
    self_part = (
        lax.psum_scatter(grad_sums[0], ("dp", "seq"), scatter_dimension=1, tiled=True),
        lax.psum_scatter(grad_sums[1], ("dp", "seq"), scatter_dimension=1, tiled=True),
        lax.psum_scatter(grad_sums[2], ("dp", "seq"), scatter_dimension=1, tiled=True),
        lax.psum_scatter(grad_sums[3], ("dp", "seq"), scatter_dimension=0, tiled=True),
        lax.psum_scatter(grad_sums[4], ("dp", "seq"), scatter_dimension=1, tiled=True),
    )
    return (
        outputs[0],
        outputs[1],
        outputs[2],
        self_part[0],
        self_part[1],
        self_part[2],
        self_part[3],
        self_part[4],
        cross_part[0],
        cross_part[1],
        cross_part[2],
        feed_part[0],
        feed_part[1],
        feed_part[2],
        feed_part[3],
    )


LOG2E = 1.4426950408889634
LN2 = 0.6931471805599453
QSCALE = HEAD ** (-0.5) * LOG2E
AXES = ("dp", "seq")
F32 = jnp.float32
BF16 = jnp.bfloat16
ANY = pl.BlockSpec(memory_space=pl.ANY)
SMEM = pl.BlockSpec(memory_space=pltpu.SMEM)


def nn(a, b):
    return lax.dot_general(a, b, (((1,), (0,)), ((), ())), preferred_element_type=F32)


def nt(a, b):
    return lax.dot_general(a, b, (((1,), (1,)), ((), ())), preferred_element_type=F32)


def tn(a, b):
    return lax.dot_general(a, b, (((0,), (0,)), ((), ())), preferred_element_type=F32)


def whole(shape):
    zeros = (0,) * len(shape)
    return pl.BlockSpec(shape, lambda *_: zeros)


def params(**kw):
    return pltpu.CompilerParams(vmem_limit_bytes=60 * 1024 * 1024, **kw)


def cost(flops, nbytes, trans=0):
    return pl.CostEstimate(flops=int(flops), bytes_accessed=int(nbytes), transcendentals=int(trans))


def stats(v):
    mean = jnp.mean(v, axis=-1, keepdims=True)
    centered = v - mean
    var = jnp.mean(centered * centered, axis=-1, keepdims=True)
    rstd = lax.rsqrt(var + 1e-05)
    return centered * rstd, rstd


def norm_back(v, e, gain):
    z, rstd = stats(v)
    f = e * gain
    grad = rstd * (
        f - jnp.mean(f, axis=-1, keepdims=True) - z * jnp.mean(f * z, axis=-1, keepdims=True)
    )
    return grad, jnp.sum(e * z, axis=0, keepdims=True), jnp.sum(e, axis=0, keepdims=True)


def qkv_kernel(meta, *refs):
    pieces = refs[:8]
    w_ref, vec_ref, bias_ref, q_ref, kv_ref, tr_ref, n1_ref, buf, sem = refs[8:]
    rows = buf.shape[0] // 8
    step = pl.program_id(0)

    @pl.when(step == 0)
    def _():
        copies = [
            pltpu.make_async_copy(pieces[i], buf.at[pl.ds(i * rows, rows), :], sem.at[i])
            for i in range(8)
        ]
        for c in copies:
            c.start()
        for c in copies:
            c.wait()

    gain, shift = vec_ref[0:1, :], vec_ref[3:4, :]
    w = w_ref[...]
    bias = bias_ref[0:1, :]
    for u in range(4):
        b = meta[32 + step * 4 + u]
        off = pl.multiple_of((b // 4) * rows + (b % 4) * 128, 32)
        x = buf[pl.ds(off, 128), :].astype(F32)
        z, _ = stats(x)
        n1 = (z * gain + shift).astype(BF16)
        r = slice(u * 128, (u + 1) * 128)
        n1_ref[r, :] = n1
        y = nn(n1, w) + bias
        kvt = jnp.transpose(y[:, 192:576]).astype(BF16)
        for t in range(2):
            for h in range(3):
                o = (t * 3 + h) * 64
                tr_ref[t * 3 + h, :, r] = kvt[o : o + 64, :]
        yq = (y[:, 0:192] * QSCALE).astype(BF16)
        yk = y[:, 192:576].astype(BF16)
        zero = jnp.zeros((128, 64), BF16)
        for h in range(3):
            q_ref[h, r, :] = jnp.concatenate([yq[:, h * 64 : h * 64 + 64], zero], axis=1)
            kv_ref[h, r, :] = jnp.concatenate(
                [yk[:, h * 64 : h * 64 + 64], yk[:, 192 + h * 64 : 256 + h * 64]], axis=1
            )


def qkv_call(meta, pieces, w2, vecs, bias):
    rows = pieces[0].shape[0]
    grid = (8,)
    return pl.pallas_call(
        qkv_kernel,
        grid_spec=pltpu.PrefetchScalarGridSpec(
            num_scalar_prefetch=1,
            grid=grid,
            in_specs=[ANY] * 8 + [whole(w2.shape), whole(vecs.shape), whole(bias.shape)],
            out_specs=[
                pl.BlockSpec((3, 512, 128), lambda i, m: (0, i, 0)),
                pl.BlockSpec((3, 512, 128), lambda i, m: (0, i, 0)),
                pl.BlockSpec((6, 64, 512), lambda i, m: (0, 0, i)),
                pl.BlockSpec((512, 768), lambda i, m: (i, 0)),
            ],
            scratch_shapes=[pltpu.VMEM((8 * rows, 768), BF16), pltpu.SemaphoreType.DMA((8,))],
        ),
        out_shape=[
            jax.ShapeDtypeStruct((3, 4096, 128), BF16),
            jax.ShapeDtypeStruct((3, 4096, 128), BF16),
            jax.ShapeDtypeStruct((6, 64, 4096), BF16),
            jax.ShapeDtypeStruct((4096, 768), BF16),
        ],
        compiler_params=params(dimension_semantics=("arbitrary",)),
        cost_estimate=cost(2 * 4096 * 768 * 576, 20e6),
        name="qkv",
    )(meta, *pieces, w2, vecs, bias)


def tile_plan(meta, qi):
    branch = qi >= 8
    fork = meta[64 + jnp.maximum(qi - 8, 0)]
    count = jnp.where(branch, (fork + 255) // 256, qi) + 1
    reach = jnp.where(branch, fork, 4096)

    def tile(t, own):
        if own:
            kt = qi
        else:
            kt = jnp.where(t == count - 1, qi, t)
        key = lax.broadcasted_iota(jnp.int32, (256, 256), 0)
        query = lax.broadcasted_iota(jnp.int32, (256, 256), 1)
        if own:
            mask = key <= query
        else:
            limit = jnp.where(t == count - 1, 0, jnp.minimum(reach - t * 256, 256) - 1)
            slope = jnp.where(t == count - 1, 1, 0)
            mask = key <= query[0:1, :] * slope + limit
        return pl.ds(pl.multiple_of(kt * 256, 256), 256), mask

    return count, tile


def tile_pairs(count, step):
    def pair(i, carry):
        step(i * 2, False)
        step(i * 2 + 1, False)
        return carry

    lax.fori_loop(0, count // 2, pair, 0)

    @pl.when(count % 2 == 1)
    def _():
        step(count - 1, True)


def attend_kernel(meta, q_ref, kv_ref, tr_ref, o_ref, lse_ref, m_ref, l_ref, acc_ref):
    def q_tile(qi, carry):
        count, tile = tile_plan(meta, qi)
        qs = pl.ds(pl.multiple_of(qi * 256, 256), 256)
        m_ref[...] = jnp.full_like(m_ref, -1e30)
        l_ref[...] = jnp.zeros_like(l_ref)
        acc_ref[...] = jnp.zeros_like(acc_ref)

        def k_tile(t, own):
            ks, mask = tile(t, own)
            s = [nt(kv_ref[h, ks, :], q_ref[h, qs, :]) for h in range(3)]
            s = [jnp.where(mask, v, -1e30) for v in s]
            old = [m_ref[h : h + 1, :] for h in range(3)]
            new = [jnp.maximum(old[h], jnp.max(s[h], axis=0, keepdims=True)) for h in range(3)]
            p = [jnp.exp2(s[h] - new[h]) for h in range(3)]
            out = [nn(tr_ref[3 + h, :, ks], p[h].astype(BF16)) for h in range(3)]
            for h in range(3):
                alpha = jnp.exp2(old[h] - new[h])
                m_ref[h : h + 1, :] = new[h]
                l_ref[h : h + 1, :] = l_ref[h : h + 1, :] * alpha + jnp.sum(p[h], axis=0, keepdims=True)
                hs = slice(h * 64, h * 64 + 64)
                acc_ref[hs, :] = acc_ref[hs, :] * alpha + out[h]

        tile_pairs(count, k_tile)
        for h in range(3):
            hs = slice(h * 64, h * 64 + 64)
            l = l_ref[h : h + 1, :]
            acc_ref[hs, :] = acc_ref[hs, :] * (1.0 / l)
            lse_ref[h : h + 1, qs] = m_ref[h : h + 1, :] + jnp.log2(l)
        out = jnp.transpose(acc_ref[...]).astype(BF16)
        for u in range(2):
            o_ref[meta[32 + qi * 2 + u]] = out[u * 128 : (u + 1) * 128, :]
        return carry

    lax.fori_loop(0, 16, q_tile, 0)


def attend_call(meta, q, kv, tr):
    return pl.pallas_call(
        attend_kernel,
        grid_spec=pltpu.PrefetchScalarGridSpec(
            num_scalar_prefetch=1,
            grid=(1,),
            in_specs=[whole(q.shape), whole(kv.shape), whole(tr.shape)],
            out_specs=[whole((32, 128, 192)), whole((8, 4096))],
            scratch_shapes=[
                pltpu.VMEM((8, 256), F32),
                pltpu.VMEM((8, 256), F32),
                pltpu.VMEM((192, 256), F32),
            ],
        ),
        out_shape=[
            jax.ShapeDtypeStruct((32, 128, 192), BF16),
            jax.ShapeDtypeStruct((8, 4096), F32),
        ],
        compiler_params=params(dimension_semantics=("arbitrary",)),
        cost_estimate=cost(20e9, 10e6, 20e6),
        name="attend",
    )(meta, q, kv, tr)


def attend_back_kernel(
    meta, q_ref, kv_ref, tr_ref, o_ref, lse_ref, d0, d1, d2, d3, w_ref,
    out_ref, x0, x1, x2, x3, do_ref, di_ref, dq_ref, acc_ref, wt_ref,
):
    pieces = (d0, d1, d2, d3)
    zero = jnp.zeros((128, 64), BF16)
    head = lax.broadcasted_iota(jnp.int32, (8, 192), 0) * 64
    lane = lax.broadcasted_iota(jnp.int32, (8, 192), 1)
    pick = jnp.where((lane >= head) & (lane < head + 64), 1.0, 0.0).astype(BF16)

    def arrange(kk, carry):
        rs = pl.ds(pl.multiple_of(kk * 128, 128), 128)
        for k in range(4):
            b = k * 8 + kk
            at = pl.ds(pl.multiple_of(meta[b] * 128, 128), 128)
            do = pieces[k][rs, :]
            prod = do.astype(F32) * o_ref[b].astype(F32)
            high = prod.astype(BF16)
            low = (prod - high.astype(F32)).astype(BF16)
            di_ref[:, at] = nt(pick, high) + nt(pick, low)
            for h in range(3):
                do_ref[h, at, :] = jnp.concatenate([zero, do[:, h * 64 : h * 64 + 64]], axis=1)
        return carry

    lax.fori_loop(0, 8, arrange, 0)
    acc_ref[...] = jnp.zeros_like(acc_ref)

    def q_tile(qi, carry):
        count, tile = tile_plan(meta, qi)
        qs = pl.ds(pl.multiple_of(qi * 256, 256), 256)
        dq_ref[...] = jnp.zeros_like(dq_ref)

        def k_tile(t, own):
            ks, mask = tile(t, own)
            q = [q_ref[h, qs, :] for h in range(3)]
            do = [do_ref[h, qs, :] for h in range(3)]
            kv = [kv_ref[h, ks, :] for h in range(3)]
            s = [nt(kv[h], q[h]) for h in range(3)]
            dp = [nt(kv[h], do[h]) for h in range(3)]
            p, ds = [], []
            for h in range(3):
                e = jnp.where(mask, jnp.exp2(s[h] - lse_ref[h : h + 1, qs]), 0.0)
                p.append(e.astype(BF16))
                ds.append((e * (dp[h] - di_ref[h : h + 1, qs])).astype(BF16))
            for h in range(3):
                acc_ref[h, ks, :] += nn(ds[h], q[h]) + nn(p[h], do[h])
                hs = slice(h * 64, h * 64 + 64)
                dq_ref[hs, :] += nn(tr_ref[h, :, ks], ds[h])

        tile_pairs(count, k_tile)
        out_ref[qs, 0:192] = (jnp.transpose(dq_ref[...]) * HEAD ** (-0.5)).astype(BF16)
        return carry

    lax.fori_loop(0, 16, q_tile, 0)

    def finish(t, carry):
        rs = pl.ds(pl.multiple_of(t * 256, 256), 256)
        a = [acc_ref[h, rs, :] for h in range(3)]
        dk = jnp.concatenate([v[:, 0:64] for v in a], axis=1) * LN2
        dv = jnp.concatenate([v[:, 64:128] for v in a], axis=1)
        out_ref[rs, 192:576] = jnp.concatenate([dk, dv], axis=1).astype(BF16)
        return carry

    lax.fori_loop(0, 16, finish, 0)
    wt = jnp.transpose(w_ref[...])
    wt_ref[...] = wt

    def spread(i, carry):
        rs = pl.ds(pl.multiple_of(i * 512, 512), 512)
        for k, x_ref in enumerate((x0, x1, x2, x3)):
            rows = [
                out_ref[pl.ds(pl.multiple_of(meta[k * 8 + i * 4 + u] * 128, 128), 128), :]
                for u in range(4)
            ]
            x_ref[rs, :] = nn(jnp.concatenate(rows, axis=0), wt_ref[...]).astype(BF16)
        return carry

    lax.fori_loop(0, 2, spread, 0)


def attend_back_call(meta, q, kv, tr, o, lse, pieces, w2):
    ins = [q, kv, tr, o, lse, *pieces, w2]
    return pl.pallas_call(
        attend_back_kernel,
        grid_spec=pltpu.PrefetchScalarGridSpec(
            num_scalar_prefetch=1,
            grid=(1,),
            in_specs=[whole(v.shape) for v in ins],
            out_specs=[whole((4096, 576))] + [whole((1024, 768))] * 4,
            scratch_shapes=[
                pltpu.VMEM((3, 4096, 128), BF16),
                pltpu.VMEM((8, 4096), F32),
                pltpu.VMEM((192, 256), F32),
                pltpu.VMEM((3, 4096, 128), F32),
                pltpu.VMEM((576, 768), BF16),
            ],
        ),
        out_shape=[jax.ShapeDtypeStruct((4096, 576), BF16)]
        + [jax.ShapeDtypeStruct((1024, 768), BF16)] * 4,
        compiler_params=params(dimension_semantics=("arbitrary",)),
        cost_estimate=cost(50e9, 15e6, 20e6),
        name="attend_back",
    )(meta, *ins)


def win_kernel(n_ref, d_ref, g_ref, s_ref, acc_ref):
    step = pl.program_id(0)

    @pl.when(step == 0)
    def _():
        acc_ref[...] = jnp.zeros_like(acc_ref)
        s_ref[...] = jnp.zeros_like(s_ref)

    d = d_ref[...]
    acc_ref[...] += tn(n_ref[...], d)
    s_ref[0:1, :] += jnp.sum(d.astype(F32), axis=0, keepdims=True)

    @pl.when(step == pl.num_programs(0) - 1)
    def _():
        g_ref[...] = acc_ref[...].astype(BF16)


def win_call(n1, dqkv):
    return pl.pallas_call(
        win_kernel,
        grid=(4,),
        in_specs=[
            pl.BlockSpec((1024, 768), lambda i: (i, 0)),
            pl.BlockSpec((1024, 576), lambda i: (i, 0)),
        ],
        out_specs=[whole((768, 576)), whole((8, 576))],
        out_shape=[
            jax.ShapeDtypeStruct((768, 576), BF16),
            jax.ShapeDtypeStruct((8, 576), F32),
        ],
        scratch_shapes=[pltpu.VMEM((768, 576), F32)],
        compiler_params=params(dimension_semantics=("arbitrary",)),
        cost_estimate=cost(2 * 4096 * 768 * 576, 12e6),
        name="win",
    )(n1, dqkv)


def head_masks(frames):
    lane = lax.broadcasted_iota(jnp.int32, (frames, 128), 1) < 64
    return lane, jnp.logical_not(lane)


def mid_kernel(
    meta, tok_ref, o0, o1, o2, o3, so_ref, ci_ref, co_ref, fr_ref, vec_ref,
    mid_ref, ac_ref, n2_ref, n3_ref, cq_ref, ca_ref, lse_ref, kc_ref, vc_ref,
    km_ref, vmt_ref,
):
    frames = fr_ref.shape[0]
    hset = meta[72]

    @pl.when(pl.program_id(0) == 0)
    def _():
        fr = fr_ref[...]
        kc = nn(fr, ci_ref[1]).astype(BF16)
        vc = (nn(fr, ci_ref[2]) + vec_ref[10:11, :]).astype(BF16)
        kc_ref[...] = kc
        vc_ref[...] = vc
        zero = jnp.zeros((frames, 128), BF16)
        masks = head_masks(frames)
        for hp in range(6):
            ls = slice(hp * 128, hp * 128 + 128)
            for e in range(2):
                km_ref[hp * 2 + e] = jnp.where(masks[e], kc[:, ls], zero)
                vmt_ref[hp * 2 + e] = jnp.transpose(
                    jnp.where(masks[e], vc[:, ls].astype(F32), 0.0)
                ).astype(BF16)

    acc = tok_ref[...].astype(F32) + vec_ref[8:9, :]
    for k, o in enumerate((o0, o1, o2, o3)):
        at = pl.ds(pl.multiple_of((hset ^ k) * 192, 64), 192)
        acc = acc + nn(o[...], so_ref[at, :])
    mid_ref[...] = acc
    z, _ = stats(acc)
    n2 = (z * vec_ref[1:2, :] + vec_ref[4:5, :]).astype(BF16)
    n2_ref[...] = n2
    cq = ((nn(n2, ci_ref[0]) + vec_ref[9:10, :]) * QSCALE).astype(BF16)
    cq_ref[...] = cq
    ca = []
    for first in range(0, 12, 4):
        heads = range(first, first + 4)
        s = [nt(km_ref[h], cq[:, (h // 2) * 128 : (h // 2) * 128 + 128]) for h in heads]
        m = [jnp.max(v, axis=0, keepdims=True) for v in s]
        p = [jnp.exp2(v - w) for v, w in zip(s, m)]
        part = [nn(vmt_ref[h], v.astype(BF16)) for h, v in zip(heads, p)]
        for i, h in enumerate(heads):
            l = jnp.sum(p[i], axis=0, keepdims=True)
            lse_ref[h : h + 1, :] = m[i] + jnp.log2(l)
            part[i] = part[i] * (1.0 / l)
        for i in (0, 2):
            ca.append(jnp.transpose(part[i] + part[i + 1]).astype(BF16))
    ca = jnp.concatenate(ca, axis=1)
    ca_ref[...] = ca
    ac = acc + nn(ca, co_ref[...]) + vec_ref[11:12, :]
    ac_ref[...] = ac
    z, _ = stats(ac)
    n3_ref[...] = (z * vec_ref[2:3, :] + vec_ref[5:6, :]).astype(BF16)


def mid_call(meta, tok, pieces, so, ci, co, frames, vecs):
    rows, width = tok.shape
    tile = 256
    nf = frames.shape[0]
    row = pl.BlockSpec((tile, width), lambda i, m: (i, 0))
    row4 = pl.BlockSpec((tile, 192), lambda i, m: (i, 0))
    sds = jax.ShapeDtypeStruct
    return pl.pallas_call(
        mid_kernel,
        grid_spec=pltpu.PrefetchScalarGridSpec(
            num_scalar_prefetch=1,
            grid=(rows // tile,),
            in_specs=[row] + [row4] * 4
            + [whole(so.shape), whole(ci.shape), whole(co.shape), whole(frames.shape), whole(vecs.shape)],
            out_specs=[row] * 6
            + [pl.BlockSpec((16, tile), lambda i, m: (0, i)), whole((nf, width)), whole((nf, width))],
            scratch_shapes=[pltpu.VMEM((12, nf, 128), BF16), pltpu.VMEM((12, 128, nf), BF16)],
        ),
        out_shape=[
            sds((rows, width), F32), sds((rows, width), F32), sds((rows, width), BF16),
            sds((rows, width), BF16), sds((rows, width), BF16), sds((rows, width), BF16),
            sds((16, rows), F32), sds((nf, width), BF16), sds((nf, width), BF16),
        ],
        compiler_params=params(dimension_semantics=("arbitrary",)),
        cost_estimate=cost(8e9, 25e6, 3e6),
        name="middle",
    )(meta, tok, *pieces, so, ci, co, frames, vecs)


def normal_parts(b):
    e = jnp.exp2(b * b * (-0.5 * LOG2E))
    a = jnp.abs(b) * 0.7071067811865476
    t = 1.0 / (1.0 + 0.3275911 * a)
    poly = t * (
        0.254829592 + t * (-0.284496736 + t * (1.421413741 + t * (-1.453152027 + t * 1.061405429)))
    )
    tail = 0.5 * poly * e
    return jnp.where(b < 0.0, tail, 1.0 - tail), e * 0.3989422804014327


def feed_kernel(
    n3_ref, og_ref, ac_ref, up_ref, dn_ref, ub_ref, vec_ref,
    res_ref, gt_ref, ug_ref, dg_ref, ubg_ref, dbg_ref,
    acc_ref, n3t_ref, act_ref, gb_ref,
):
    step = pl.program_id(0)
    rows, width = n3_ref.shape

    @pl.when(step == 0)
    def _():
        acc_ref[...] = ac_ref[...] + vec_ref[12:13, :]
        gt_ref[...] = jnp.zeros_like(gt_ref)
        dbg_ref[...] = jnp.zeros_like(dbg_ref)
        dbg_ref[0:1, :] = jnp.sum(og_ref[...].astype(F32), axis=0, keepdims=True)
        n3t_ref[...] = jnp.transpose(n3_ref[...])

    up = up_ref[...].reshape(width, width)
    dn = dn_ref[...].reshape(width, width)
    ub = ub_ref[pl.ds(step, 1), :]
    total = jnp.zeros((1, width), F32)
    for r in range(rows // 256):
        rs = slice(r * 256, (r + 1) * 256)
        n3 = n3_ref[rs, :]
        og = og_ref[rs, :]
        b = nn(n3, up) + ub
        cdf, pdf = normal_parts(b)
        act = (b * cdf).astype(BF16)
        gb = (nt(og, dn) * (cdf + b * pdf)).astype(BF16)
        act_ref[rs, :] = act
        gb_ref[rs, :] = gb
        total = total + jnp.sum(gb.astype(F32), axis=0, keepdims=True)
        acc_ref[rs, :] += nn(act, dn)
        gt_ref[rs, :] += nt(gb, up)
    ubg_ref[...] = jnp.broadcast_to(total, (8, width))
    ug_ref[...] = nn(n3t_ref[...], gb_ref[...]).astype(BF16).reshape(ug_ref.shape)
    dg_ref[...] = tn(act_ref[...], og_ref[...]).astype(BF16).reshape(dg_ref.shape)

    @pl.when(step == pl.num_programs(0) - 1)
    def _():
        res_ref[...] = acc_ref[...].astype(BF16)


def feed_call(n3, og, ac, up4, dn4, ub4, vecs):
    rows, width = n3.shape
    sds = jax.ShapeDtypeStruct
    tiles = up4.shape[0]
    tile = pl.BlockSpec((1, width, width), lambda i: (i, 0, 0))
    return pl.pallas_call(
        feed_kernel,
        grid=(tiles,),
        in_specs=[whole(n3.shape), whole(og.shape), whole(ac.shape), tile, tile, whole(ub4.shape), whole(vecs.shape)],
        out_specs=[
            whole((rows, width)), whole((rows, width)), tile, tile,
            pl.BlockSpec((8, width), lambda i: (i, 0)), whole((8, width)),
        ],
        out_shape=[
            sds((rows, width), BF16), sds((rows, width), F32),
            sds((tiles, width, width), BF16), sds((tiles, width, width), BF16),
            sds((tiles * 8, width), F32), sds((8, width), F32),
        ],
        scratch_shapes=[
            pltpu.VMEM((rows, width), F32), pltpu.VMEM((width, rows), BF16),
            pltpu.VMEM((rows, width), BF16), pltpu.VMEM((rows, width), BF16),
        ],
        compiler_params=params(dimension_semantics=("arbitrary",)),
        cost_estimate=cost(2 * 6 * rows * width * width * tiles, 35e6, 6e6),
        name="feed",
    )(n3, og, ac, up4, dn4, ub4, vecs)


def mid_back_kernel(
    meta, gt_ref, og_ref, ac_ref, mid_ref, n2_ref, cq_ref, ca_ref, lse_ref, kc_ref, vc_ref,
    fr_ref, so_ref, ci_ref, co_ref, vec_ref, o0, o1, o2, o3,
    gm_ref, do0, do1, do2, do3, sog_ref, cig_ref, cog_ref, eg_ref, sums_ref,
    km_ref, kmt_ref, vm_ref, dk_ref, dv_ref, so_acc, cq_acc, co_acc,
):
    frames = fr_ref.shape[0]
    hset = meta[72]
    step = pl.program_id(0)
    last = pl.num_programs(0) - 1
    masks = head_masks(frames)

    @pl.when(step == 0)
    def _():
        zero = jnp.zeros((frames, 128), BF16)
        for hp in range(6):
            ls = slice(hp * 128, hp * 128 + 128)
            k, v = kc_ref[:, ls], vc_ref[:, ls]
            for e in range(2):
                km_ref[hp * 2 + e] = jnp.where(masks[e], k, zero)
                vm_ref[hp * 2 + e] = jnp.where(masks[e], v, zero)
                kmt_ref[hp * 2 + e] = jnp.transpose(
                    jnp.where(masks[e], k.astype(F32), 0.0)
                ).astype(BF16)
        for ref in (dk_ref, dv_ref, so_acc, cq_acc, co_acc, sums_ref):
            ref[...] = jnp.zeros_like(ref)

    def count(row, value):
        sums_ref[row : row + 1, :] += value

    gt = gt_ref[...]
    back, gain, shift = norm_back(ac_ref[...], gt, vec_ref[2:3, :])
    count(2, gain)
    count(5, shift)
    ga = og_ref[...].astype(F32) + back
    gal = ga.astype(BF16)
    count(11, jnp.sum(gal.astype(F32), axis=0, keepdims=True))
    ca = ca_ref[...]
    co_acc[...] += tn(ca, gal)
    dca = nt(gal, co_ref[...]).astype(BF16)
    cq = cq_ref[...]
    dq = []
    for first in range(0, 12, 4):
        heads = range(first, first + 4)
        slices = [slice((h // 2) * 128, (h // 2) * 128 + 128) for h in heads]
        s = [nt(km_ref[h], cq[:, ls]) for h, ls in zip(heads, slices)]
        dp = [nt(vm_ref[h], dca[:, ls]) for h, ls in zip(heads, slices)]
        p = [jnp.exp2(v - lse_ref[h : h + 1, :]) for h, v in zip(heads, s)]
        ds = []
        for i in range(4):
            inner = jnp.sum(dp[i] * p[i], axis=0, keepdims=True)
            ds.append((p[i] * (dp[i] - inner)).astype(BF16))
        dqt = [nn(kmt_ref[h], v) for h, v in zip(heads, ds)]
        dk = [nn(v, cq[:, ls]) for v, ls in zip(ds, slices)]
        dv = [nn(v.astype(BF16), dca[:, ls]) for v, ls in zip(p, slices)]
        for i in (0, 2):
            dq.append(jnp.transpose(dqt[i] + dqt[i + 1]))
            dk_ref[:, slices[i]] += jnp.where(masks[0], dk[i], dk[i + 1])
            dv_ref[:, slices[i]] += jnp.where(masks[0], dv[i], dv[i + 1])
    dcq = (jnp.concatenate(dq, axis=1) * HEAD ** (-0.5)).astype(BF16)
    count(9, jnp.sum(dcq.astype(F32), axis=0, keepdims=True))
    cq_acc[...] += tn(n2_ref[...], dcq)
    gs = nt(dcq, ci_ref[0])
    back, gain, shift = norm_back(mid_ref[...], gs, vec_ref[1:2, :])
    count(1, gain)
    count(4, shift)
    gm = ga + back
    gm_ref[...] = gm
    gml = gm.astype(BF16)
    count(8, jnp.sum(gml.astype(F32), axis=0, keepdims=True))
    for k, (o, do) in enumerate(zip((o0, o1, o2, o3), (do0, do1, do2, do3))):
        at = pl.ds(pl.multiple_of((hset ^ k) * 192, 64), 192)
        do[...] = nt(gml, so_ref[at, :]).astype(BF16)
        so_acc[at, :] += tn(o[...], gml)

    @pl.when(step == last)
    def _():
        dk = (dk_ref[...] * LN2).astype(BF16)
        dv = dv_ref[...].astype(BF16)
        count(10, jnp.sum(dv.astype(F32), axis=0, keepdims=True))
        fr = fr_ref[...]
        sog_ref[...] = so_acc[...].astype(BF16)
        cog_ref[...] = co_acc[...].astype(BF16)
        cig_ref[0] = cq_acc[...].astype(BF16)
        cig_ref[1] = tn(fr, dk).astype(BF16)
        cig_ref[2] = tn(fr, dv).astype(BF16)
        eg_ref[...] = (nt(dk, ci_ref[1]) + nt(dv, ci_ref[2])).astype(BF16)


def mid_back_call(meta, gt, og, ac, mid, n2, cq, ca, lse, kc, vc, frames, so, ci, co, vecs, pieces):
    rows, width = gt.shape
    tile = 256
    nf = frames.shape[0]
    row = pl.BlockSpec((tile, width), lambda i, m: (i, 0))
    row4 = pl.BlockSpec((tile, 192), lambda i, m: (i, 0))
    sds = jax.ShapeDtypeStruct
    acc = pltpu.VMEM((width, width), F32)
    return pl.pallas_call(
        mid_back_kernel,
        grid_spec=pltpu.PrefetchScalarGridSpec(
            num_scalar_prefetch=1,
            grid=(rows // tile,),
            in_specs=[row] * 7
            + [pl.BlockSpec((16, tile), lambda i, m: (0, i))]
            + [whole(v.shape) for v in (kc, vc, frames, so, ci, co, vecs)]
            + [row4] * 4,
            out_specs=[row] + [row4] * 4
            + [whole((width, width)), whole((3, width, width)), whole((width, width)), whole((nf, width)), whole((24, width))],
            scratch_shapes=[
                pltpu.VMEM((12, nf, 128), BF16), pltpu.VMEM((12, 128, nf), BF16), pltpu.VMEM((12, nf, 128), BF16),
                pltpu.VMEM((nf, width), F32), pltpu.VMEM((nf, width), F32), acc, acc, acc,
            ],
        ),
        out_shape=[sds((rows, width), F32)] + [sds((rows, 192), BF16)] * 4
        + [sds((width, width), BF16), sds((3, width, width), BF16), sds((width, width), BF16), sds((nf, width), BF16), sds((24, width), F32)],
        compiler_params=params(dimension_semantics=("arbitrary",)),
        cost_estimate=cost(22e9, 35e6, 3e6),
        name="middle_back",
    )(meta, gt, og, ac, mid, n2, cq, ca, lse, kc, vc, frames, so, ci, co, vecs, *pieces)


def first_back_kernel(a_ref, b_ref, c_ref, gm_ref, tok_ref, vec_ref, out_ref, sums_ref):
    @pl.when(pl.program_id(0) == 0)
    def _():
        sums_ref[...] = jnp.zeros_like(sums_ref)

    e = a_ref[...].astype(F32) + b_ref[...].astype(F32) + c_ref[...].astype(F32)
    back, gain, shift = norm_back(tok_ref[...].astype(F32), e, vec_ref[0:1, :])
    sums_ref[0:1, :] += gain
    sums_ref[1:2, :] += shift
    out_ref[...] = (gm_ref[...] + back).astype(BF16)


def first_back_call(a, b, c, gm, tok, vecs, part):
    width = a.shape[1]
    base = part * 2
    row = pl.BlockSpec((256, width), lambda i: (i, 0))
    off = pl.BlockSpec((256, width), lambda i: (i + base, 0))
    return pl.pallas_call(
        first_back_kernel,
        grid=(2,),
        in_specs=[off, off, row, off, off, whole(vecs.shape)],
        out_specs=[row, whole((8, width))],
        out_shape=[jax.ShapeDtypeStruct((512, width), BF16), jax.ShapeDtypeStruct((8, width), F32)],
        compiler_params=params(dimension_semantics=("arbitrary",)),
        cost_estimate=cost(1e7, 6e6),
        name="first_back%d" % part,
    )(a, b, c, gm, tok, vecs)


def device_pairs(dp_count, move, back=False):
    pairs = []
    for dp in range(dp_count):
        for seq in range(8):
            y, c, z, x = move(dp // 2, dp % 2, seq // 2, seq % 2)
            pair = (dp * 8 + seq, (y * 2 + c) * 8 + z * 2 + x)
            pairs.append(pair[::-1] if back else pair)
    return pairs


def home_body(
    tokens, encoder_states, out_grad, block_map, branch_fork, norm_gain, norm_bias, self_in,
    self_out, self_bias, cross_in, cross_out, cross_bias, up_weight, up_bias, down_weight, down_bias,
):
    dp_count = lax.axis_size("dp")
    dp, seq = lax.axis_index("dp"), lax.axis_index("seq")
    c, z, x = dp & 1, seq >> 1, seq & 1
    y = dp >> 1
    flat = dp * 8 + seq
    hset = 2 * c + x
    parity = z & 1
    rows, width = tokens.shape[1:]
    frames = encoder_states.shape[1]

    def send(v, move, back=False):
        return lax.ppermute(v, AXES, device_pairs(dp_count, move, back))

    def flip(k):
        return lambda y, c, z, x: (y, c ^ (k >> 1), z, x ^ (k & 1))

    def home(p):
        return lambda y, c, z, x: (y, z >> 1, 2 * c + (p ^ (z & 1)), x)

    def pick(v, p):
        return jnp.where(parity == p, v[0], v[1])

    def piece(v, parts):
        return v.reshape(parts, -1).astype(BF16)

    small = jnp.concatenate(
        [v.reshape(-1) for v in (norm_gain, norm_bias, self_bias, cross_bias, down_bias, up_bias)]
    )
    small = jnp.pad(small, (0, 8 * 192 - small.shape[0])).reshape(8, 192)
    shard = self_in.reshape(-1, width)
    options = jnp.stack(
        [jnp.concatenate([shard[:, 192 * j : 192 * j + 192], small]) for j in range(4)]
    )

    def merge(own, other, bit):
        return jnp.stack([jnp.where(bit == 0, own, other), jnp.where(bit == 0, other, own)])

    def option(k):
        return lax.dynamic_index_in_dim(options, hset ^ k, 0, False)

    got = [option(0)] + [send(option(k), flip(k)) for k in (1, 2, 3)]
    tree = merge(merge(got[0], got[1], x), merge(got[2], got[3], x), c)
    for bit in range((dp_count // 2).bit_length() - 1):
        tree = merge(
            tree, send(tree, lambda y, c, z, x, bit=bit: (y ^ (1 << bit), c, z, x)), (y >> bit) & 1
        )
    both = jnp.concatenate([tokens, encoder_states], axis=1)
    mine = [send(pick(both, p), home(p)) for p in range(2)]
    tree, *mine = lax.optimization_barrier((tree, *mine))
    across = [send(v, flip(1)) for v in mine]
    near = [send(v, flip(2)) for v in mine]
    tree = merge(tree, send(tree, lambda y, c, z, x: (y, c, z ^ 2, x)), z >> 1)
    tree = merge(tree, send(tree, lambda y, c, z, x: (y, c, z ^ 1, x)), z & 1)
    y_count = dp_count // 2
    nw = shard.shape[0] // 3
    tree = tree.reshape(2, 2, y_count, 2, 2, 3 * nw + 8, 192).transpose(2, 3, 1, 0, 4, 5, 6)
    tree = tree.reshape(dp_count * 8, 3 * nw + 8, 192)
    w2 = jnp.concatenate(
        [tree[:, t * nw : (t + 1) * nw].reshape(width, 192) for t in range(3)], axis=1
    )
    flats = tree[:, 3 * nw :].reshape(dp_count * 8, -1)
    lists = [
        flats[:, i * nw : (i + 1) * nw].reshape(1, width) for i in range(13)
    ]
    tiles = up_weight.shape[1] // width
    ub4 = flats[:, 13 * nw : (13 + tiles) * nw].reshape(tiles, width).astype(F32)
    vecs = jnp.concatenate(lists + [jnp.zeros((3, width), BF16)]).astype(F32)
    own_cols = lambda v: lax.dynamic_slice_in_dim(v, hset * 192, 192, 1)
    zero_row = jnp.zeros((1, 192), F32)
    qkv_bias = jnp.concatenate([own_cols(vecs[6:7]), zero_row, own_cols(vecs[7:8])], axis=1)

    info = jnp.concatenate([block_map, branch_fork], axis=1)
    info = jnp.where((z >> 1) == c, info, send(info, flip(2)))
    info = jnp.where(parity == 0, info[0], info[1])
    place = jnp.arange(32, dtype=jnp.int32)
    k_of, p_of = place >> 3, (place >> 2) & 1
    stored = (2 * (2 * (c ^ (k_of >> 1)) + (p_of ^ parity)) + (x ^ (k_of & 1))) * 4 + (place & 3)
    logical = jnp.sum(jnp.where(stored[:, None] == place[None, :], info[None, :32], 0), axis=1)
    spot = jnp.sum(jnp.where(logical[None, :] == place[:, None], place[None, :], 0), axis=1)
    meta = jnp.concatenate(
        [logical, spot, info[32:40], jnp.full((56,), hset, jnp.int32)]
    ).astype(jnp.int32)

    dense = jnp.concatenate(
        [down_weight]
        + [up_weight[:, j * width : (j + 1) * width] for j in range(tiles)]
        + [self_out, cross_in[0], cross_in[1], cross_in[2], cross_out]
    )
    dense, w2, *across = lax.optimization_barrier((dense, w2, *across))
    dense = lax.all_gather(dense, AXES, axis=0)
    far = [send(v, flip(2)) for v in across]
    out_grad, far[1] = lax.optimization_barrier((out_grad, far[1]))
    pieces = mine + across + near + far
    nd = down_weight.shape[0]

    def gathered(i):
        at = nd + i * nw
        return dense[:, at : at + nw].reshape(width, width)

    dn4 = dense[:, :nd].reshape(tiles, width, width)
    up4 = jnp.stack([gathered(j) for j in range(tiles)])
    so = gathered(tiles)
    ci = jnp.stack([gathered(tiles + 1 + t) for t in range(3)])
    co = gathered(tiles + 4)

    q, kv, tr, n1 = qkv_call(meta, pieces, w2, vecs, qkv_bias)
    og = jnp.concatenate([send(pick(out_grad, p), home(p)) for p in range(2)])
    tok = jnp.concatenate([v[:rows] for v in mine])
    all_frames = jnp.concatenate([v[rows:] for v in pieces])

    o, lse = attend_call(meta, q, kv, tr)
    o4 = o.reshape(4, 1024, 192)
    o_home = [o4[0]] + [send(o4[k], flip(k)) for k in (1, 2, 3)]
    mid, ac, n2, n3, cq, ca, lse_c, kc, vc = mid_call(
        meta, tok, o_home, so, ci, co, all_frames, vecs
    )
    res, gt, ug, dg, ubg, dbg = feed_call(n3, og, ac, up4, dn4, ub4, vecs)
    gm, d0, d1, d2, d3, sog, cig, cog, eg, sums = mid_back_call(
        meta, gt, og, ac, mid, n2, cq, ca, lse_c, kc, vc, all_frames, so, ci, co, vecs, o_home
    )
    d_home = [d0] + [send(d, flip(k)) for k, d in ((1, d1), (2, d2), (3, d3))]

    def rows_of(grad):
        return grad.reshape(dp_count * 8, -1, width)

    packed = jnp.concatenate(
        [rows_of(dg)] + [rows_of(ug[j]) for j in range(tiles)]
        + [rows_of(sog), rows_of(cig[0]), rows_of(cig[1]), rows_of(cig[2]), rows_of(cog)],
        axis=1,
    )
    packed, *d_home = lax.optimization_barrier((packed, *d_home))
    dense_grad = lax.psum_scatter(packed, AXES, scatter_dimension=0, tiled=True)[0].astype(F32)

    results = [send(res[p * rows : (p + 1) * rows], home(p), True) for p in range(2)]
    eg4 = eg.reshape(4, 2 * frames, width)
    eg_near = send(eg4[2:4], flip(2)).astype(F32)
    eg_side = (eg4[1].astype(F32) + eg_near[1]).astype(BF16)
    eg_sum = eg4[0].astype(F32) + eg_near[0] + send(eg_side, flip(1)).astype(F32)
    eg_sum = eg_sum.astype(BF16)
    eg_back = [send(eg_sum[p * frames : (p + 1) * frames], home(p), True) for p in range(2)]

    dqkv, dx0, dx1, dx2, dx3 = attend_back_call(meta, q, kv, tr, o, lse, d_home, w2)
    dx3, results[0], results[1], eg_back[0], eg_back[1] = lax.optimization_barrier(
        (dx3, *results, *eg_back)
    )
    near3 = send(dx3, flip(2))
    side = (dx1.astype(F32) + near3.astype(F32)).astype(BF16)
    side_parts = [side[p * rows : (p + 1) * rows] for p in range(2)]
    side = [send(v, flip(1)) for v in side_parts]
    near2 = send(dx2, flip(2))
    n1, near3 = lax.optimization_barrier((n1, near3))

    wg, colsum = win_call(n1, dqkv)
    wg = wg.reshape(y_count, 2, 4, 2, nw, 576)

    def halve(v, move, bit, axis):
        keep = lax.dynamic_index_in_dim(v, bit, axis, False)
        give = lax.dynamic_index_in_dim(v, 1 - bit, axis, False)
        return (keep.astype(F32) + send(give, move).astype(F32)).astype(BF16)

    for bit in reversed(range((dp_count // 2).bit_length() - 1)):
        half = wg.shape[0] // 2
        wg = halve(
            wg.reshape((2, half) + wg.shape[1:]),
            lambda y, c, z, x, bit=bit: (y ^ (1 << bit), c, z, x), (y >> bit) & 1, 0,
        )
    wg = wg.reshape(2, 2, 2, 2, nw, 576)
    wg = halve(wg, lambda y, c, z, x: (y, c, z ^ 1, x), z & 1, 2)

    first = [first_back_call(dx0, near2, side[p], gm, tok, vecs, p) for p in range(2)]
    grads = [v[0] for v in first]
    first_sums = first[0][1] + first[1][1]
    wg, grads[0] = lax.optimization_barrier((wg, grads[0]))
    grads = [send(v, home(p), True) for p, v in enumerate(grads)]
    wg = halve(wg, lambda y, c, z, x: (y, c, z ^ 2, x), z >> 1, 1)
    wg = wg.reshape(4, nw, 576)

    def shard_for(k):
        return lax.dynamic_index_in_dim(wg, hset ^ k, 0, False)

    parts = jnp.stack([shard_for(0)] + [send(shard_for(k), flip(k)) for k in (1, 2, 3)])
    cols = [lax.dynamic_index_in_dim(parts, hset ^ j, 0, False) for j in range(4)]
    self_in_grad = jnp.stack(
        [jnp.concatenate([v[:, 192 * t : 192 * t + 192] for v in cols], axis=1) for t in range(3)]
    ).astype(F32)

    def returned(pair, dtype):
        pair = [v.astype(dtype) for v in pair]
        return jnp.stack([jnp.where(parity == 0, pair[0], pair[1]), jnp.where(parity == 0, pair[1], pair[0])])

    own_bias = lambda v: lax.dynamic_update_slice(
        jnp.zeros((1, width), F32), v, (0, hset * 192)
    )
    ubg = ubg.reshape(tiles, 8, width)[:, 0]
    def over_all(table):
        for k in (1, 2):
            table = table + send(table, flip(k))
        table = table + send(table, lambda y, c, z, x: (y, c, z ^ 1, x))
        table = table + send(table, lambda y, c, z, x: (y, c, z ^ 2, x))
        for bit in range((dp_count // 2).bit_length() - 1):
            table = table + send(table, lambda y, c, z, x, bit=bit: (y ^ (1 << bit), c, z, x))
        return table

    table = jnp.concatenate(
        [
            sums[1:3], sums[4:6], sums[8:12],
            own_bias(colsum[0:1, 0:192]), own_bias(colsum[0:1, 384:576]),
            dbg[0:1], ubg, jnp.zeros((16 - 11 - tiles, width), F32),
        ]
    )
    table = over_all(table)
    first_table = over_all(first_sums)
    table = jnp.concatenate(
        [
            first_table[0:1], table[0:2], first_table[1:2], table[2:4],
            table[8:10], table[4:8], table[10 : 11 + tiles],
        ]
    )
    mine_of = lambda v: lax.dynamic_slice_in_dim(v, flat * nw, nw, 1)
    vec_grad = mine_of(table[:13])
    up_bias_grad = lax.dynamic_slice_in_dim(
        table[13 : 13 + tiles].reshape(-1), flat * tiles * nw, tiles * nw, 0
    )

    def shard_grad(i):
        at = nd + i * nw
        return dense_grad[at : at + nw]

    return (
        returned(results, BF16),
        returned(grads, F32),
        returned(eg_back, F32),
        vec_grad[0:3],
        vec_grad[3:6],
        self_in_grad,
        shard_grad(tiles),
        vec_grad[6:9],
        jnp.stack([shard_grad(tiles + 1 + t) for t in range(3)]),
        shard_grad(tiles + 4),
        vec_grad[9:12],
        jnp.concatenate([shard_grad(j) for j in range(tiles)], axis=1),
        up_bias_grad,
        dense_grad[:nd],
        vec_grad[12],
    )


def solution(mesh):
    in_specs = (
        P("dp", "seq", None),
        P("dp", "seq", None),
        P("dp", "seq", None),
        P("dp", None),
        P("dp", None),
        P(None, ("dp", "seq")),
        P(None, ("dp", "seq")),
        P(None, ("dp", "seq"), None),
        P(("dp", "seq"), None),
        P(None, ("dp", "seq")),
        P(None, ("dp", "seq"), None),
        P(("dp", "seq"), None),
        P(None, ("dp", "seq")),
        P(("dp", "seq"), None),
        P(("dp", "seq")),
        P(("dp", "seq"), None),
        P(("dp", "seq")),
    )
    out_specs = (
        P("dp", "seq", None),
        P("dp", "seq", None),
        P("dp", "seq", None),
        P(None, ("dp", "seq")),
        P(None, ("dp", "seq")),
        P(None, ("dp", "seq"), None),
        P(("dp", "seq"), None),
        P(None, ("dp", "seq")),
        P(None, ("dp", "seq"), None),
        P(("dp", "seq"), None),
        P(None, ("dp", "seq")),
        P(("dp", "seq"), None),
        P(("dp", "seq")),
        P(("dp", "seq"), None),
        P(("dp", "seq")),
    )
    sizes = dict(mesh.shape)
    chosen = home_body if sizes["dp"] == 4 and sizes["seq"] == 8 else body
    return jax.shard_map(chosen, mesh=mesh, in_specs=in_specs, out_specs=out_specs, check_vma=False)
```

```python
import functools

import jax
import jax.numpy as jnp
from jax import lax
from jax.experimental import pallas as pl
from jax.experimental.pallas import tpu as pltpu
from jax.sharding import PartitionSpec as P

HEADS = 12
HEAD = 64
PROMPT = 2048
BRANCHES = 8
BLEN = 256
BLOCK = 128


def product(former, latter):
    return jnp.dot(former, latter, preferred_element_type=jnp.float32)


def product_left(former, latter):
    return lax.dot_general(
        former, latter, (((0,), (0,)), ((), ())), preferred_element_type=jnp.float32
    )


def product_right(former, latter):
    return lax.dot_general(
        former, latter, (((1,), (1,)), ((), ())), preferred_element_type=jnp.float32
    )


def column_sum(matrix):
    return jnp.sum(matrix.astype(jnp.float32), axis=0)


def norm_layer(stream, norm_gain, norm_shift):
    center = jnp.mean(stream, axis=-1, keepdims=True)
    centered = stream - center
    spread = jnp.mean(centered * centered, axis=-1, keepdims=True)
    return centered * lax.rsqrt(spread + 1e-05) * norm_gain + norm_shift


def gelu_exact(before):
    return jax.nn.gelu(before, approximate=False)


def token_info(blocks, branch_forks):
    offsets = jnp.arange(BLOCK, dtype=jnp.int32)
    logical = (blocks[:, None] * BLOCK + offsets[None, :]).reshape(-1)
    relative = logical - PROMPT
    in_branch = relative >= 0
    segment = jnp.where(in_branch, relative // BLEN + 1, 0)
    position = jnp.where(in_branch, relative % BLEN, logical)
    labels = jnp.arange(1, BRANCHES + 1, dtype=jnp.int32)
    fork_reach = jnp.sum(
        jnp.where(segment[:, None] == labels[None, :], branch_forks[None, :], 0), axis=1
    )
    return (segment, position, fork_reach)


def allowed(query_info, key_info):
    same = (query_info[0][:, None] == key_info[0][None, :]) & (
        key_info[1][None, :] <= query_info[1][:, None]
    )
    shared = (
        (query_info[0][:, None] > 0)
        & (key_info[0][None, :] == 0)
        & (key_info[1][None, :] < query_info[2][:, None])
    )
    return same | shared


def head_split(matrix):
    return matrix.reshape(matrix.shape[0], HEADS, HEAD)


def score_block(queries, key_rows, key_mask):
    scores = jnp.einsum(
        "rhd,khd->hrk",
        head_split(queries),
        head_split(key_rows),
        preferred_element_type=jnp.float32,
    ) * HEAD ** (-0.5)
    if key_mask is None:
        return scores
    return jnp.where(key_mask[None], scores, -1e30)


def attend_forward(queries, key_rows, value_rows, key_mask):
    scores = score_block(queries, key_rows, key_mask)
    row_max = jnp.max(scores, axis=2, keepdims=True)
    weights = jnp.exp(scores - row_max)
    row_total = jnp.sum(weights, axis=2, keepdims=True)
    shares = (weights / row_total).astype(jnp.bfloat16)
    attended = jnp.einsum(
        "hrk,khd->rhd", shares, head_split(value_rows), preferred_element_type=jnp.float32
    )
    return (attended.reshape(queries.shape[0], -1).astype(jnp.bfloat16), row_max, row_total)


def attend_backward(queries, key_rows, value_rows, key_mask, row_max, row_total, incoming):
    scores = score_block(queries, key_rows, key_mask)
    shares_full = jnp.exp(scores - row_max) / row_total
    shares_low = shares_full.astype(jnp.bfloat16)
    grad_heads = head_split(incoming)
    grad_values = jnp.einsum(
        "hrk,rhd->khd", shares_low, grad_heads, preferred_element_type=jnp.float32
    )
    grad_shares = jnp.einsum(
        "rhd,khd->hrk", grad_heads, head_split(value_rows), preferred_element_type=jnp.float32
    )
    inner_sum = jnp.sum(grad_shares * shares_full, axis=2, keepdims=True)
    grad_scores = (shares_full * (grad_shares - inner_sum)).astype(jnp.bfloat16)
    grad_queries = jnp.einsum(
        "hrk,khd->rhd", grad_scores, head_split(key_rows), preferred_element_type=jnp.float32
    ) * HEAD ** (-0.5)
    grad_keys = jnp.einsum(
        "hrk,rhd->khd", grad_scores, head_split(queries), preferred_element_type=jnp.float32
    ) * HEAD ** (-0.5)
    row_count = queries.shape[0]
    key_count = key_rows.shape[0]
    return (
        grad_queries.reshape(row_count, -1),
        grad_keys.reshape(key_count, -1),
        grad_values.reshape(key_count, -1),
    )


def fetch_self(shards):
    return (
        lax.all_gather(shards[0][0], ("dp", "seq"), axis=0, tiled=True),
        lax.all_gather(shards[1][0], ("dp", "seq"), axis=0, tiled=True),
        lax.all_gather(shards[2], ("dp", "seq"), axis=1, tiled=True),
        lax.all_gather(shards[3], ("dp", "seq"), axis=0, tiled=True),
        lax.all_gather(shards[4], ("dp", "seq"), axis=1, tiled=True),
    )


def fetch_cross(shards):
    return (
        lax.all_gather(shards[0][1], ("dp", "seq"), axis=0, tiled=True),
        lax.all_gather(shards[1][1], ("dp", "seq"), axis=0, tiled=True),
        lax.all_gather(shards[5], ("dp", "seq"), axis=1, tiled=True),
        lax.all_gather(shards[6], ("dp", "seq"), axis=0, tiled=True),
        lax.all_gather(shards[7], ("dp", "seq"), axis=1, tiled=True),
    )


def fetch_feed(shards):
    return (
        lax.all_gather(shards[0][2], ("dp", "seq"), axis=0, tiled=True),
        lax.all_gather(shards[1][2], ("dp", "seq"), axis=0, tiled=True),
        lax.all_gather(shards[8], ("dp", "seq"), axis=0, tiled=True),
        lax.all_gather(shards[9], ("dp", "seq"), axis=0, tiled=True),
        lax.all_gather(shards[10], ("dp", "seq"), axis=0, tiled=True),
        lax.all_gather(shards[11], ("dp", "seq"), axis=0, tiled=True),
    )


def body(
    tokens,
    encoder_states,
    out_grad,
    block_map,
    branch_fork,
    norm_gain,
    norm_bias,
    self_in,
    self_out,
    self_bias,
    cross_in,
    cross_out,
    cross_bias,
    up_weight,
    up_bias,
    down_weight,
    down_bias,
):
    shards = (
        norm_gain,
        norm_bias,
        self_in,
        self_out,
        self_bias,
        cross_in,
        cross_out,
        cross_bias,
        up_weight,
        up_bias,
        down_weight,
        down_bias,
    )
    model_width = tokens.shape[2]
    hidden_width = up_weight.shape[1]
    seq_count = lax.axis_size("seq")
    seq_place = lax.axis_index("seq")

    def micro_step(grad_sums, inputs):
        tokens_in, encoded, cotangent, blocks, branch_forks = inputs
        slot_count = blocks.shape[0] // seq_count
        own_blocks = lax.dynamic_slice_in_dim(blocks, seq_place * slot_count, slot_count)
        query_info = token_info(own_blocks, branch_forks)
        full_info = token_info(blocks, branch_forks)
        key_mask = allowed(query_info, full_info)
        gain_first, shift_first, attend_in, attend_out, attend_bias = fetch_self(shards)
        stream = tokens_in.astype(jnp.float32)
        norm_full, pull_first = jax.vjp(
            norm_layer, stream, gain_first.astype(jnp.float32), shift_first.astype(jnp.float32)
        )
        norm_first = norm_full.astype(jnp.bfloat16)
        queries = (product(norm_first, attend_in[0]) + attend_bias[0].astype(jnp.float32)).astype(
            jnp.bfloat16
        )
        key_local = product(norm_first, attend_in[1]).astype(jnp.bfloat16)
        value_local = (
            product(norm_first, attend_in[2]) + attend_bias[1].astype(jnp.float32)
        ).astype(jnp.bfloat16)
        key_rows, value_rows = (
            lax.all_gather(key_local, "seq", axis=0, tiled=True),
            lax.all_gather(value_local, "seq", axis=0, tiled=True),
        )
        attended, self_max, self_total = attend_forward(queries, key_rows, value_rows, key_mask)
        middle = stream + product(attended, attend_out) + attend_bias[2].astype(jnp.float32)
        gain_second, shift_second, cross_proj, cross_back, cross_shift = fetch_cross(shards)
        cross_key_local = product(encoded, cross_proj[1]).astype(jnp.bfloat16)
        cross_value_local = (
            product(encoded, cross_proj[2]) + cross_shift[1].astype(jnp.float32)
        ).astype(jnp.bfloat16)
        cross_keys, cross_values = (
            lax.all_gather(cross_key_local, "seq", axis=0, tiled=True),
            lax.all_gather(cross_value_local, "seq", axis=0, tiled=True),
        )
        norm_full_second, pull_second = jax.vjp(
            norm_layer, middle, gain_second.astype(jnp.float32), shift_second.astype(jnp.float32)
        )
        norm_second = norm_full_second.astype(jnp.bfloat16)
        cross_queries = (
            product(norm_second, cross_proj[0]) + cross_shift[0].astype(jnp.float32)
        ).astype(jnp.bfloat16)
        cross_attended, cross_max, cross_total = attend_forward(
            cross_queries, cross_keys, cross_values, None
        )
        after_cross = (
            middle + product(cross_attended, cross_back) + cross_shift[2].astype(jnp.float32)
        )
        gain_third, shift_third, feed_up, feed_up_bias, feed_down, feed_down_bias = fetch_feed(
            shards
        )
        norm_full_third, pull_third = jax.vjp(
            norm_layer, after_cross, gain_third.astype(jnp.float32), shift_third.astype(jnp.float32)
        )
        norm_third = norm_full_third.astype(jnp.bfloat16)
        before = product(norm_third, feed_up) + feed_up_bias.astype(jnp.float32)
        activated_full, gelu_pull = jax.vjp(gelu_exact, before)
        activated = activated_full.astype(jnp.bfloat16)
        result = after_cross + product(activated, feed_down) + feed_down_bias.astype(jnp.float32)
        gain_third, shift_third, feed_up, feed_up_bias, feed_down, feed_down_bias = fetch_feed(
            shards
        )
        cot_float = cotangent.astype(jnp.float32)
        grad_act = product_right(cotangent, feed_down)
        grad_down = product_left(activated, cotangent)
        grad_down_bias = jnp.sum(cot_float, axis=0)
        grad_before = gelu_pull(grad_act)[0].astype(jnp.bfloat16)
        grad_up = product_left(norm_third, grad_before)
        grad_up_bias = column_sum(grad_before)
        grad_third = product_right(grad_before, feed_up)
        grad_after_norm, grad_gain_third, grad_shift_third = pull_third(grad_third)
        grad_after = cot_float + grad_after_norm
        gain_second, shift_second, cross_proj, cross_back, cross_shift = fetch_cross(shards)
        grad_after_low = grad_after.astype(jnp.bfloat16)
        grad_cross_back = product_left(cross_attended, grad_after_low)
        grad_cross_out_bias = column_sum(grad_after_low)
        grad_cross_attended = product_right(grad_after_low, cross_back).astype(jnp.bfloat16)
        grad_cross_queries, grad_cross_keys, grad_cross_values = attend_backward(
            cross_queries,
            cross_keys,
            cross_values,
            None,
            cross_max,
            cross_total,
            grad_cross_attended,
        )
        cross_key_part, cross_value_part = (
            lax.psum_scatter(
                grad_cross_keys.astype(jnp.bfloat16), "seq", scatter_dimension=0, tiled=True
            ).astype(jnp.float32),
            lax.psum_scatter(
                grad_cross_values.astype(jnp.bfloat16), "seq", scatter_dimension=0, tiled=True
            ).astype(jnp.float32),
        )
        cross_key_low = cross_key_part.astype(jnp.bfloat16)
        cross_value_low = cross_value_part.astype(jnp.bfloat16)
        cross_query_low = grad_cross_queries.astype(jnp.bfloat16)
        grad_cross_proj = jnp.stack(
            [
                product_left(norm_second, cross_query_low),
                product_left(encoded, cross_key_low),
                product_left(encoded, cross_value_low),
            ]
        )
        grad_cross_shift = jnp.stack(
            [column_sum(cross_query_low), column_sum(cross_value_low), grad_cross_out_bias]
        )
        encoder_grad = product_right(cross_key_low, cross_proj[1]) + product_right(
            cross_value_low, cross_proj[2]
        )
        grad_second = product_right(cross_query_low, cross_proj[0])
        grad_middle_norm, grad_gain_second, grad_shift_second = pull_second(grad_second)
        grad_middle = grad_after + grad_middle_norm
        gain_first, shift_first, attend_in, attend_out, attend_bias = fetch_self(shards)
        grad_middle_low = grad_middle.astype(jnp.bfloat16)
        grad_attend_out = product_left(attended, grad_middle_low)
        grad_out_bias = column_sum(grad_middle_low)
        grad_attended = product_right(grad_middle_low, attend_out).astype(jnp.bfloat16)
        grad_queries, grad_keys, grad_values = attend_backward(
            queries, key_rows, value_rows, key_mask, self_max, self_total, grad_attended
        )
        key_part, value_part = (
            lax.psum_scatter(
                grad_keys.astype(jnp.bfloat16), "seq", scatter_dimension=0, tiled=True
            ).astype(jnp.float32),
            lax.psum_scatter(
                grad_values.astype(jnp.bfloat16), "seq", scatter_dimension=0, tiled=True
            ).astype(jnp.float32),
        )
        key_low = key_part.astype(jnp.bfloat16)
        value_low = value_part.astype(jnp.bfloat16)
        query_low = grad_queries.astype(jnp.bfloat16)
        grad_attend_in = jnp.stack(
            [
                product_left(norm_first, query_low),
                product_left(norm_first, key_low),
                product_left(norm_first, value_low),
            ]
        )
        grad_attend_bias = jnp.stack([column_sum(query_low), column_sum(value_low), grad_out_bias])
        grad_first = (
            product_right(query_low, attend_in[0])
            + product_right(key_low, attend_in[1])
            + product_right(value_low, attend_in[2])
        )
        grad_stream_norm, grad_gain_first, grad_shift_first = pull_first(grad_first)
        tokens_grad = grad_middle + grad_stream_norm
        updates = (
            jnp.stack([grad_gain_first, grad_gain_second, grad_gain_third]),
            jnp.stack([grad_shift_first, grad_shift_second, grad_shift_third]),
            grad_attend_in,
            grad_attend_out,
            grad_attend_bias,
            grad_cross_proj,
            grad_cross_back,
            grad_cross_shift,
            grad_up,
            grad_up_bias,
            grad_down,
            grad_down_bias,
        )
        grad_sums = tuple((former + latter for former, latter in zip(grad_sums, updates)))
        return (grad_sums, (result.astype(jnp.bfloat16), tokens_grad, encoder_grad))

    starting = (
        jnp.zeros((3, model_width), jnp.float32),
        jnp.zeros((3, model_width), jnp.float32),
        jnp.zeros((3, model_width, model_width), jnp.float32),
        jnp.zeros((model_width, model_width), jnp.float32),
        jnp.zeros((3, model_width), jnp.float32),
        jnp.zeros((3, model_width, model_width), jnp.float32),
        jnp.zeros((model_width, model_width), jnp.float32),
        jnp.zeros((3, model_width), jnp.float32),
        jnp.zeros((model_width, hidden_width), jnp.float32),
        jnp.zeros((hidden_width,), jnp.float32),
        jnp.zeros((hidden_width, model_width), jnp.float32),
        jnp.zeros((model_width,), jnp.float32),
    )
    grad_sums, outputs = lax.scan(
        micro_step, starting, (tokens, encoder_states, out_grad, block_map, branch_fork)
    )
    feed_part = (
        lax.psum_scatter(grad_sums[8], ("dp", "seq"), scatter_dimension=0, tiled=True),
        lax.psum_scatter(grad_sums[9], ("dp", "seq"), scatter_dimension=0, tiled=True),
        lax.psum_scatter(grad_sums[10], ("dp", "seq"), scatter_dimension=0, tiled=True),
        lax.psum_scatter(grad_sums[11], ("dp", "seq"), scatter_dimension=0, tiled=True),
    )
    cross_part = (
        lax.psum_scatter(grad_sums[5], ("dp", "seq"), scatter_dimension=1, tiled=True),
        lax.psum_scatter(grad_sums[6], ("dp", "seq"), scatter_dimension=0, tiled=True),
        lax.psum_scatter(grad_sums[7], ("dp", "seq"), scatter_dimension=1, tiled=True),
    )
    self_part = (
        lax.psum_scatter(grad_sums[0], ("dp", "seq"), scatter_dimension=1, tiled=True),
        lax.psum_scatter(grad_sums[1], ("dp", "seq"), scatter_dimension=1, tiled=True),
        lax.psum_scatter(grad_sums[2], ("dp", "seq"), scatter_dimension=1, tiled=True),
        lax.psum_scatter(grad_sums[3], ("dp", "seq"), scatter_dimension=0, tiled=True),
        lax.psum_scatter(grad_sums[4], ("dp", "seq"), scatter_dimension=1, tiled=True),
    )
    return (
        outputs[0],
        outputs[1],
        outputs[2],
        self_part[0],
        self_part[1],
        self_part[2],
        self_part[3],
        self_part[4],
        cross_part[0],
        cross_part[1],
        cross_part[2],
        feed_part[0],
        feed_part[1],
        feed_part[2],
        feed_part[3],
    )


LOG2E = 1.4426950408889634
LN2 = 0.6931471805599453
QSCALE = HEAD ** (-0.5) * LOG2E
AXES = ("dp", "seq")
F32 = jnp.float32
BF16 = jnp.bfloat16
ANY = pl.BlockSpec(memory_space=pl.ANY)
SMEM = pl.BlockSpec(memory_space=pltpu.SMEM)


def nn(a, b):
    return lax.dot_general(a, b, (((1,), (0,)), ((), ())), preferred_element_type=F32)


def nt(a, b):
    return lax.dot_general(a, b, (((1,), (1,)), ((), ())), preferred_element_type=F32)


def tn(a, b):
    return lax.dot_general(a, b, (((0,), (0,)), ((), ())), preferred_element_type=F32)


def whole(shape):
    zeros = (0,) * len(shape)
    return pl.BlockSpec(shape, lambda *_: zeros)


def params(**kw):
    return pltpu.CompilerParams(vmem_limit_bytes=60 * 1024 * 1024, **kw)


def cost(flops, nbytes, trans=0):
    return pl.CostEstimate(flops=int(flops), bytes_accessed=int(nbytes), transcendentals=int(trans))


def stats(v):
    mean = jnp.mean(v, axis=-1, keepdims=True)
    centered = v - mean
    var = jnp.mean(centered * centered, axis=-1, keepdims=True)
    rstd = lax.rsqrt(var + 1e-05)
    return centered * rstd, rstd


def norm_back(v, e, gain):
    z, rstd = stats(v)
    f = e * gain
    grad = rstd * (
        f - jnp.mean(f, axis=-1, keepdims=True) - z * jnp.mean(f * z, axis=-1, keepdims=True)
    )
    return grad, jnp.sum(e * z, axis=0, keepdims=True), jnp.sum(e, axis=0, keepdims=True)


def qkv_kernel(meta, *refs):
    pieces = refs[:8]
    w_ref, vec_ref, bias_ref, q_ref, kv_ref, tr_ref, n1_ref, buf, sem = refs[8:]
    rows = buf.shape[0] // 8
    step = pl.program_id(0)

    @pl.when(step == 0)
    def _():
        copies = [
            pltpu.make_async_copy(pieces[i], buf.at[pl.ds(i * rows, rows), :], sem.at[i])
            for i in range(8)
        ]
        for c in copies:
            c.start()
        for c in copies:
            c.wait()

    gain, shift = vec_ref[0:1, :], vec_ref[3:4, :]
    w = w_ref[...]
    bias = bias_ref[0:1, :]
    for u in range(4):
        b = meta[32 + step * 4 + u]
        off = pl.multiple_of((b // 4) * rows + (b % 4) * 128, 32)
        x = buf[pl.ds(off, 128), :].astype(F32)
        z, _ = stats(x)
        n1 = (z * gain + shift).astype(BF16)
        r = slice(u * 128, (u + 1) * 128)
        n1_ref[r, :] = n1
        y = nn(n1, w) + bias
        kvt = jnp.transpose(y[:, 192:576]).astype(BF16)
        for t in range(2):
            for h in range(3):
                o = (t * 3 + h) * 64
                tr_ref[t * 3 + h, :, r] = kvt[o : o + 64, :]
        yq = (y[:, 0:192] * QSCALE).astype(BF16)
        yk = y[:, 192:576].astype(BF16)
        zero = jnp.zeros((128, 64), BF16)
        for h in range(3):
            q_ref[h, r, :] = jnp.concatenate([yq[:, h * 64 : h * 64 + 64], zero], axis=1)
            kv_ref[h, r, :] = jnp.concatenate(
                [yk[:, h * 64 : h * 64 + 64], yk[:, 192 + h * 64 : 256 + h * 64]], axis=1
            )


def qkv_call(meta, pieces, w2, vecs, bias):
    rows = pieces[0].shape[0]
    grid = (8,)
    return pl.pallas_call(
        qkv_kernel,
        grid_spec=pltpu.PrefetchScalarGridSpec(
            num_scalar_prefetch=1,
            grid=grid,
            in_specs=[ANY] * 8 + [whole(w2.shape), whole(vecs.shape), whole(bias.shape)],
            out_specs=[
                pl.BlockSpec((3, 512, 128), lambda i, m: (0, i, 0)),
                pl.BlockSpec((3, 512, 128), lambda i, m: (0, i, 0)),
                pl.BlockSpec((6, 64, 512), lambda i, m: (0, 0, i)),
                pl.BlockSpec((512, 768), lambda i, m: (i, 0)),
            ],
            scratch_shapes=[pltpu.VMEM((8 * rows, 768), BF16), pltpu.SemaphoreType.DMA((8,))],
        ),
        out_shape=[
            jax.ShapeDtypeStruct((3, 4096, 128), BF16),
            jax.ShapeDtypeStruct((3, 4096, 128), BF16),
            jax.ShapeDtypeStruct((6, 64, 4096), BF16),
            jax.ShapeDtypeStruct((4096, 768), BF16),
        ],
        compiler_params=params(dimension_semantics=("arbitrary",)),
        cost_estimate=cost(2 * 4096 * 768 * 576, 20e6),
        name="qkv",
    )(meta, *pieces, w2, vecs, bias)


def tile_plan(meta, qi):
    branch = qi >= 8
    fork = meta[64 + jnp.maximum(qi - 8, 0)]
    count = jnp.where(branch, (fork + 255) // 256, qi) + 1
    reach = jnp.where(branch, fork, 4096)

    def tile(t, own):
        if own:
            kt = qi
        else:
            kt = jnp.where(t == count - 1, qi, t)
        key = lax.broadcasted_iota(jnp.int32, (256, 256), 0)
        query = lax.broadcasted_iota(jnp.int32, (256, 256), 1)
        if own:
            mask = key <= query
        else:
            limit = jnp.where(t == count - 1, 0, jnp.minimum(reach - t * 256, 256) - 1)
            slope = jnp.where(t == count - 1, 1, 0)
            mask = key <= query[0:1, :] * slope + limit
        return pl.ds(pl.multiple_of(kt * 256, 256), 256), mask

    return count, tile


def tile_pairs(count, step):
    def pair(i, carry):
        step(i * 2, False)
        step(i * 2 + 1, False)
        return carry

    lax.fori_loop(0, count // 2, pair, 0)

    @pl.when(count % 2 == 1)
    def _():
        step(count - 1, True)


def attend_kernel(meta, q_ref, kv_ref, tr_ref, o_ref, lse_ref, m_ref, l_ref, acc_ref):
    def q_tile(qi, carry):
        count, tile = tile_plan(meta, qi)
        qs = pl.ds(pl.multiple_of(qi * 256, 256), 256)
        m_ref[...] = jnp.full_like(m_ref, -1e30)
        l_ref[...] = jnp.zeros_like(l_ref)
        acc_ref[...] = jnp.zeros_like(acc_ref)

        def k_tile(t, own):
            ks, mask = tile(t, own)
            s = [nt(kv_ref[h, ks, :], q_ref[h, qs, :]) for h in range(3)]
            s = [jnp.where(mask, v, -1e30) for v in s]
            old = [m_ref[h : h + 1, :] for h in range(3)]
            new = [jnp.maximum(old[h], jnp.max(s[h], axis=0, keepdims=True)) for h in range(3)]
            p = [jnp.exp2(s[h] - new[h]) for h in range(3)]
            out = [nn(tr_ref[3 + h, :, ks], p[h].astype(BF16)) for h in range(3)]
            for h in range(3):
                alpha = jnp.exp2(old[h] - new[h])
                m_ref[h : h + 1, :] = new[h]
                l_ref[h : h + 1, :] = l_ref[h : h + 1, :] * alpha + jnp.sum(p[h], axis=0, keepdims=True)
                hs = slice(h * 64, h * 64 + 64)
                acc_ref[hs, :] = acc_ref[hs, :] * alpha + out[h]

        tile_pairs(count, k_tile)
        for h in range(3):
            hs = slice(h * 64, h * 64 + 64)
            l = l_ref[h : h + 1, :]
            acc_ref[hs, :] = acc_ref[hs, :] * (1.0 / l)
            lse_ref[h : h + 1, qs] = m_ref[h : h + 1, :] + jnp.log2(l)
        out = jnp.transpose(acc_ref[...]).astype(BF16)
        for u in range(2):
            o_ref[meta[32 + qi * 2 + u]] = out[u * 128 : (u + 1) * 128, :]
        return carry

    lax.fori_loop(0, 16, q_tile, 0)


def attend_call(meta, q, kv, tr):
    return pl.pallas_call(
        attend_kernel,
        grid_spec=pltpu.PrefetchScalarGridSpec(
            num_scalar_prefetch=1,
            grid=(1,),
            in_specs=[whole(q.shape), whole(kv.shape), whole(tr.shape)],
            out_specs=[whole((32, 128, 192)), whole((8, 4096))],
            scratch_shapes=[
                pltpu.VMEM((8, 256), F32),
                pltpu.VMEM((8, 256), F32),
                pltpu.VMEM((192, 256), F32),
            ],
        ),
        out_shape=[
            jax.ShapeDtypeStruct((32, 128, 192), BF16),
            jax.ShapeDtypeStruct((8, 4096), F32),
        ],
        compiler_params=params(dimension_semantics=("arbitrary",)),
        cost_estimate=cost(20e9, 10e6, 20e6),
        name="attend",
    )(meta, q, kv, tr)


def attend_back_kernel(
    meta, q_ref, kv_ref, tr_ref, o_ref, lse_ref, d0, d1, d2, d3, w_ref,
    out_ref, x0, x1, x2, x3, do_ref, di_ref, dq_ref, acc_ref, wt_ref,
):
    pieces = (d0, d1, d2, d3)
    zero = jnp.zeros((128, 64), BF16)
    head = lax.broadcasted_iota(jnp.int32, (8, 192), 0) * 64
    lane = lax.broadcasted_iota(jnp.int32, (8, 192), 1)
    pick = jnp.where((lane >= head) & (lane < head + 64), 1.0, 0.0).astype(BF16)

    def arrange(kk, carry):
        rs = pl.ds(pl.multiple_of(kk * 128, 128), 128)
        for k in range(4):
            b = k * 8 + kk
            at = pl.ds(pl.multiple_of(meta[b] * 128, 128), 128)
            do = pieces[k][rs, :]
            prod = do.astype(F32) * o_ref[b].astype(F32)
            high = prod.astype(BF16)
            low = (prod - high.astype(F32)).astype(BF16)
            di_ref[:, at] = nt(pick, high) + nt(pick, low)
            for h in range(3):
                do_ref[h, at, :] = jnp.concatenate([zero, do[:, h * 64 : h * 64 + 64]], axis=1)
        return carry

    lax.fori_loop(0, 8, arrange, 0)
    acc_ref[...] = jnp.zeros_like(acc_ref)

    def q_tile(qi, carry):
        count, tile = tile_plan(meta, qi)
        qs = pl.ds(pl.multiple_of(qi * 256, 256), 256)
        dq_ref[...] = jnp.zeros_like(dq_ref)

        def k_tile(t, own):
            ks, mask = tile(t, own)
            q = [q_ref[h, qs, :] for h in range(3)]
            do = [do_ref[h, qs, :] for h in range(3)]
            kv = [kv_ref[h, ks, :] for h in range(3)]
            s = [nt(kv[h], q[h]) for h in range(3)]
            dp = [nt(kv[h], do[h]) for h in range(3)]
            p, ds = [], []
            for h in range(3):
                e = jnp.where(mask, jnp.exp2(s[h] - lse_ref[h : h + 1, qs]), 0.0)
                p.append(e.astype(BF16))
                ds.append((e * (dp[h] - di_ref[h : h + 1, qs])).astype(BF16))
            for h in range(3):
                acc_ref[h, ks, :] += nn(ds[h], q[h]) + nn(p[h], do[h])
                hs = slice(h * 64, h * 64 + 64)
                dq_ref[hs, :] += nn(tr_ref[h, :, ks], ds[h])

        tile_pairs(count, k_tile)
        out_ref[qs, 0:192] = (jnp.transpose(dq_ref[...]) * HEAD ** (-0.5)).astype(BF16)
        return carry

    lax.fori_loop(0, 16, q_tile, 0)

    def finish(t, carry):
        rs = pl.ds(pl.multiple_of(t * 256, 256), 256)
        a = [acc_ref[h, rs, :] for h in range(3)]
        dk = jnp.concatenate([v[:, 0:64] for v in a], axis=1) * LN2
        dv = jnp.concatenate([v[:, 64:128] for v in a], axis=1)
        out_ref[rs, 192:576] = jnp.concatenate([dk, dv], axis=1).astype(BF16)
        return carry

    lax.fori_loop(0, 16, finish, 0)
    wt = jnp.transpose(w_ref[...])
    wt_ref[...] = wt

    def spread(i, carry):
        rs = pl.ds(pl.multiple_of(i * 512, 512), 512)
        for k, x_ref in enumerate((x0, x1, x2, x3)):
            rows = [
                out_ref[pl.ds(pl.multiple_of(meta[k * 8 + i * 4 + u] * 128, 128), 128), :]
                for u in range(4)
            ]
            x_ref[rs, :] = nn(jnp.concatenate(rows, axis=0), wt_ref[...]).astype(BF16)
        return carry

    lax.fori_loop(0, 2, spread, 0)


def attend_back_call(meta, q, kv, tr, o, lse, pieces, w2):
    ins = [q, kv, tr, o, lse, *pieces, w2]
    return pl.pallas_call(
        attend_back_kernel,
        grid_spec=pltpu.PrefetchScalarGridSpec(
            num_scalar_prefetch=1,
            grid=(1,),
            in_specs=[whole(v.shape) for v in ins],
            out_specs=[whole((4096, 576))] + [whole((1024, 768))] * 4,
            scratch_shapes=[
                pltpu.VMEM((3, 4096, 128), BF16),
                pltpu.VMEM((8, 4096), F32),
                pltpu.VMEM((192, 256), F32),
                pltpu.VMEM((3, 4096, 128), F32),
                pltpu.VMEM((576, 768), BF16),
            ],
        ),
        out_shape=[jax.ShapeDtypeStruct((4096, 576), BF16)]
        + [jax.ShapeDtypeStruct((1024, 768), BF16)] * 4,
        compiler_params=params(dimension_semantics=("arbitrary",)),
        cost_estimate=cost(50e9, 15e6, 20e6),
        name="attend_back",
    )(meta, *ins)


def win_kernel(n_ref, d_ref, g_ref, s_ref, acc_ref):
    step = pl.program_id(0)

    @pl.when(step == 0)
    def _():
        acc_ref[...] = jnp.zeros_like(acc_ref)
        s_ref[...] = jnp.zeros_like(s_ref)

    d = d_ref[...]
    acc_ref[...] += tn(n_ref[...], d)
    s_ref[0:1, :] += jnp.sum(d.astype(F32), axis=0, keepdims=True)

    @pl.when(step == pl.num_programs(0) - 1)
    def _():
        g_ref[...] = acc_ref[...].astype(BF16)


def win_call(n1, dqkv):
    return pl.pallas_call(
        win_kernel,
        grid=(4,),
        in_specs=[
            pl.BlockSpec((1024, 768), lambda i: (i, 0)),
            pl.BlockSpec((1024, 576), lambda i: (i, 0)),
        ],
        out_specs=[whole((768, 576)), whole((8, 576))],
        out_shape=[
            jax.ShapeDtypeStruct((768, 576), BF16),
            jax.ShapeDtypeStruct((8, 576), F32),
        ],
        scratch_shapes=[pltpu.VMEM((768, 576), F32)],
        compiler_params=params(dimension_semantics=("arbitrary",)),
        cost_estimate=cost(2 * 4096 * 768 * 576, 12e6),
        name="win",
    )(n1, dqkv)


def head_masks(frames):
    lane = lax.broadcasted_iota(jnp.int32, (frames, 128), 1) < 64
    return lane, jnp.logical_not(lane)


def mid_kernel(
    meta, tok_ref, o0, o1, o2, o3, so_ref, ci_ref, co_ref, fr_ref, vec_ref,
    mid_ref, ac_ref, n2_ref, n3_ref, cq_ref, ca_ref, lse_ref, kc_ref, vc_ref,
    km_ref, vmt_ref,
):
    frames = fr_ref.shape[0]
    hset = meta[72]

    @pl.when(pl.program_id(0) == 0)
    def _():
        fr = fr_ref[...]
        kc = nn(fr, ci_ref[1]).astype(BF16)
        vc = (nn(fr, ci_ref[2]) + vec_ref[10:11, :]).astype(BF16)
        kc_ref[...] = kc
        vc_ref[...] = vc
        zero = jnp.zeros((frames, 128), BF16)
        masks = head_masks(frames)
        for hp in range(6):
            ls = slice(hp * 128, hp * 128 + 128)
            for e in range(2):
                km_ref[hp * 2 + e] = jnp.where(masks[e], kc[:, ls], zero)
                vmt_ref[hp * 2 + e] = jnp.transpose(
                    jnp.where(masks[e], vc[:, ls].astype(F32), 0.0)
                ).astype(BF16)

    acc = tok_ref[...].astype(F32) + vec_ref[8:9, :]
    for k, o in enumerate((o0, o1, o2, o3)):
        at = pl.ds(pl.multiple_of((hset ^ k) * 192, 64), 192)
        acc = acc + nn(o[...], so_ref[at, :])
    mid_ref[...] = acc
    z, _ = stats(acc)
    n2 = (z * vec_ref[1:2, :] + vec_ref[4:5, :]).astype(BF16)
    n2_ref[...] = n2
    cq = ((nn(n2, ci_ref[0]) + vec_ref[9:10, :]) * QSCALE).astype(BF16)
    cq_ref[...] = cq
    ca = []
    for first in range(0, 12, 4):
        heads = range(first, first + 4)
        s = [nt(km_ref[h], cq[:, (h // 2) * 128 : (h // 2) * 128 + 128]) for h in heads]
        m = [jnp.max(v, axis=0, keepdims=True) for v in s]
        p = [jnp.exp2(v - w) for v, w in zip(s, m)]
        part = [nn(vmt_ref[h], v.astype(BF16)) for h, v in zip(heads, p)]
        for i, h in enumerate(heads):
            l = jnp.sum(p[i], axis=0, keepdims=True)
            lse_ref[h : h + 1, :] = m[i] + jnp.log2(l)
            part[i] = part[i] * (1.0 / l)
        for i in (0, 2):
            ca.append(jnp.transpose(part[i] + part[i + 1]).astype(BF16))
    ca = jnp.concatenate(ca, axis=1)
    ca_ref[...] = ca
    ac = acc + nn(ca, co_ref[...]) + vec_ref[11:12, :]
    ac_ref[...] = ac
    z, _ = stats(ac)
    n3_ref[...] = (z * vec_ref[2:3, :] + vec_ref[5:6, :]).astype(BF16)


def mid_call(meta, tok, pieces, so, ci, co, frames, vecs):
    rows, width = tok.shape
    tile = 256
    nf = frames.shape[0]
    row = pl.BlockSpec((tile, width), lambda i, m: (i, 0))
    row4 = pl.BlockSpec((tile, 192), lambda i, m: (i, 0))
    sds = jax.ShapeDtypeStruct
    return pl.pallas_call(
        mid_kernel,
        grid_spec=pltpu.PrefetchScalarGridSpec(
            num_scalar_prefetch=1,
            grid=(rows // tile,),
            in_specs=[row] + [row4] * 4
            + [whole(so.shape), whole(ci.shape), whole(co.shape), whole(frames.shape), whole(vecs.shape)],
            out_specs=[row] * 6
            + [pl.BlockSpec((16, tile), lambda i, m: (0, i)), whole((nf, width)), whole((nf, width))],
            scratch_shapes=[pltpu.VMEM((12, nf, 128), BF16), pltpu.VMEM((12, 128, nf), BF16)],
        ),
        out_shape=[
            sds((rows, width), F32), sds((rows, width), F32), sds((rows, width), BF16),
            sds((rows, width), BF16), sds((rows, width), BF16), sds((rows, width), BF16),
            sds((16, rows), F32), sds((nf, width), BF16), sds((nf, width), BF16),
        ],
        compiler_params=params(dimension_semantics=("arbitrary",)),
        cost_estimate=cost(8e9, 25e6, 3e6),
        name="middle",
    )(meta, tok, *pieces, so, ci, co, frames, vecs)


def normal_parts(b):
    e = jnp.exp2(b * b * (-0.5 * LOG2E))
    a = jnp.abs(b) * 0.7071067811865476
    t = 1.0 / (1.0 + 0.3275911 * a)
    poly = t * (
        0.254829592 + t * (-0.284496736 + t * (1.421413741 + t * (-1.453152027 + t * 1.061405429)))
    )
    tail = 0.5 * poly * e
    return jnp.where(b < 0.0, tail, 1.0 - tail), e * 0.3989422804014327


def feed_kernel(
    n3_ref, og_ref, ac_ref, up_ref, dn_ref, ub_ref, vec_ref,
    res_ref, gt_ref, ug_ref, dg_ref, ubg_ref, dbg_ref,
    acc_ref, n3t_ref, act_ref, gb_ref,
):
    step = pl.program_id(0)
    rows, width = n3_ref.shape

    @pl.when(step == 0)
    def _():
        acc_ref[...] = ac_ref[...] + vec_ref[12:13, :]
        gt_ref[...] = jnp.zeros_like(gt_ref)
        dbg_ref[...] = jnp.zeros_like(dbg_ref)
        dbg_ref[0:1, :] = jnp.sum(og_ref[...].astype(F32), axis=0, keepdims=True)
        n3t_ref[...] = jnp.transpose(n3_ref[...])

    up = up_ref[...].reshape(width, width)
    dn = dn_ref[...].reshape(width, width)
    ub = ub_ref[pl.ds(step, 1), :]
    total = jnp.zeros((1, width), F32)
    for r in range(rows // 256):
        rs = slice(r * 256, (r + 1) * 256)
        n3 = n3_ref[rs, :]
        og = og_ref[rs, :]
        b = nn(n3, up) + ub
        cdf, pdf = normal_parts(b)
        act = (b * cdf).astype(BF16)
        gb = (nt(og, dn) * (cdf + b * pdf)).astype(BF16)
        act_ref[rs, :] = act
        gb_ref[rs, :] = gb
        total = total + jnp.sum(gb.astype(F32), axis=0, keepdims=True)
        acc_ref[rs, :] += nn(act, dn)
        gt_ref[rs, :] += nt(gb, up)
    ubg_ref[...] = jnp.broadcast_to(total, (8, width))
    ug_ref[...] = nn(n3t_ref[...], gb_ref[...]).astype(BF16).reshape(ug_ref.shape)
    dg_ref[...] = tn(act_ref[...], og_ref[...]).astype(BF16).reshape(dg_ref.shape)

    @pl.when(step == pl.num_programs(0) - 1)
    def _():
        res_ref[...] = acc_ref[...].astype(BF16)


def feed_call(n3, og, ac, up4, dn4, ub4, vecs):
    rows, width = n3.shape
    sds = jax.ShapeDtypeStruct
    tiles = up4.shape[0]
    tile = pl.BlockSpec((1, width, width), lambda i: (i, 0, 0))
    return pl.pallas_call(
        feed_kernel,
        grid=(tiles,),
        in_specs=[whole(n3.shape), whole(og.shape), whole(ac.shape), tile, tile, whole(ub4.shape), whole(vecs.shape)],
        out_specs=[
            whole((rows, width)), whole((rows, width)), tile, tile,
            pl.BlockSpec((8, width), lambda i: (i, 0)), whole((8, width)),
        ],
        out_shape=[
            sds((rows, width), BF16), sds((rows, width), F32),
            sds((tiles, width, width), BF16), sds((tiles, width, width), BF16),
            sds((tiles * 8, width), F32), sds((8, width), F32),
        ],
        scratch_shapes=[
            pltpu.VMEM((rows, width), F32), pltpu.VMEM((width, rows), BF16),
            pltpu.VMEM((rows, width), BF16), pltpu.VMEM((rows, width), BF16),
        ],
        compiler_params=params(dimension_semantics=("arbitrary",)),
        cost_estimate=cost(2 * 6 * rows * width * width * tiles, 35e6, 6e6),
        name="feed",
    )(n3, og, ac, up4, dn4, ub4, vecs)


def mid_back_kernel(
    meta, gt_ref, og_ref, ac_ref, mid_ref, n2_ref, cq_ref, ca_ref, lse_ref, kc_ref, vc_ref,
    fr_ref, so_ref, ci_ref, co_ref, vec_ref, o0, o1, o2, o3,
    gm_ref, do0, do1, do2, do3, sog_ref, cig_ref, cog_ref, eg_ref, sums_ref,
    km_ref, kmt_ref, vm_ref, dk_ref, dv_ref, so_acc, cq_acc, co_acc,
):
    frames = fr_ref.shape[0]
    hset = meta[72]
    step = pl.program_id(0)
    last = pl.num_programs(0) - 1
    masks = head_masks(frames)

    @pl.when(step == 0)
    def _():
        zero = jnp.zeros((frames, 128), BF16)
        for hp in range(6):
            ls = slice(hp * 128, hp * 128 + 128)
            k, v = kc_ref[:, ls], vc_ref[:, ls]
            for e in range(2):
                km_ref[hp * 2 + e] = jnp.where(masks[e], k, zero)
                vm_ref[hp * 2 + e] = jnp.where(masks[e], v, zero)
                kmt_ref[hp * 2 + e] = jnp.transpose(
                    jnp.where(masks[e], k.astype(F32), 0.0)
                ).astype(BF16)
        for ref in (dk_ref, dv_ref, so_acc, cq_acc, co_acc, sums_ref):
            ref[...] = jnp.zeros_like(ref)

    def count(row, value):
        sums_ref[row : row + 1, :] += value

    gt = gt_ref[...]
    back, gain, shift = norm_back(ac_ref[...], gt, vec_ref[2:3, :])
    count(2, gain)
    count(5, shift)
    ga = og_ref[...].astype(F32) + back
    gal = ga.astype(BF16)
    count(11, jnp.sum(gal.astype(F32), axis=0, keepdims=True))
    ca = ca_ref[...]
    co_acc[...] += tn(ca, gal)
    dca = nt(gal, co_ref[...]).astype(BF16)
    cq = cq_ref[...]
    dq = []
    for first in range(0, 12, 4):
        heads = range(first, first + 4)
        slices = [slice((h // 2) * 128, (h // 2) * 128 + 128) for h in heads]
        s = [nt(km_ref[h], cq[:, ls]) for h, ls in zip(heads, slices)]
        dp = [nt(vm_ref[h], dca[:, ls]) for h, ls in zip(heads, slices)]
        p = [jnp.exp2(v - lse_ref[h : h + 1, :]) for h, v in zip(heads, s)]
        ds = []
        for i in range(4):
            inner = jnp.sum(dp[i] * p[i], axis=0, keepdims=True)
            ds.append((p[i] * (dp[i] - inner)).astype(BF16))
        dqt = [nn(kmt_ref[h], v) for h, v in zip(heads, ds)]
        dk = [nn(v, cq[:, ls]) for v, ls in zip(ds, slices)]
        dv = [nn(v.astype(BF16), dca[:, ls]) for v, ls in zip(p, slices)]
        for i in (0, 2):
            dq.append(jnp.transpose(dqt[i] + dqt[i + 1]))
            dk_ref[:, slices[i]] += jnp.where(masks[0], dk[i], dk[i + 1])
            dv_ref[:, slices[i]] += jnp.where(masks[0], dv[i], dv[i + 1])
    dcq = (jnp.concatenate(dq, axis=1) * HEAD ** (-0.5)).astype(BF16)
    count(9, jnp.sum(dcq.astype(F32), axis=0, keepdims=True))
    cq_acc[...] += tn(n2_ref[...], dcq)
    gs = nt(dcq, ci_ref[0])
    back, gain, shift = norm_back(mid_ref[...], gs, vec_ref[1:2, :])
    count(1, gain)
    count(4, shift)
    gm = ga + back
    gm_ref[...] = gm
    gml = gm.astype(BF16)
    count(8, jnp.sum(gml.astype(F32), axis=0, keepdims=True))
    for k, (o, do) in enumerate(zip((o0, o1, o2, o3), (do0, do1, do2, do3))):
        at = pl.ds(pl.multiple_of((hset ^ k) * 192, 64), 192)
        do[...] = nt(gml, so_ref[at, :]).astype(BF16)
        so_acc[at, :] += tn(o[...], gml)

    @pl.when(step == last)
    def _():
        dk = (dk_ref[...] * LN2).astype(BF16)
        dv = dv_ref[...].astype(BF16)
        count(10, jnp.sum(dv.astype(F32), axis=0, keepdims=True))
        fr = fr_ref[...]
        sog_ref[...] = so_acc[...].astype(BF16)
        cog_ref[...] = co_acc[...].astype(BF16)
        cig_ref[0] = cq_acc[...].astype(BF16)
        cig_ref[1] = tn(fr, dk).astype(BF16)
        cig_ref[2] = tn(fr, dv).astype(BF16)
        eg_ref[...] = (nt(dk, ci_ref[1]) + nt(dv, ci_ref[2])).astype(BF16)


def mid_back_call(meta, gt, og, ac, mid, n2, cq, ca, lse, kc, vc, frames, so, ci, co, vecs, pieces):
    rows, width = gt.shape
    tile = 256
    nf = frames.shape[0]
    row = pl.BlockSpec((tile, width), lambda i, m: (i, 0))
    row4 = pl.BlockSpec((tile, 192), lambda i, m: (i, 0))
    sds = jax.ShapeDtypeStruct
    acc = pltpu.VMEM((width, width), F32)
    return pl.pallas_call(
        mid_back_kernel,
        grid_spec=pltpu.PrefetchScalarGridSpec(
            num_scalar_prefetch=1,
            grid=(rows // tile,),
            in_specs=[row] * 7
            + [pl.BlockSpec((16, tile), lambda i, m: (0, i))]
            + [whole(v.shape) for v in (kc, vc, frames, so, ci, co, vecs)]
            + [row4] * 4,
            out_specs=[row] + [row4] * 4
            + [whole((width, width)), whole((3, width, width)), whole((width, width)), whole((nf, width)), whole((24, width))],
            scratch_shapes=[
                pltpu.VMEM((12, nf, 128), BF16), pltpu.VMEM((12, 128, nf), BF16), pltpu.VMEM((12, nf, 128), BF16),
                pltpu.VMEM((nf, width), F32), pltpu.VMEM((nf, width), F32), acc, acc, acc,
            ],
        ),
        out_shape=[sds((rows, width), F32)] + [sds((rows, 192), BF16)] * 4
        + [sds((width, width), BF16), sds((3, width, width), BF16), sds((width, width), BF16), sds((nf, width), BF16), sds((24, width), F32)],
        compiler_params=params(dimension_semantics=("arbitrary",)),
        cost_estimate=cost(22e9, 35e6, 3e6),
        name="middle_back",
    )(meta, gt, og, ac, mid, n2, cq, ca, lse, kc, vc, frames, so, ci, co, vecs, *pieces)


def first_back_kernel(a_ref, b_ref, c_ref, gm_ref, tok_ref, vec_ref, out_ref, sums_ref):
    @pl.when(pl.program_id(0) == 0)
    def _():
        sums_ref[...] = jnp.zeros_like(sums_ref)

    e = a_ref[...].astype(F32) + b_ref[...].astype(F32) + c_ref[...].astype(F32)
    back, gain, shift = norm_back(tok_ref[...].astype(F32), e, vec_ref[0:1, :])
    sums_ref[0:1, :] += gain
    sums_ref[1:2, :] += shift
    out_ref[...] = (gm_ref[...] + back).astype(BF16)


def first_back_call(a, b, c, gm, tok, vecs, part):
    width = a.shape[1]
    base = part * 2
    row = pl.BlockSpec((256, width), lambda i: (i, 0))
    off = pl.BlockSpec((256, width), lambda i: (i + base, 0))
    return pl.pallas_call(
        first_back_kernel,
        grid=(2,),
        in_specs=[off, off, row, off, off, whole(vecs.shape)],
        out_specs=[row, whole((8, width))],
        out_shape=[jax.ShapeDtypeStruct((512, width), BF16), jax.ShapeDtypeStruct((8, width), F32)],
        compiler_params=params(dimension_semantics=("arbitrary",)),
        cost_estimate=cost(1e7, 6e6),
        name="first_back%d" % part,
    )(a, b, c, gm, tok, vecs)


def device_pairs(dp_count, move, back=False):
    pairs = []
    for dp in range(dp_count):
        for seq in range(8):
            y, c, z, x = move(dp // 2, dp % 2, seq // 2, seq % 2)
            pair = (dp * 8 + seq, (y * 2 + c) * 8 + z * 2 + x)
            pairs.append(pair[::-1] if back else pair)
    return pairs


def home_body(
    tokens, encoder_states, out_grad, block_map, branch_fork, norm_gain, norm_bias, self_in,
    self_out, self_bias, cross_in, cross_out, cross_bias, up_weight, up_bias, down_weight, down_bias,
):
    dp_count = lax.axis_size("dp")
    dp, seq = lax.axis_index("dp"), lax.axis_index("seq")
    c, z, x = dp & 1, seq >> 1, seq & 1
    y = dp >> 1
    flat = dp * 8 + seq
    hset = 2 * c + x
    parity = z & 1
    rows, width = tokens.shape[1:]
    frames = encoder_states.shape[1]

    def send(v, move, back=False):
        return lax.ppermute(v, AXES, device_pairs(dp_count, move, back))

    def flip(k):
        return lambda y, c, z, x: (y, c ^ (k >> 1), z, x ^ (k & 1))

    def home(p):
        return lambda y, c, z, x: (y, z >> 1, 2 * c + (p ^ (z & 1)), x)

    def pick(v, p):
        return jnp.where(parity == p, v[0], v[1])

    def piece(v, parts):
        return v.reshape(parts, -1).astype(BF16)

    small = jnp.concatenate(
        [v.reshape(-1) for v in (norm_gain, norm_bias, self_bias, cross_bias, down_bias, up_bias)]
    )
    small = jnp.pad(small, (0, 8 * 192 - small.shape[0])).reshape(8, 192)
    shard = self_in.reshape(-1, width)
    options = jnp.stack(
        [jnp.concatenate([shard[:, 192 * j : 192 * j + 192], small]) for j in range(4)]
    )

    def merge(own, other, bit):
        return jnp.stack([jnp.where(bit == 0, own, other), jnp.where(bit == 0, other, own)])

    def option(k):
        return lax.dynamic_index_in_dim(options, hset ^ k, 0, False)

    got = [option(0)] + [send(option(k), flip(k)) for k in (1, 2, 3)]
    tree = merge(merge(got[0], got[1], x), merge(got[2], got[3], x), c)
    for bit in range((dp_count // 2).bit_length() - 1):
        tree = merge(
            tree, send(tree, lambda y, c, z, x, bit=bit: (y ^ (1 << bit), c, z, x)), (y >> bit) & 1
        )
    both = jnp.concatenate([tokens, encoder_states], axis=1)
    mine = [send(pick(both, p), home(p)) for p in range(2)]
    tree, *mine = lax.optimization_barrier((tree, *mine))
    across = [send(v, flip(1)) for v in mine]
    near = [send(v, flip(2)) for v in mine]
    tree = merge(tree, send(tree, lambda y, c, z, x: (y, c, z ^ 2, x)), z >> 1)
    tree = merge(tree, send(tree, lambda y, c, z, x: (y, c, z ^ 1, x)), z & 1)
    y_count = dp_count // 2
    nw = shard.shape[0] // 3
    tree = tree.reshape(2, 2, y_count, 2, 2, 3 * nw + 8, 192).transpose(2, 3, 1, 0, 4, 5, 6)
    tree = tree.reshape(dp_count * 8, 3 * nw + 8, 192)
    w2 = jnp.concatenate(
        [tree[:, t * nw : (t + 1) * nw].reshape(width, 192) for t in range(3)], axis=1
    )
    flats = tree[:, 3 * nw :].reshape(dp_count * 8, -1)
    lists = [
        flats[:, i * nw : (i + 1) * nw].reshape(1, width) for i in range(13)
    ]
    tiles = up_weight.shape[1] // width
    ub4 = flats[:, 13 * nw : (13 + tiles) * nw].reshape(tiles, width).astype(F32)
    vecs = jnp.concatenate(lists + [jnp.zeros((3, width), BF16)]).astype(F32)
    own_cols = lambda v: lax.dynamic_slice_in_dim(v, hset * 192, 192, 1)
    zero_row = jnp.zeros((1, 192), F32)
    qkv_bias = jnp.concatenate([own_cols(vecs[6:7]), zero_row, own_cols(vecs[7:8])], axis=1)

    info = jnp.concatenate([block_map, branch_fork], axis=1)
    info = jnp.where((z >> 1) == c, info, send(info, flip(2)))
    info = jnp.where(parity == 0, info[0], info[1])
    place = jnp.arange(32, dtype=jnp.int32)
    k_of, p_of = place >> 3, (place >> 2) & 1
    stored = (2 * (2 * (c ^ (k_of >> 1)) + (p_of ^ parity)) + (x ^ (k_of & 1))) * 4 + (place & 3)
    logical = jnp.sum(jnp.where(stored[:, None] == place[None, :], info[None, :32], 0), axis=1)
    spot = jnp.sum(jnp.where(logical[None, :] == place[:, None], place[None, :], 0), axis=1)
    meta = jnp.concatenate(
        [logical, spot, info[32:40], jnp.full((56,), hset, jnp.int32)]
    ).astype(jnp.int32)

    dense = jnp.concatenate(
        [down_weight]
        + [up_weight[:, j * width : (j + 1) * width] for j in range(tiles)]
        + [self_out, cross_in[0], cross_in[1], cross_in[2], cross_out]
    )
    dense, w2, across[0] = lax.optimization_barrier((dense, w2, across[0]))
    dense = lax.all_gather(dense, AXES, axis=0)
    far = [send(v, flip(2)) for v in across]
    out_grad, far[1] = lax.optimization_barrier((out_grad, far[1]))
    pieces = mine + across + near + far
    nd = down_weight.shape[0]

    def gathered(i):
        at = nd + i * nw
        return dense[:, at : at + nw].reshape(width, width)

    dn4 = dense[:, :nd].reshape(tiles, width, width)
    up4 = jnp.stack([gathered(j) for j in range(tiles)])
    so = gathered(tiles)
    ci = jnp.stack([gathered(tiles + 1 + t) for t in range(3)])
    co = gathered(tiles + 4)

    q, kv, tr, n1 = qkv_call(meta, pieces, w2, vecs, qkv_bias)
    og = jnp.concatenate([send(pick(out_grad, p), home(p)) for p in range(2)])
    tok = jnp.concatenate([v[:rows] for v in mine])
    all_frames = jnp.concatenate([v[rows:] for v in pieces])

    o, lse = attend_call(meta, q, kv, tr)
    o4 = o.reshape(4, 1024, 192)
    o_home = [o4[0]] + [send(o4[k], flip(k)) for k in (1, 2, 3)]
    mid, ac, n2, n3, cq, ca, lse_c, kc, vc = mid_call(
        meta, tok, o_home, so, ci, co, all_frames, vecs
    )
    res, gt, ug, dg, ubg, dbg = feed_call(n3, og, ac, up4, dn4, ub4, vecs)
    gm, d0, d1, d2, d3, sog, cig, cog, eg, sums = mid_back_call(
        meta, gt, og, ac, mid, n2, cq, ca, lse_c, kc, vc, all_frames, so, ci, co, vecs, o_home
    )
    d_home = [d0] + [send(d, flip(k)) for k, d in ((1, d1), (2, d2), (3, d3))]

    def rows_of(grad):
        return grad.reshape(dp_count * 8, -1, width)

    packed = jnp.concatenate(
        [rows_of(dg)] + [rows_of(ug[j]) for j in range(tiles)]
        + [rows_of(sog), rows_of(cig[0]), rows_of(cig[1]), rows_of(cig[2]), rows_of(cog)],
        axis=1,
    )
    packed, *d_home = lax.optimization_barrier((packed, *d_home))
    dense_grad = lax.psum_scatter(packed, AXES, scatter_dimension=0, tiled=True)[0].astype(F32)

    results = [send(res[p * rows : (p + 1) * rows], home(p), True) for p in range(2)]
    eg4 = eg.reshape(4, 2 * frames, width)
    eg_near = send(eg4[2:4], flip(2)).astype(F32)
    eg_side = (eg4[1].astype(F32) + eg_near[1]).astype(BF16)
    eg_sum = eg4[0].astype(F32) + eg_near[0] + send(eg_side, flip(1)).astype(F32)
    eg_sum = eg_sum.astype(BF16)
    eg_back = [send(eg_sum[p * frames : (p + 1) * frames], home(p), True) for p in range(2)]

    dqkv, dx0, dx1, dx2, dx3 = attend_back_call(meta, q, kv, tr, o, lse, d_home, w2)
    dx3, results[0], results[1], eg_back[0], eg_back[1] = lax.optimization_barrier(
        (dx3, *results, *eg_back)
    )
    near3 = send(dx3, flip(2))
    side = (dx1.astype(F32) + near3.astype(F32)).astype(BF16)
    side_parts = [side[p * rows : (p + 1) * rows] for p in range(2)]
    side = [send(v, flip(1)) for v in side_parts]
    near2 = send(dx2, flip(2))
    n1, near3 = lax.optimization_barrier((n1, near3))

    wg, colsum = win_call(n1, dqkv)
    wg = wg.reshape(y_count, 2, 4, 2, nw, 576)

    def halve(v, move, bit, axis):
        keep = lax.dynamic_index_in_dim(v, bit, axis, False)
        give = lax.dynamic_index_in_dim(v, 1 - bit, axis, False)
        return (keep.astype(F32) + send(give, move).astype(F32)).astype(BF16)

    for bit in reversed(range((dp_count // 2).bit_length() - 1)):
        half = wg.shape[0] // 2
        wg = halve(
            wg.reshape((2, half) + wg.shape[1:]),
            lambda y, c, z, x, bit=bit: (y ^ (1 << bit), c, z, x), (y >> bit) & 1, 0,
        )
    wg = wg.reshape(2, 2, 2, 2, nw, 576)
    wg = halve(wg, lambda y, c, z, x: (y, c, z ^ 1, x), z & 1, 2)

    first = [first_back_call(dx0, near2, side[p], gm, tok, vecs, p) for p in range(2)]
    grads = [v[0] for v in first]
    first_sums = first[0][1] + first[1][1]
    wg, grads[0] = lax.optimization_barrier((wg, grads[0]))
    grads = [send(v, home(p), True) for p, v in enumerate(grads)]
    wg = halve(wg, lambda y, c, z, x: (y, c, z ^ 2, x), z >> 1, 1)
    wg = wg.reshape(4, nw, 576)

    def shard_for(k):
        return lax.dynamic_index_in_dim(wg, hset ^ k, 0, False)

    parts = jnp.stack([shard_for(0)] + [send(shard_for(k), flip(k)) for k in (1, 2, 3)])
    cols = [lax.dynamic_index_in_dim(parts, hset ^ j, 0, False) for j in range(4)]
    self_in_grad = jnp.stack(
        [jnp.concatenate([v[:, 192 * t : 192 * t + 192] for v in cols], axis=1) for t in range(3)]
    ).astype(F32)

    def returned(pair, dtype):
        pair = [v.astype(dtype) for v in pair]
        return jnp.stack([jnp.where(parity == 0, pair[0], pair[1]), jnp.where(parity == 0, pair[1], pair[0])])

    own_bias = lambda v: lax.dynamic_update_slice(
        jnp.zeros((1, width), F32), v, (0, hset * 192)
    )
    ubg = ubg.reshape(tiles, 8, width)[:, 0]
    def over_all(table):
        for k in (1, 2):
            table = table + send(table, flip(k))
        table = table + send(table, lambda y, c, z, x: (y, c, z ^ 1, x))
        table = table + send(table, lambda y, c, z, x: (y, c, z ^ 2, x))
        for bit in range((dp_count // 2).bit_length() - 1):
            table = table + send(table, lambda y, c, z, x, bit=bit: (y ^ (1 << bit), c, z, x))
        return table

    table = jnp.concatenate(
        [
            sums[1:3], sums[4:6], sums[8:12],
            own_bias(colsum[0:1, 0:192]), own_bias(colsum[0:1, 384:576]),
            dbg[0:1], ubg, jnp.zeros((16 - 11 - tiles, width), F32),
        ]
    )
    table = over_all(table)
    first_table = over_all(first_sums)
    table = jnp.concatenate(
        [
            first_table[0:1], table[0:2], first_table[1:2], table[2:4],
            table[8:10], table[4:8], table[10 : 11 + tiles],
        ]
    )
    mine_of = lambda v: lax.dynamic_slice_in_dim(v, flat * nw, nw, 1)
    vec_grad = mine_of(table[:13])
    up_bias_grad = lax.dynamic_slice_in_dim(
        table[13 : 13 + tiles].reshape(-1), flat * tiles * nw, tiles * nw, 0
    )

    def shard_grad(i):
        at = nd + i * nw
        return dense_grad[at : at + nw]

    return (
        returned(results, BF16),
        returned(grads, F32),
        returned(eg_back, F32),
        vec_grad[0:3],
        vec_grad[3:6],
        self_in_grad,
        shard_grad(tiles),
        vec_grad[6:9],
        jnp.stack([shard_grad(tiles + 1 + t) for t in range(3)]),
        shard_grad(tiles + 4),
        vec_grad[9:12],
        jnp.concatenate([shard_grad(j) for j in range(tiles)], axis=1),
        up_bias_grad,
        dense_grad[:nd],
        vec_grad[12],
    )


def solution(mesh):
    in_specs = (
        P("dp", "seq", None),
        P("dp", "seq", None),
        P("dp", "seq", None),
        P("dp", None),
        P("dp", None),
        P(None, ("dp", "seq")),
        P(None, ("dp", "seq")),
        P(None, ("dp", "seq"), None),
        P(("dp", "seq"), None),
        P(None, ("dp", "seq")),
        P(None, ("dp", "seq"), None),
        P(("dp", "seq"), None),
        P(None, ("dp", "seq")),
        P(("dp", "seq"), None),
        P(("dp", "seq")),
        P(("dp", "seq"), None),
        P(("dp", "seq")),
    )
    out_specs = (
        P("dp", "seq", None),
        P("dp", "seq", None),
        P("dp", "seq", None),
        P(None, ("dp", "seq")),
        P(None, ("dp", "seq")),
        P(None, ("dp", "seq"), None),
        P(("dp", "seq"), None),
        P(None, ("dp", "seq")),
        P(None, ("dp", "seq"), None),
        P(("dp", "seq"), None),
        P(None, ("dp", "seq")),
        P(("dp", "seq"), None),
        P(("dp", "seq")),
        P(("dp", "seq"), None),
        P(("dp", "seq")),
    )
    sizes = dict(mesh.shape)
    chosen = home_body if sizes["dp"] == 4 and sizes["seq"] == 8 else body
    return jax.shard_map(chosen, mesh=mesh, in_specs=in_specs, out_specs=out_specs, check_vma=False)
```
